32 devices in a mesh: row: 4 (over y, x), col: 2 (over core), vol: 4 (over z).
Axes of the slice: x: 2, y: 2, z: 4, core: 2. Of those that a mesh axis runs over, the one named last changes fastest.
Arguments:
- panel: bfloat16 [512, 131072], P('row', ('col', 'vol')), may hold values from -0.015625 to 0.015625
- density: float32 [32, 131072], P(None, ('col', 'vol')), may hold values from -6 to 6
- source: float32 [32, 32, 16, 512], P(None, 'row', 'col', 'vol'), may hold values from -6 to 6
- class_index: int32 [32, 16, 512], P('row', 'col', 'vol'), may hold values from 0 to 15
- class_values: float32 [16], replicated, may hold values from 0.2 to 5
- trace_count: int32 [4, 8], P('row'), may hold values from 1 to 64, 128 in all within a row
- trace_cell: int32 [4, 8, 64], P('row'), may hold values from 0 to 8191
Outputs:
- density_out: float32 [32, 131072], P(None, ('col', 'vol'))
- volume_out: float32 [32, 32, 16, 512], P(None, 'row', 'col', 'vol')
The draws below stay inside these ranges and needn't reach their ends.
Inputs may be any that keep to these rules, and one draw needn't show every extreme that they name: `trace_count`: in each row r, the counts of the 8 blocks are 1 or more and sum to 128, so that every target of row tile r has exactly one live slot; the largest count of each row is 64. `trace_cell`: only the first trace_count[r, j] slots of block j are read; two slots may hit one cell.
All inputs are finite; a program needn't handle non-finite values.
Results may differ from the reference program's by a relative error of at most 0.00035.
Values may be sent and summed in bfloat16 or wider, within the bound.
No kernel may reach another device: no remote copies, remote signals or barrier semaphores. Data moves between devices by JAX's collectives and lax.ppermute only.
A program may use at most 128 MiB of HBM per device.

```python
import math
import jax
import jax.numpy as jnp
import numpy as np
from jax import lax

NS = 131072
E = 32
TGT_DEV = 128
CX = 8
CY = 8
CZ = 128
SWEEPS = 4
OUTER = 2
NCLASS = 16
BLOCKS = 8
SLOTS = 64
TGT = 512
NX = 32
NY = 16
NZ = 512
N_ROW = 4
N_VOL = 4


def plant(values, key, low, high):
    longest = values.shape.index(max(values.shape))
    spots = []
    for shift in (0, 1):
        where = [jax.random.randint(jax.random.fold_in(key, axis), (), 0, length) for axis, length in enumerate(values.shape)]
        where[longest] = (where[longest] + shift) % values.shape[longest]
        spots.append(tuple(where))
    return values.at[spots[0]].set(low).at[spots[1]].set(high)


def levels(rng, shape, split, smallest, largest):
    def one(position, parts):
        heights = jax.random.uniform(jax.random.fold_in(jax.random.fold_in(rng, 6), position), (parts,), jnp.float32, smallest / len(split), largest / len(split))
        return jnp.repeat(jnp.exp(heights), shape[position] // parts).reshape((-1,) + (1,) * (len(shape) - position - 1))

    gain = one(*split[0])
    for cut in split[1:]:
        gain = gain * one(*cut)
    return gain


def split_up(number_of, total, limit, skew):
    loads = [(1 << 20) // math.isqrt(rank ** skew) + 1 for rank in range(2, number_of + 1)]
    rest, given = total - limit - (number_of - 1), [1] * (number_of - 1)
    while rest > 0:
        free = [i for i in range(number_of - 1) if given[i] < limit]
        mass, remaining = sum([loads[i] for i in free]), rest
        for i in free:
            extra = min(limit - given[i], max(1, remaining * loads[i] // mass), rest)
            given[i] = given[i] + extra
            rest = rest - extra
    return np.array([limit] + given)


def ragged_sizes(key, number_of, total, limit, lean):
    if number_of == 2:
        one = jax.random.randint(key, (), max(1, total - limit), min(limit, total - 1) + 1)
        return jnp.stack([one, total - one])
    tallies = jnp.asarray(split_up(number_of, total, limit, lean), jnp.int32)
    twos = (number_of - 1) // 2
    giver, taker = tallies[1:1 + 2 * twos:2], tallies[2:2 + 2 * twos:2]
    margin = jnp.minimum(giver - 1, limit - taker)
    moved = jax.random.randint(jax.random.fold_in(key, 1), (twos,), 0, 1 << 20) % (margin + 1)
    tallies = tallies.at[1:1 + 2 * twos:2].set(giver - moved).at[2:2 + 2 * twos:2].set(taker + moved)
    return tallies[jax.random.permutation(jax.random.fold_in(key, 2), number_of)]


def centred(rng, dims, scale, reach, cuts=(), kind=jnp.bfloat16):
    drawn = scale * jax.random.normal(rng, dims, jnp.float32)
    if cuts:
        drawn = drawn * levels(rng, dims, cuts, -0.22, 0.18)
    return jnp.clip(drawn, -reach, reach).astype(kind)


def setup_inputs(seed: int = 0) -> dict:
    key_of = jax.random.split(jax.random.key(seed), 8)
    panel = centred(key_of[0], (TGT, NS), NS ** -0.5, 0.015625, ((0, 4), (1, 8)))
    density = centred(key_of[1], (E, NS), 1.0, 6.0, ((1, 8),), jnp.float32)
    source = centred(key_of[2], (E, NX, NY, NZ), 1.0, 6.0, ((1, 4), (2, 2), (3, 4)), jnp.float32)
    class_index = plant(jax.random.randint(key_of[3], (NX, NY, NZ), 0, NCLASS), jax.random.fold_in(key_of[3], 1), 0, NCLASS - 1).astype(jnp.int32)
    class_values = jnp.clip(jnp.exp(jax.random.uniform(key_of[4], (NCLASS,), jnp.float32, math.log(0.2), math.log(5.0))), 0.2, 5.0)
    trace_count = jax.vmap(lambda own: ragged_sizes(own, BLOCKS, TGT_DEV, SLOTS, 2))(jax.random.split(key_of[5], N_ROW)).reshape((N_ROW, BLOCKS)).astype(jnp.int32)
    trace_cell = plant(jax.random.randint(key_of[6], (N_ROW, BLOCKS, SLOTS), 0, CX * CY * CZ), jax.random.fold_in(key_of[6], 1), 0, (CX * CY * CZ) - 1).astype(jnp.int32)
    return dict(panel=panel, density=density, source=source, class_index=class_index, class_values=class_values, trace_count=trace_count, trace_cell=trace_cell)


MASS_TERM = 0.1
RELAXATION = 0.5
SPECTRUM_LOW = 0.1
SPECTRUM_HIGH = 2.0


def relax_factors(count):
    middle = (SPECTRUM_HIGH + SPECTRUM_LOW) / 2.0
    spread = (SPECTRUM_HIGH - SPECTRUM_LOW) / 2.0
    return [1.0 / (middle + spread * math.cos(math.pi * (2 * order + 1) / (2 * count))) for order in range(count)]


def neighbours(padded):
    center = padded[..., 1:-1, 1:-1, 1:-1]
    beside_all = padded[..., 2:, 1:-1, 1:-1] + padded[..., :-2, 1:-1, 1:-1]
    beside_all = beside_all + padded[..., 1:-1, 2:, 1:-1] + padded[..., 1:-1, :-2, 1:-1]
    beside_all = beside_all + padded[..., 1:-1, 1:-1, 2:] + padded[..., 1:-1, 1:-1, :-2]
    return center, beside_all


def reference(panel, density, source, class_index, class_values, trace_count, trace_cell):
    conduct = jnp.take(class_values, class_index)
    diagonal = MASS_TERM + 6.0 * conduct
    offsets = jnp.cumsum(trace_count, axis=1) - trace_count
    slot_ids = jnp.arange(SLOTS, dtype=jnp.int32)
    live_slots = slot_ids[None, None, :] < trace_count[:, :, None]
    row_ids = jnp.arange(N_ROW, dtype=jnp.int32)[:, None, None]
    block_ids = jnp.arange(BLOCKS, dtype=jnp.int32)[None, :, None]
    targets = row_ids * TGT_DEV + jnp.minimum(offsets[:, :, None] + slot_ids[None, None, :], TGT_DEV - 1)
    col_place = block_ids // N_VOL
    vol_place = block_ids % N_VOL
    local_x = trace_cell // (CY * CZ)
    local_y = (trace_cell // CZ) % CY
    local_z = trace_cell % CZ
    global_cell = ((row_ids * CX + local_x) * NY + col_place * CY + local_y) * NZ + vol_place * CZ + local_z
    targets = targets.reshape(-1).astype(jnp.int32)
    global_cell = global_cell.reshape(-1).astype(jnp.int32)
    weights = live_slots.reshape(-1).astype(jnp.float32)
    factors = relax_factors(SWEEPS)

    def relax_one(pair):
        volume, right_side = pair
        for factor in factors:
            padded = jnp.pad(volume, 1)
            center, beside_all = neighbours(padded)
            volume = center + factor * (right_side - diagonal * center + conduct * beside_all) / diagonal
        return volume

    volume = jnp.zeros(source.shape, jnp.float32)
    for iteration in range(OUTER):
        rounded = density.astype(jnp.bfloat16)
        potential = jnp.dot(rounded, panel.T, preferred_element_type=jnp.float32)
        slot_values = potential[:, targets] * weights
        right_side = source.reshape(E, -1).at[:, global_cell].add(slot_values).reshape(source.shape)
        volume = lax.map(relax_one, (volume, right_side))
        mismatch = (volume.reshape(E, -1)[:, global_cell] - slot_values) * weights
        fluxes = jnp.zeros((E, TGT), jnp.float32).at[:, targets].add(mismatch)
        update = jnp.dot(fluxes.astype(jnp.bfloat16), panel, preferred_element_type=jnp.float32)
        density = density + RELAXATION * update
    return density, volume
```

```python
import functools
import math

import jax
import jax.numpy as jnp
from jax import lax
from jax.experimental import pallas as pl
from jax.experimental.pallas import tpu as pltpu
from jax.sharding import PartitionSpec as P

SWEEPS = 4
OUTER = 2


MASS_TERM = 0.1
RELAXATION = 0.5
SPECTRUM_LOW = 0.1
SPECTRUM_HIGH = 2.0

ALL = ("row", "col", "vol")
HIGHEST = lax.Precision.HIGHEST


def relax_factors(count):
    middle = (SPECTRUM_HIGH + SPECTRUM_LOW) / 2.0
    spread = (SPECTRUM_HIGH - SPECTRUM_LOW) / 2.0
    return [
        1.0 / (middle + spread * math.cos(math.pi * (2 * order + 1) / (2 * count)))
        for order in range(count)
    ]


def conduct_of(class_index, class_values):
    classes = jnp.arange(class_values.shape[0], dtype=jnp.int32)
    return jnp.sum(
        jnp.where(
            class_index[None] == classes[:, None, None, None],
            class_values[:, None, None, None],
            jnp.float32(0.0),
        ),
        axis=0,
    )


def exchange(value, axis):
    size = lax.axis_size(axis)
    got = [value]
    for k in range(1, size):
        got.append(lax.ppermute(value, axis, [(i, i ^ k) for i in range(size)]))
    return jnp.stack(got)


def slab_kernel(shape, first, place, source, others, parts, start, volume, plane_out, flux,
                old, new, ratio, scaled):
    rows, cols, vols, bx, by, bz = shape
    blocks = cols * vols
    targets = parts.shape[-1]
    factors = relax_factors(SWEEPS)
    height = bx * blocks * by
    r0, c0, v0 = place[0], place[1], place[2]
    row_ids = lax.broadcasted_iota(jnp.int32, (height, targets), 0)
    lane_ids = lax.broadcasted_iota(jnp.int32, (bz, targets), 0)
    zero_plane = jnp.zeros((blocks, by, bz), jnp.float32)
    for ref in (old, new):
        ref[0] = zero_plane
        ref[rows * bx + 1] = zero_plane

    potentials, hits, lanes = [], [], []
    for r in range(rows):
        if first:
            potential = jnp.sum(parts[r], axis=0, keepdims=True)
        else:
            potential = jnp.zeros((1, targets), jnp.float32)
            for s in range(rows):
                potential = potential + jnp.sum(parts[s, :, s ^ r, :], axis=0, keepdims=True)
        spot = others[c0, r ^ r0, v0, bx * by:bx * by + 2, :].astype(jnp.int32)
        hit = (row_ids == spot[0:1]).astype(jnp.float32)
        lane = lane_ids == spot[1:2]
        weighted = jnp.where(lane, potential, 0.0)
        added = lax.dot_general(
            hit, weighted, (((1,), (1,)), ((), ())),
            precision=HIGHEST, preferred_element_type=jnp.float32,
        ).reshape(bx, blocks, by, bz)
        potentials.append(potential)
        hits.append(hit)
        lanes.append(lane)
        for j in range(blocks):
            c, v = j // vols, j % vols
            conduct = others[c ^ c0, r ^ r0, v ^ v0, 0:bx * by, :].reshape(bx, by, bz)
            inverse = 1.0 / (MASS_TERM + 6.0 * conduct)
            ratio[r * bx:(r + 1) * bx, j] = conduct * inverse
            scaled[r * bx:(r + 1) * bx, j] = (source[r, j] + added[:, j]) * inverse
    if not first:
        old[1:rows * bx + 1] = start[...]

    sub = lax.broadcasted_iota(jnp.int32, (by, bz), 0)
    lan = lax.broadcasted_iota(jnp.int32, (by, bz), 1)
    zero = jnp.zeros((by, bz), jnp.float32)
    here, there = old, new
    for order, factor in enumerate(factors):
        def plane(x, here=here, there=there, order=order, factor=factor):
            if first and order == 0:
                there[x + 1] = factor * scaled[x]
                return
            tile = [here[x + 1, j] for j in range(blocks)]
            y_up = [pltpu.roll(t, 1, 0) for t in tile]
            y_dn = [pltpu.roll(t, by - 1, 0) for t in tile]
            z_up = [pltpu.roll(t, 1, 1) for t in tile]
            z_dn = [pltpu.roll(t, bz - 1, 1) for t in tile]
            for j in range(blocks):
                c, v = j // vols, j % vols
                around = here[x, j] + here[x + 2, j]
                around += jnp.where(sub == 0, y_up[j - vols] if c > 0 else zero, y_up[j])
                around += jnp.where(sub == by - 1, y_dn[j + vols] if c < cols - 1 else zero, y_dn[j])
                around += jnp.where(lan == 0, z_up[j - 1] if v > 0 else zero, z_up[j])
                around += jnp.where(lan == bz - 1, z_dn[j + 1] if v < vols - 1 else zero, z_dn[j])
                there[x + 1, j] = (1.0 - factor) * tile[j] + factor * (
                    scaled[x, j] + ratio[x, j] * around
                )

        def step(x, carry, plane=plane):
            plane(x)
            return carry

        lax.fori_loop(0, rows * bx, step, 0)
        here, there = there, here

    for r in range(rows):
        part = here[1 + r * bx:1 + (r + 1) * bx]
        if first:
            plane_out[r * bx:(r + 1) * bx] = part
        else:
            for x in range(bx):
                volume[r, :, x] = here[1 + r * bx + x]
        met = lax.dot_general(
            part.reshape(height, bz), hits[r], (((0,), (0,)), ((), ())),
            precision=HIGHEST, preferred_element_type=jnp.float32,
        )
        value = jnp.sum(jnp.where(lanes[r], met, 0.0), axis=0, keepdims=True) - potentials[r]
        for q in range(rows):
            flux[q, :, q ^ r, :] = jnp.broadcast_to(value, (blocks, targets))


def slab_call(shape, first, place, source, others, parts, start):
    rows, cols, vols, bx, by, bz = shape
    blocks = cols * vols
    targets = parts.shape[-1]
    planes = (rows * bx, blocks, by, bz)
    padded = (rows * bx + 2, blocks, by, bz)
    vmem = pl.BlockSpec(memory_space=pltpu.VMEM)
    operands = [place, source, others, parts]
    out_shape = [
        jax.ShapeDtypeStruct(planes if first else source.shape, jnp.float32),
        jax.ShapeDtypeStruct((rows, blocks, rows, targets), jnp.float32),
    ]
    if not first:
        operands.append(start)

    def body(place_ref, source_ref, others_ref, parts_ref, *rest):
        if first:
            out_ref, flux_ref, *scratch = rest
            slab_kernel(shape, True, place_ref, source_ref, others_ref, parts_ref, None, None,
                        out_ref, flux_ref, *scratch)
        else:
            start_ref, out_ref, flux_ref, *scratch = rest
            slab_kernel(shape, False, place_ref, source_ref, others_ref, parts_ref, start_ref,
                        out_ref, None, flux_ref, *scratch)

    return pl.pallas_call(
        body,
        out_shape=out_shape,
        in_specs=[pl.BlockSpec(memory_space=pltpu.SMEM)] + [vmem] * (len(operands) - 1),
        out_specs=[vmem, vmem],
        scratch_shapes=[
            pltpu.VMEM(padded, jnp.float32),
            pltpu.VMEM(padded, jnp.float32),
            pltpu.VMEM(planes, jnp.float32),
            pltpu.VMEM(planes, jnp.float32),
        ],
        compiler_params=pltpu.CompilerParams(vmem_limit_bytes=40 * 2 ** 20),
        name="slab_first" if first else "slab_last",
    )(*operands)


def update_call(flux, chunks, density, last):
    excitations, rows, targets = flux.shape
    width = density.shape[1]
    tile = math.gcd(width, 1024)

    def body(flux_ref, *refs):
        panels, density_ref, out_ref = refs[:rows], refs[rows], refs[rows + 1]
        pieces = [panels[k][...] for k in range(rows)]
        update = jnp.zeros((excitations, tile), jnp.float32)
        for k in range(rows):
            update += jnp.dot(
                flux_ref[:, k, :].astype(jnp.bfloat16), pieces[k],
                preferred_element_type=jnp.float32,
            )
        if last:
            out_ref[...] = (density_ref[...] + RELAXATION * update).astype(out_ref.dtype)
            return
        part_ref = refs[rows + 2]
        total = RELAXATION * update
        out_ref[...] = total
        rounded = (density_ref[...] + total).astype(jnp.bfloat16)

        @pl.when(pl.program_id(0) == 0)
        def _():
            part_ref[...] = jnp.zeros_like(part_ref)

        for k in range(rows):
            part_ref[:, k, :] += lax.dot_general(
                rounded, pieces[k], (((1,), (1,)), ((), ())), preferred_element_type=jnp.float32
            )

    out_shape = [jax.ShapeDtypeStruct(density.shape, jnp.bfloat16 if last else jnp.float32)]
    out_specs = [pl.BlockSpec((excitations, tile), lambda i: (0, i))]
    if not last:
        out_shape.append(jax.ShapeDtypeStruct(flux.shape, jnp.float32))
        out_specs.append(pl.BlockSpec(flux.shape, lambda i: (0, 0, 0)))
    return pl.pallas_call(
        body,
        grid=(width // tile,),
        out_shape=out_shape,
        in_specs=[pl.BlockSpec(flux.shape, lambda i: (0, 0, 0))]
        + [pl.BlockSpec((targets, tile), lambda i: (0, i))] * rows
        + [pl.BlockSpec((excitations, tile), lambda i: (0, i))],
        out_specs=out_specs,
        name="update_last" if last else "update_first",
    )(flux, *chunks, density)


def final_call(place, density, updates):
    rows = len(updates)
    excitations, width = updates[0].shape

    def body(place_ref, density_ref, *refs):
        out_ref = refs[rows]
        for k in range(rows):
            @pl.when(pl.program_id(0) == k)
            def _():
                out_ref[...] = density_ref[...] + refs[k][...].astype(jnp.float32)

    moved = pl.BlockSpec((excitations, width), lambda k, place: (0, k ^ place[0]))
    return pl.pallas_call(
        body,
        grid_spec=pltpu.PrefetchScalarGridSpec(
            num_scalar_prefetch=1,
            grid=(rows,),
            in_specs=[moved] + [pl.BlockSpec((excitations, width), lambda k, place: (0, 0))] * rows,
            out_specs=moved,
        ),
        out_shape=jax.ShapeDtypeStruct(density.shape, jnp.float32),
        name="density_join",
    )(place, density, *updates)


def split_by_excitation(panel, density, source, class_index, class_values, trace_count, trace_cell):
    rows, cols, vols = (lax.axis_size(a) for a in ALL)
    blocks = cols * vols
    excitations, bx, by, bz = source.shape
    targets, nodes = panel.shape
    width = nodes // rows
    here = lax.axis_index("row")
    place = jnp.stack([lax.axis_index(a) for a in ALL]).astype(jnp.int32)
    shape = (rows, cols, vols, bx, by, bz)

    slab = lax.all_to_all(source, ALL, 0, 0, tiled=True).reshape(rows, blocks, bx, by, bz)

    def columns(k):
        return lax.dynamic_slice_in_dim(panel, (here ^ k) * width, width, 1)

    chunks = [columns(0)]
    for k in range(1, rows):
        chunks.append(lax.ppermute(columns(k), "row", [(i, i ^ k) for i in range(rows)]))
    share = lax.dynamic_slice_in_dim(density, here * width, width, 1)

    conduct = conduct_of(class_index, class_values)
    counts = trace_count[0]
    offsets = jnp.cumsum(counts) - counts
    slot_ids = jnp.arange(trace_cell.shape[2], dtype=jnp.int32)
    live = slot_ids[None, :] < counts[:, None]
    owner = jnp.where(live, offsets[:, None] + slot_ids[None, :], -1)
    cell = trace_cell[0]
    block_ids = jnp.arange(blocks, dtype=jnp.int32)[:, None]
    line = (cell // (by * bz)) * (blocks * by) + block_ids * by + (cell // bz) % by
    match = owner[:, :, None] == jnp.arange(targets, dtype=jnp.int32)
    spots = [
        jnp.sum(jnp.where(match, value[:, :, None], 0), axis=(0, 1))
        for value in (line, cell % bz)
    ]
    spots = jnp.stack(spots).astype(jnp.float32)
    spots = jnp.pad(spots, ((0, 6), (0, bz - targets) if bz > targets else (0, 0)))
    others = jnp.concatenate([conduct.reshape(bx * by, bz), spots], axis=0)
    for axis in ("vol", "row", "col"):
        others = exchange(others, axis)

    rounded = density.astype(jnp.bfloat16)
    parts = lax.dot_general(
        rounded, panel, (((1,), (1,)), ((), ())), preferred_element_type=jnp.float32
    )
    parts = lax.all_to_all(parts, ALL, 0, 0, tiled=True).reshape(rows, blocks, targets)

    volume, flux = slab_call(shape, True, place, slab, others, parts, None)
    flux = lax.all_to_all(flux.reshape(excitations, rows, targets), ALL, 0, 0, tiled=True)
    total, parts = update_call(flux, chunks, share, False)
    parts = lax.all_to_all(parts, ALL, 0, 0, tiled=True).reshape(rows, blocks, rows, targets)
    volume, flux = slab_call(shape, False, place, slab, others, parts, volume)
    volume = lax.all_to_all(
        volume.reshape(excitations, bx, by, bz), ALL, 0, 0, tiled=True
    )
    flux = lax.all_to_all(flux.reshape(excitations, rows, targets), ALL, 0, 0, tiled=True)
    (total,) = update_call(flux, chunks, total, True)
    totals = [total]
    for k in range(1, rows):
        totals.append(lax.ppermute(total, "row", [(i, i ^ k) for i in range(rows)]))
    return (final_call(place, density, totals), volume)


def padded_2(value, sides, width):
    for axis, dim in sides:
        size, length = (lax.axis_size(axis), value.shape[dim])
        up = [(i, (i + 1) % size) for i in range(size - 1)]
        down = [(j, i) for i, j in up]
        last = lax.slice_in_dim(value, length - width, length, axis=dim)
        first = lax.slice_in_dim(value, 0, width, axis=dim)
        before = lax.ppermute(last, axis, up)
        after = lax.ppermute(first, axis, down)
        value = jnp.concatenate([before, value, after], axis=dim)
    return value


def neighbours(padded):
    center = padded[..., 1:-1, 1:-1, 1:-1]
    beside_all = padded[..., 2:, 1:-1, 1:-1] + padded[..., :-2, 1:-1, 1:-1]
    beside_all = beside_all + padded[..., 1:-1, 2:, 1:-1] + padded[..., 1:-1, :-2, 1:-1]
    beside_all = beside_all + padded[..., 1:-1, 1:-1, 2:] + padded[..., 1:-1, 1:-1, :-2]
    return (center, beside_all)


def split_by_block(panel, density, source, class_index, class_values, trace_count, trace_cell):
    factors = relax_factors(SWEEPS)
    conduct = conduct_of(class_index, class_values)
    diagonal = MASS_TERM + 6.0 * conduct
    counts = trace_count[0]
    block_index = lax.axis_index(("col", "vol"))
    offsets = jnp.cumsum(counts) - counts
    target_rows = panel.shape[0]
    slot_count = trace_cell.shape[2]
    slot_ids = jnp.arange(slot_count, dtype=jnp.int32)
    target_ids = jnp.arange(target_rows, dtype=jnp.int32)
    own_count = lax.dynamic_index_in_dim(counts, block_index, keepdims=False)
    first_target = lax.dynamic_index_in_dim(offsets, block_index, keepdims=False)
    cell_ids = lax.dynamic_index_in_dim(trace_cell[0], block_index, keepdims=False)
    live_slots = slot_ids < own_count
    select = (
        ((first_target + slot_ids)[:, None] == target_ids[None, :]) & live_slots[:, None]
    ).astype(jnp.float32)
    volume = jnp.zeros(source.shape, jnp.float32)
    field_shape = volume.shape
    share_width = density.shape[1] // lax.axis_size("row")
    share_state = lax.dynamic_slice_in_dim(
        density, lax.axis_index("row") * share_width, share_width, 1
    )
    rounded = density.astype(jnp.bfloat16)
    lead = field_shape[0]
    for iteration in range(OUTER):
        partial_value = lax.dot_general(
            rounded, panel, (((1,), (1,)), ((), ())), preferred_element_type=jnp.float32
        )
        potential = lax.psum(partial_value, ("col", "vol"))
        slot_values = jnp.dot(potential, select.T, precision=lax.Precision.HIGHEST)
        right_side = source.reshape(lead, -1).at[:, cell_ids].add(slot_values).reshape(field_shape)
        relax_volume = volume
        for factor in factors:
            padded = padded_2(relax_volume, (("row", 1), ("col", 2), ("vol", 3)), 1)
            center, beside_all = neighbours(padded)
            relax_volume = (
                center + factor * (right_side - diagonal * center + conduct * beside_all) / diagonal
            )
        volume = relax_volume
        mismatch = volume.reshape(lead, -1)[:, cell_ids] - slot_values
        own_fluxes = jnp.dot(mismatch, select, precision=lax.Precision.HIGHEST)
        fluxes = lax.psum(own_fluxes, ("col", "vol"))
        update = jnp.dot(fluxes.astype(jnp.bfloat16), panel, preferred_element_type=jnp.float32)
        share_state = share_state + RELAXATION * lax.psum_scatter(
            update, "row", scatter_dimension=1, tiled=True
        )
        if iteration + 1 < OUTER:
            rounded = lax.all_gather(share_state.astype(jnp.bfloat16), "row", axis=1, tiled=True)
    density = lax.all_gather(share_state, "row", axis=1, tiled=True)
    return (density, volume)


def local(*args):
    sizes = [lax.axis_size(a) for a in ALL]
    source, targets = args[2], args[0].shape[0]
    whole = math.prod(sizes) == source.shape[0] and targets == source.shape[3]
    if whole and all(size & (size - 1) == 0 for size in sizes):
        return split_by_excitation(*args)
    return split_by_block(*args)


def solution(mesh):
    placed = (
        P("row", ("col", "vol")),
        P(None, ("col", "vol")),
        P(None, "row", "col", "vol"),
        P("row", "col", "vol"),
        P(),
        P("row", None),
        P("row", None, None),
    )
    return jax.shard_map(
        local,
        mesh=mesh,
        in_specs=placed,
        out_specs=(P(None, ("col", "vol")), P(None, "row", "col", "vol")),
        check_vma=False,
    )
```

```python
import functools
import math

import jax
import jax.numpy as jnp
from jax import lax
from jax.experimental import pallas as pl
from jax.experimental.pallas import tpu as pltpu
from jax.sharding import PartitionSpec as P

SWEEPS = 4
OUTER = 2


MASS_TERM = 0.1
RELAXATION = 0.5
SPECTRUM_LOW = 0.1
SPECTRUM_HIGH = 2.0

ALL = ("row", "col", "vol")


def relax_factors(count):
    middle = (SPECTRUM_HIGH + SPECTRUM_LOW) / 2.0
    spread = (SPECTRUM_HIGH - SPECTRUM_LOW) / 2.0
    return [
        1.0 / (middle + spread * math.cos(math.pi * (2 * order + 1) / (2 * count)))
        for order in range(count)
    ]


def conduct_of(class_index, class_values):
    classes = jnp.arange(class_values.shape[0], dtype=jnp.int32)
    return jnp.sum(
        jnp.where(
            class_index[None] == classes[:, None, None, None],
            class_values[:, None, None, None],
            jnp.float32(0.0),
        ),
        axis=0,
    )


MATES = (0, 1, 2)


def exchange(value, axis):
    size = lax.axis_size(axis)
    if axis == "row":
        value, k = value[None], 1
        while k < size:
            value = jnp.concatenate([value, lax.ppermute(value, axis, [(i, i ^ k) for i in range(size)])])
            k = 2 * k
        return value
    moved = [lax.ppermute(value, axis, [(i, i ^ k) for i in range(size)]) for k in range(1, size)]
    return jnp.stack([value] + moved)


def prepare_call(shape, place, values, others, targets):
    rows, cols, vols, bx, by, bz = shape
    blocks = cols * vols
    height = bx * blocks * by

    def body(place_ref, values_ref, others_ref, ratio_ref, inverse_ref, hit_ref, lane_ref):
        r0, c0, v0 = place_ref[0], place_ref[1], place_ref[2]
        count = values_ref.shape[0]
        row_ids = lax.broadcasted_iota(jnp.int32, (height, targets), 0)
        lane_ids = lax.broadcasted_iota(jnp.int32, (bz, targets), 0)
        for r in range(rows):
            spot = others_ref[c0, r ^ r0, v0, bx * by:bx * by + 16, :].astype(jnp.float32)
            spot = spot.astype(jnp.int32)
            line = spot[0:1] * (blocks * by) + spot[1:2]
            hit_ref[r] = (row_ids == line).astype(jnp.bfloat16)
            lane_ref[r] = (lane_ids == spot[2:3]).astype(jnp.bfloat16)

        def block(index, carry):
            r, rest = index // blocks, index % blocks
            c, v = rest // vols, rest % vols
            kind = others_ref[c ^ c0, r ^ r0, v ^ v0, 0:bx * by, :].astype(jnp.float32)
            conduct = jnp.zeros((bx * by, bz), jnp.float32)
            for i in range(count):
                conduct = jnp.where(kind == float(i), values_ref[i], conduct)
            inverse = 1.0 / (MASS_TERM + 6.0 * conduct)
            ratio = (conduct * inverse).reshape(bx, by, bz)
            start = pl.multiple_of(c * by, by)
            ratio_ref[pl.ds(r * bx, bx), v, pl.ds(start, by)] = ratio
            inverse_ref[pl.ds(r * bx, bx), v, pl.ds(start, by)] = inverse.reshape(bx, by, bz)
            return carry

        lax.fori_loop(0, rows * blocks, block, 0)

    planes = (rows * bx, vols, cols * by, bz)
    vmem = pl.BlockSpec(memory_space=pltpu.VMEM)
    smem = pl.BlockSpec(memory_space=pltpu.SMEM)
    return pl.pallas_call(
        body,
        out_shape=[
            jax.ShapeDtypeStruct(planes, jnp.float32),
            jax.ShapeDtypeStruct(planes, jnp.float32),
            jax.ShapeDtypeStruct((rows, height, targets), jnp.bfloat16),
            jax.ShapeDtypeStruct((rows, bz, targets), jnp.bfloat16),
        ],
        in_specs=[smem, smem, vmem],
        out_specs=[vmem] * 4,
        name="prepare",
    )(place, values, others)


def parts_of(value, count):
    pieces = []
    for _ in range(count):
        piece = value.astype(jnp.bfloat16)
        pieces.append(piece)
        value = value - piece.astype(jnp.float32)
    return pieces


def slab_call(shape, first, source, parts, ratio, inverse, hit, lane, start):
    rows, cols, vols, bx, by, bz = shape
    blocks = cols * vols
    targets = parts.shape[-1]
    height = bx * blocks * by
    depth = rows * bx
    planes = (depth, vols, cols * by, bz)
    padded = (depth + 2, vols, cols * by, bz)
    factors = relax_factors(SWEEPS)

    def body(source_ref, parts_ref, ratio_ref, inverse_ref, hit_ref, lane_ref, *rest):
        if first:
            out_ref, flux_ref, other_ref, scaled_ref = rest
            volume_ref = None
        else:
            start_ref, volume_ref, flux_ref, out_ref, other_ref, scaled_ref = rest
        sub = lax.broadcasted_iota(jnp.int32, (by, bz), 0)
        lan = lax.broadcasted_iota(jnp.int32, (by, bz), 1)
        for ref in (out_ref, other_ref):
            ref[0] = jnp.zeros(planes[1:], jnp.float32)
            ref[depth + 1] = jnp.zeros(planes[1:], jnp.float32)
        here = other_ref if first else start_ref
        potentials = []
        for r in range(rows):
            if first:
                potential = jnp.sum(parts_ref[r], axis=0, keepdims=True)
            else:
                potential = sum(
                    jnp.sum(parts_ref[r ^ mate, :, k, :], axis=0, keepdims=True)
                    for k, mate in enumerate(MATES)
                )
            potentials.append(potential)
            weights = [
                lane_ref[r] * piece.astype(jnp.bfloat16) for piece in parts_of(potential, 3)
            ]
            added = lax.dot_general(
                hit_ref[r], jnp.concatenate(weights, axis=0), (((1,), (1,)), ((), ())),
                preferred_element_type=jnp.float32,
            )
            added = added[:, :bz] + added[:, bz:2 * bz] + added[:, 2 * bz:]
            added = added.reshape(bx, vols, cols, by, bz)
            for j in range(blocks):
                c, v = j // vols, j % vols
                span = (slice(r * bx, (r + 1) * bx), v, slice(c * by, (c + 1) * by))
                scaled = (source_ref[r, j] + added[:, v, c]) * inverse_ref[span]
                scaled_ref[span] = scaled
                if first:
                    here[1 + r * bx:1 + (r + 1) * bx, v, c * by:(c + 1) * by] = factors[0] * scaled

        sweeps = factors[1:] if first else factors
        for order, factor in enumerate(sweeps):
            last = order + 1 == len(sweeps)
            there = out_ref if (len(sweeps) - order) % 2 == 1 else other_ref

            def plane(x, here=here, there=there, last=last, factor=factor):
                tile = [here[x + 1, j % vols, (j // vols) * by:(j // vols + 1) * by]
                        for j in range(blocks)]
                z_up = [pltpu.roll(t, 1, 1) for t in tile]
                z_dn = [pltpu.roll(t, bz - 1, 1) for t in tile]
                for j in range(blocks):
                    c, v = j // vols, j % vols
                    own = slice(c * by, (c + 1) * by)
                    around = here[x, v, own] + here[x + 2, v, own]
                    if c > 0:
                        around += here[x + 1, v, c * by - 1:(c + 1) * by - 1]
                    else:
                        around += jnp.where(sub == 0, 0.0, pltpu.roll(tile[j], 1, 0))
                    if c < cols - 1:
                        around += here[x + 1, v, c * by + 1:(c + 1) * by + 1]
                    else:
                        around += jnp.where(sub == by - 1, 0.0, pltpu.roll(tile[j], by - 1, 0))
                    around += jnp.where(lan == 0, z_up[j - 1] if v > 0 else 0.0, z_up[j])
                    around += jnp.where(lan == bz - 1, z_dn[j + 1] if v < vols - 1 else 0.0, z_dn[j])
                    value = (1.0 - factor) * tile[j] + factor * (
                        scaled_ref[x, v, own] + ratio_ref[x, v, own] * around
                    )
                    there[x + 1, v, own] = value
                    if last and not first:
                        volume_ref[x // bx, j, x % bx] = value

            def step(x, carry, plane=plane):
                plane(x)
                return carry

            lax.fori_loop(0, depth, step, 0, unroll=2)
            here = there

        for r in range(rows):
            part = here[1 + r * bx:1 + (r + 1) * bx].reshape(height, bz)
            met = sum(
                jnp.dot(piece, lane_ref[r], preferred_element_type=jnp.float32)
                for piece in parts_of(part, 2)
            )
            value = jnp.sum(met * hit_ref[r].astype(jnp.float32), axis=0, keepdims=True)
            value = value - potentials[r]
            for k, mate in enumerate(MATES):
                flux_ref[r ^ mate, :, k, :] = jnp.broadcast_to(value, (blocks, targets))

    vmem = pl.BlockSpec(memory_space=pltpu.VMEM)
    operands = [source, parts, ratio, inverse, hit, lane] + ([] if first else [start])
    fluxes = jax.ShapeDtypeStruct((rows, blocks, len(MATES), targets), jnp.float32)
    field = jax.ShapeDtypeStruct(padded if first else source.shape, jnp.float32)
    scratch = [pltpu.VMEM(padded, jnp.float32)] * (1 if first else 2)
    return pl.pallas_call(
        body,
        out_shape=[field, fluxes],
        in_specs=[vmem] * len(operands),
        out_specs=[vmem, vmem],
        scratch_shapes=scratch + [pltpu.VMEM(planes, jnp.float32)],
        name="slab_first" if first else "slab_last",
    )(*operands)


def update_call(flux, panels):
    excitations, width = flux.shape[0], panels[0].shape[1]

    def body(flux_ref, a_own, a_mate, b_own, b_mate, a_ref, b_ref):
        fluxes = [flux_ref[:, k, :].astype(jnp.bfloat16) for k in range(len(MATES))]
        for out, own, mate, k in ((a_ref, a_own, a_mate, 1), (b_ref, b_own, b_mate, 2)):
            value = jnp.dot(fluxes[0], own[...], preferred_element_type=jnp.float32)
            value += jnp.dot(fluxes[k], mate[...], preferred_element_type=jnp.float32)
            out[...] = value.astype(jnp.bfloat16)

    vmem = pl.BlockSpec(memory_space=pltpu.VMEM)
    return pl.pallas_call(
        body,
        out_shape=[jax.ShapeDtypeStruct((excitations, width), jnp.bfloat16)] * 2,
        in_specs=[vmem] * 5,
        out_specs=[vmem] * 2,
        name="update",
    )(flux, *panels)


def potential_call(densities, halves, mates, panels):
    excitations = densities[0].shape[0]
    targets = panels[0].shape[0]

    def body(a_density, b_density, a_half, b_half, a_other, b_other,
             a_own, a_mate, b_own, b_mate, out_ref):
        rounded = [
            (density[...] + RELAXATION * (half[...].astype(jnp.float32)
                                          + other[...].astype(jnp.float32))).astype(jnp.bfloat16)
            for density, half, other in (
                (a_density, a_half, a_other), (b_density, b_half, b_other))
        ]

        def met(value, panel):
            return lax.dot_general(
                value, panel[...], (((1,), (1,)), ((), ())), preferred_element_type=jnp.float32
            )

        out_ref[:, 0, :] = met(rounded[0], a_own) + met(rounded[1], b_own)
        out_ref[:, 1, :] = met(rounded[0], a_mate)
        out_ref[:, 2, :] = met(rounded[1], b_mate)

    vmem = pl.BlockSpec(memory_space=pltpu.VMEM)
    return pl.pallas_call(
        body,
        out_shape=jax.ShapeDtypeStruct((excitations, len(MATES), targets), jnp.float32),
        in_specs=[vmem] * 10,
        out_specs=vmem,
        name="potential",
    )(*densities, *halves, *mates, *panels)


def trace_spots(trace_count, trace_cell, targets, shape):
    rows, cols, vols, bx, by, bz = shape
    counts = trace_count[0]
    offsets = jnp.cumsum(counts) - counts
    slot_ids = jnp.arange(trace_cell.shape[2], dtype=jnp.int32)
    live = slot_ids[None, :] < counts[:, None]
    owner = jnp.where(live, offsets[:, None] + slot_ids[None, :], -1)
    cell = trace_cell[0]
    block_ids = jnp.arange(cols * vols, dtype=jnp.int32)[:, None]
    line = (block_ids % vols) * (cols * by) + (block_ids // vols) * by + (cell // bz) % by
    code = ((cell // (by * bz)) * (cols * vols * by) + line) * bz + cell % bz
    match = owner[:, :, None] == jnp.arange(targets, dtype=jnp.int32)
    code = jnp.sum(jnp.where(match, code[:, :, None], 0), axis=(0, 1))
    line = code // bz
    span = cols * vols * by
    return jnp.stack([line // span, line % span, code % bz])


def split_by_excitation(panel, density, source, class_index, class_values, trace_count, trace_cell):
    rows, cols, vols = (lax.axis_size(a) for a in ALL)
    blocks = cols * vols
    excitations, bx, by, bz = source.shape
    targets, nodes = panel.shape
    width = nodes // rows
    here = lax.axis_index("row")
    low, high = here & 1, here >> 1
    place = jnp.stack([lax.axis_index(a) for a in ALL]).astype(jnp.int32)
    shape = (rows, cols, vols, bx, by, bz)

    def along(value, mate):
        return lax.ppermute(value, "row", [(i, i ^ mate) for i in range(rows)])

    def columns(array, place):
        return lax.dynamic_slice_in_dim(array, place * width, width, 1)

    spots = trace_spots(trace_count, trace_cell, targets, shape).astype(jnp.bfloat16)
    others = jnp.concatenate(
        [class_index.reshape(bx * by, bz).astype(jnp.bfloat16), jnp.pad(spots, ((0, 13), (0, 0)))]
    )
    for axis in ("vol", "row", "col"):
        others = exchange(others, axis)

    slab = lax.all_to_all(source, ALL, 0, 0, tiled=True).reshape(rows, blocks, bx, by, bz)

    rounded = density.astype(jnp.bfloat16)
    parts = lax.dot_general(
        rounded, panel, (((1,), (1,)), ((), ())), preferred_element_type=jnp.float32
    )
    parts = lax.all_to_all(parts, ALL, 0, 0, tiled=True).reshape(rows, blocks, targets)

    panels = [
        columns(panel, low), along(columns(panel, low ^ 1), 1),
        columns(panel, 2 + high), along(columns(panel, 2 + (high ^ 1)), 2),
    ]
    densities = [columns(density, low), columns(density, 2 + high)]

    ratio, inverse, hit, lane = prepare_call(shape, place, class_values, others, targets)
    volume, flux = slab_call(shape, True, slab, parts, ratio, inverse, hit, lane, None)
    flux = lax.all_to_all(flux.reshape(excitations, len(MATES), targets), ALL, 0, 0, tiled=True)
    halves = update_call(flux, panels)
    mates = [along(halves[0], 2), along(halves[1], 1)]
    parts = potential_call(densities, halves, mates, panels)
    parts = lax.all_to_all(parts, ALL, 0, 0, tiled=True)
    parts = parts.reshape(rows, blocks, len(MATES), targets)
    volume, flux = slab_call(shape, False, slab, parts, ratio, inverse, hit, lane, volume)
    flux = lax.all_to_all(flux.reshape(excitations, len(MATES), targets), ALL, 0, 0, tiled=True)
    volume = lax.all_to_all(
        volume.reshape(excitations, bx, by, bz), ALL, 0, 0, tiled=True
    )
    ends = update_call(flux, panels)
    end_mates = [along(ends[0], 2), along(ends[1], 1)]
    totals = []
    for group in zip(halves, mates, ends, end_mates):
        a, b, c, d = (value.astype(jnp.float32) for value in group)
        totals.append((RELAXATION * ((a + b) + (c + d))).astype(jnp.bfloat16))
    moved = [along(totals[0], 1), along(totals[1], 2)]
    change = [
        jnp.where(low == 0, totals[0], moved[0]), jnp.where(low == 0, moved[0], totals[0]),
        jnp.where(high == 0, totals[1], moved[1]), jnp.where(high == 0, moved[1], totals[1]),
    ]
    return (density + jnp.concatenate(change, axis=1).astype(jnp.float32), volume)


def padded_2(value, sides, width):
    for axis, dim in sides:
        size, length = (lax.axis_size(axis), value.shape[dim])
        up = [(i, (i + 1) % size) for i in range(size - 1)]
        down = [(j, i) for i, j in up]
        last = lax.slice_in_dim(value, length - width, length, axis=dim)
        first = lax.slice_in_dim(value, 0, width, axis=dim)
        before = lax.ppermute(last, axis, up)
        after = lax.ppermute(first, axis, down)
        value = jnp.concatenate([before, value, after], axis=dim)
    return value


def neighbours(padded):
    center = padded[..., 1:-1, 1:-1, 1:-1]
    beside_all = padded[..., 2:, 1:-1, 1:-1] + padded[..., :-2, 1:-1, 1:-1]
    beside_all = beside_all + padded[..., 1:-1, 2:, 1:-1] + padded[..., 1:-1, :-2, 1:-1]
    beside_all = beside_all + padded[..., 1:-1, 1:-1, 2:] + padded[..., 1:-1, 1:-1, :-2]
    return (center, beside_all)


def split_by_block(panel, density, source, class_index, class_values, trace_count, trace_cell):
    factors = relax_factors(SWEEPS)
    conduct = conduct_of(class_index, class_values)
    diagonal = MASS_TERM + 6.0 * conduct
    counts = trace_count[0]
    block_index = lax.axis_index(("col", "vol"))
    offsets = jnp.cumsum(counts) - counts
    target_rows = panel.shape[0]
    slot_count = trace_cell.shape[2]
    slot_ids = jnp.arange(slot_count, dtype=jnp.int32)
    target_ids = jnp.arange(target_rows, dtype=jnp.int32)
    own_count = lax.dynamic_index_in_dim(counts, block_index, keepdims=False)
    first_target = lax.dynamic_index_in_dim(offsets, block_index, keepdims=False)
    cell_ids = lax.dynamic_index_in_dim(trace_cell[0], block_index, keepdims=False)
    live_slots = slot_ids < own_count
    select = (
        ((first_target + slot_ids)[:, None] == target_ids[None, :]) & live_slots[:, None]
    ).astype(jnp.float32)
    volume = jnp.zeros(source.shape, jnp.float32)
    field_shape = volume.shape
    share_width = density.shape[1] // lax.axis_size("row")
    share_state = lax.dynamic_slice_in_dim(
        density, lax.axis_index("row") * share_width, share_width, 1
    )
    rounded = density.astype(jnp.bfloat16)
    lead = field_shape[0]
    for iteration in range(OUTER):
        partial_value = lax.dot_general(
            rounded, panel, (((1,), (1,)), ((), ())), preferred_element_type=jnp.float32
        )
        potential = lax.psum(partial_value, ("col", "vol"))
        slot_values = jnp.dot(potential, select.T, precision=lax.Precision.HIGHEST)
        right_side = source.reshape(lead, -1).at[:, cell_ids].add(slot_values).reshape(field_shape)
        relax_volume = volume
        for factor in factors:
            padded = padded_2(relax_volume, (("row", 1), ("col", 2), ("vol", 3)), 1)
            center, beside_all = neighbours(padded)
            relax_volume = (
                center + factor * (right_side - diagonal * center + conduct * beside_all) / diagonal
            )
        volume = relax_volume
        mismatch = volume.reshape(lead, -1)[:, cell_ids] - slot_values
        own_fluxes = jnp.dot(mismatch, select, precision=lax.Precision.HIGHEST)
        fluxes = lax.psum(own_fluxes, ("col", "vol"))
        update = jnp.dot(fluxes.astype(jnp.bfloat16), panel, preferred_element_type=jnp.float32)
        share_state = share_state + RELAXATION * lax.psum_scatter(
            update, "row", scatter_dimension=1, tiled=True
        )
        if iteration + 1 < OUTER:
            rounded = lax.all_gather(share_state.astype(jnp.bfloat16), "row", axis=1, tiled=True)
    density = lax.all_gather(share_state, "row", axis=1, tiled=True)
    return (density, volume)


def local(*args):
    sizes = [lax.axis_size(a) for a in ALL]
    source, targets = args[2], args[0].shape[0]
    whole = math.prod(sizes) == source.shape[0] and targets == source.shape[3] and sizes[0] == 4
    if whole and all(size & (size - 1) == 0 for size in sizes):
        return split_by_excitation(*args)
    return split_by_block(*args)


def solution(mesh):
    placed = (
        P("row", ("col", "vol")),
        P(None, ("col", "vol")),
        P(None, "row", "col", "vol"),
        P("row", "col", "vol"),
        P(),
        P("row", None),
        P("row", None, None),
    )
    return jax.shard_map(
        local,
        mesh=mesh,
        in_specs=placed,
        out_specs=(P(None, ("col", "vol")), P(None, "row", "col", "vol")),
        check_vma=False,
    )
```

```python
import math

import jax
import jax.numpy as jnp
from jax import lax
from jax.experimental import pallas as pl
from jax.experimental.pallas import tpu as pltpu
from jax.sharding import PartitionSpec as P


SWEEPS = 4
OUTER = 2


MASS_TERM = 0.1
RELAXATION = 0.5
SPECTRUM_LOW = 0.1
SPECTRUM_HIGH = 2.0

ALL = ("row", "col", "vol")
GROUP = 8
SPOT_ROWS = 16
PART_ROWS = 8
VMEM_BYTES = 16 * 2 ** 20


def relax_factors(count):
    middle = (SPECTRUM_HIGH + SPECTRUM_LOW) / 2.0
    spread = (SPECTRUM_HIGH - SPECTRUM_LOW) / 2.0
    return [
        1.0 / (middle + spread * math.cos(math.pi * (2 * order + 1) / (2 * count)))
        for order in range(count)
    ]


def conduct_of(class_index, class_values):
    classes = jnp.arange(class_values.shape[0], dtype=jnp.int32)
    return jnp.sum(
        jnp.where(
            class_index[None] == classes[:, None, None, None],
            class_values[:, None, None, None],
            jnp.float32(0.0),
        ),
        axis=0,
    )


MATES = (0, 1, 2)


def mated(value, axis, mate):
    return lax.ppermute(value, axis, [(i, i ^ mate) for i in range(lax.axis_size(axis))])


def stacked(value, axis):
    size = lax.axis_size(axis)
    return jnp.stack([value] + [mated(value, axis, k) for k in range(1, size)])


def gather_call(density, panel, source):
    excitations, lines, bz = source.shape
    targets, nodes = panel.shape
    steps = math.gcd(excitations, 8)
    width, few = nodes // steps, excitations // steps

    def body(density_ref, panel_ref, source_ref, out_ref, part_ref):
        index = pl.program_id(0)
        part = lax.dot_general(
            density_ref[...].astype(jnp.bfloat16), panel_ref[...], (((1,), (1,)), ((), ())),
            preferred_element_type=jnp.float32,
        )

        @pl.when(index == 0)
        def _():
            part_ref[...] = part

        @pl.when(index > 0)
        def _():
            part_ref[...] += part

        out_ref[pl.ds(index * few, few), 0:lines] = source_ref[...]

        @pl.when(index == steps - 1)
        def _():
            for i in range(excitations):
                out_ref[i, lines:lines + PART_ROWS] = jnp.broadcast_to(
                    part_ref[i:i + 1], (PART_ROWS, targets)
                )

    return pl.pallas_call(
        body,
        grid=(steps,),
        out_shape=jax.ShapeDtypeStruct((excitations, lines + PART_ROWS, bz), jnp.float32),
        in_specs=[
            pl.BlockSpec((excitations, width), lambda i: (0, i)),
            pl.BlockSpec((targets, width), lambda i: (0, i)),
            pl.BlockSpec((few, lines, bz), lambda i: (i, 0, 0)),
        ],
        out_specs=pl.BlockSpec((excitations, lines + PART_ROWS, bz), lambda i: (0, 0, 0)),
        scratch_shapes=[pltpu.VMEM((excitations, targets), jnp.float32)],
        compiler_params=pltpu.CompilerParams(vmem_limit_bytes=VMEM_BYTES),
        name="gather",
    )(density, panel, source)


def prepare_call(shape, place, values, kinds, spots):
    rows, cols, vols, bx, by, bz = shape
    blocks = cols * vols
    height = bx * blocks * by
    targets = spots.shape[-1]

    def body(place_ref, values_ref, kinds_ref, spots_ref, ratio_ref, inverse_ref, hit_ref, lane_ref):
        r0, c0, v0 = place_ref[0], place_ref[1], place_ref[2]
        count = values_ref.shape[0]
        row_ids = lax.broadcasted_iota(jnp.int32, (height, targets), 0)
        lane_ids = lax.broadcasted_iota(jnp.int32, (bz, targets), 0)
        for r in range(rows):
            spot = spots_ref[r ^ r0].astype(jnp.float32).astype(jnp.int32)
            line = spot[0:1] * (blocks * by) + spot[1:2]
            hit_ref[r] = (row_ids == line).astype(jnp.bfloat16)
            lane_ref[r] = (lane_ids == spot[2:3]).astype(jnp.bfloat16)

        def block(index, carry):
            r, rest = index // blocks, index % blocks
            c, v = rest // vols, rest % vols
            kind = kinds_ref[c ^ c0, r ^ r0, v ^ v0].astype(jnp.float32)
            conduct = jnp.zeros((bx * by, bz), jnp.float32)
            for i in range(count):
                conduct = jnp.where(kind == float(i), values_ref[i], conduct)
            inverse = 1.0 / (MASS_TERM + 6.0 * conduct)
            ratio = (conduct * inverse).reshape(bx, by, bz)
            start = pl.multiple_of(c * by, by)
            ratio_ref[pl.ds(r * bx, bx), v, pl.ds(start, by)] = ratio
            inverse_ref[pl.ds(r * bx, bx), v, pl.ds(start, by)] = inverse.reshape(bx, by, bz)
            return carry

        lax.fori_loop(0, rows * blocks, block, 0)

    planes = (rows * bx, vols, cols * by, bz)
    vmem = pl.BlockSpec(memory_space=pltpu.VMEM)
    smem = pl.BlockSpec(memory_space=pltpu.SMEM)
    return pl.pallas_call(
        body,
        out_shape=[
            jax.ShapeDtypeStruct(planes, jnp.float32),
            jax.ShapeDtypeStruct(planes, jnp.float32),
            jax.ShapeDtypeStruct((rows, height, targets), jnp.bfloat16),
            jax.ShapeDtypeStruct((rows, bz, targets), jnp.bfloat16),
        ],
        in_specs=[smem, smem, vmem, vmem],
        out_specs=[vmem] * 4,
        compiler_params=pltpu.CompilerParams(vmem_limit_bytes=VMEM_BYTES),
        name="prepare",
    )(place, values, kinds, spots)


def parts_of(value, count):
    pieces = []
    for _ in range(count):
        piece = value.astype(jnp.bfloat16)
        pieces.append(piece)
        value = value - piece.astype(jnp.float32)
    return pieces


def slab_call(shape, first, source, ratio, inverse, hit, lane, parts=None, start=None):
    rows, cols, vols, bx, by, bz = shape
    blocks = cols * vols
    targets = lane.shape[-1]
    height = bx * blocks * by
    depth = rows * bx
    planes = (depth, vols, cols * by, bz)
    padded = (depth + 2, vols, cols * by, bz)
    factors = relax_factors(SWEEPS)

    lines = bx * by

    def body(source_ref, ratio_ref, inverse_ref, hit_ref, lane_ref, *rest):
        if first:
            out_ref, flux_ref, other_ref, scaled_ref = rest
            volume_ref = None
        else:
            parts_ref, start_ref, volume_ref, flux_ref, out_ref, other_ref, scaled_ref = rest
        sub = lax.broadcasted_iota(jnp.int32, (by, bz), 0)
        lan = lax.broadcasted_iota(jnp.int32, (by, bz), 1)
        for ref in (out_ref, other_ref):
            ref[0] = jnp.zeros(planes[1:], jnp.float32)
            ref[depth + 1] = jnp.zeros(planes[1:], jnp.float32)
        here = other_ref if first else start_ref
        potentials = []
        for r in range(rows):
            if first:
                potential = sum(source_ref[r, j, lines:lines + 1] for j in range(blocks))
            else:
                potential = sum(
                    jnp.sum(parts_ref[r ^ mate, :, k, :], axis=0, keepdims=True)
                    for k, mate in enumerate(MATES)
                )
            potentials.append(potential)
            weights = [
                lane_ref[r] * piece.astype(jnp.bfloat16) for piece in parts_of(potential, 3)
            ]
            added = lax.dot_general(
                hit_ref[r], jnp.concatenate(weights, axis=0), (((1,), (1,)), ((), ())),
                preferred_element_type=jnp.float32,
            )
            added = added[:, :bz] + added[:, bz:2 * bz] + added[:, 2 * bz:]
            added = added.reshape(bx, vols, cols, by, bz)
            for j in range(blocks):
                c, v = j // vols, j % vols
                span = (slice(r * bx, (r + 1) * bx), v, slice(c * by, (c + 1) * by))
                scaled = source_ref[r, j, 0:lines].reshape(bx, by, bz) + added[:, v, c]
                scaled = scaled * inverse_ref[span]
                scaled_ref[span] = scaled
                if first:
                    here[1 + r * bx:1 + (r + 1) * bx, v, c * by:(c + 1) * by] = factors[0] * scaled

        sweeps = factors[1:] if first else factors
        for order, factor in enumerate(sweeps):
            last = order + 1 == len(sweeps)
            there = out_ref if (len(sweeps) - order) % 2 == 1 else other_ref

            def step(index, carry, here=here, there=there, last=last, factor=factor):
                for x in (GROUP * index + i for i in range(GROUP)):
                    tile = [here[x + 1, j % vols, (j // vols) * by:(j // vols + 1) * by]
                            for j in range(blocks)]
                    up = [pltpu.roll(t, 1, 1) for t in tile]
                    down = [pltpu.roll(t, bz - 1, 1) for t in tile]
                    for j in range(blocks):
                        c, v = j // vols, j % vols
                        own = slice(c * by, (c + 1) * by)
                        around = here[x, v, own] + here[x + 2, v, own]
                        if c > 0:
                            around += here[x + 1, v, c * by - 1:(c + 1) * by - 1]
                        else:
                            around += jnp.where(sub == 0, 0.0, pltpu.roll(tile[j], 1, 0))
                        if c < cols - 1:
                            around += here[x + 1, v, c * by + 1:(c + 1) * by + 1]
                        else:
                            around += jnp.where(sub == by - 1, 0.0, pltpu.roll(tile[j], by - 1, 0))
                        around += jnp.where(lan == 0, up[j - 1] if v > 0 else 0.0, up[j])
                        around += jnp.where(
                            lan == bz - 1, down[j + 1] if v < vols - 1 else 0.0, down[j]
                        )
                        value = (1.0 - factor) * tile[j] + factor * (
                            scaled_ref[x, v, own] + ratio_ref[x, v, own] * around
                        )
                        there[x + 1, v, own] = value
                        if last and not first:
                            volume_ref[x // bx, j, x % bx] = value
                return carry

            lax.fori_loop(0, depth // GROUP, step, 0)
            here = there

        for r in range(rows):
            part = here[1 + r * bx:1 + (r + 1) * bx].reshape(height, bz)
            met = sum(
                jnp.dot(piece, lane_ref[r], preferred_element_type=jnp.float32)
                for piece in parts_of(part, 2)
            )
            value = jnp.sum(met * hit_ref[r].astype(jnp.float32), axis=0, keepdims=True)
            value = value - potentials[r]
            for k, mate in enumerate(MATES):
                flux_ref[r ^ mate, :, k, :] = jnp.broadcast_to(value, (blocks, targets))

    vmem = pl.BlockSpec(memory_space=pltpu.VMEM)
    operands = [source, ratio, inverse, hit, lane] + ([] if first else [parts, start])
    fluxes = jax.ShapeDtypeStruct((rows, blocks, len(MATES), targets), jnp.float32)
    field = padded if first else (rows, blocks, bx, by, bz)
    field = jax.ShapeDtypeStruct(field, jnp.float32)
    scratch = [pltpu.VMEM(padded, jnp.float32)] * (1 if first else 2)
    return pl.pallas_call(
        body,
        out_shape=[field, fluxes],
        in_specs=[vmem] * len(operands),
        out_specs=[vmem, vmem],
        scratch_shapes=scratch + [pltpu.VMEM(planes, jnp.float32)],
        compiler_params=pltpu.CompilerParams(vmem_limit_bytes=VMEM_BYTES),
        name="slab_first" if first else "slab_last",
    )(*operands)


def update_call(flux, panels):
    excitations, width = flux.shape[0], panels[0].shape[1]

    def body(flux_ref, a_own, a_mate, b_own, b_mate, a_ref, b_ref):
        fluxes = [flux_ref[:, k, :].astype(jnp.bfloat16) for k in range(len(MATES))]
        for out, own, mate, k in ((a_ref, a_own, a_mate, 1), (b_ref, b_own, b_mate, 2)):
            value = jnp.dot(fluxes[0], own[...], preferred_element_type=jnp.float32)
            value += jnp.dot(fluxes[k], mate[...], preferred_element_type=jnp.float32)
            out[...] = value.astype(jnp.bfloat16)

    vmem = pl.BlockSpec(memory_space=pltpu.VMEM)
    return pl.pallas_call(
        body,
        out_shape=[jax.ShapeDtypeStruct((excitations, width), jnp.bfloat16)] * 2,
        in_specs=[vmem] * 5,
        out_specs=[vmem] * 2,
        compiler_params=pltpu.CompilerParams(vmem_limit_bytes=VMEM_BYTES),
        name="update",
    )(flux, *panels)


def potential_call(densities, halves, mates, panels):
    excitations = densities[0].shape[0]
    targets = panels[0].shape[0]

    def body(a_density, b_density, a_half, b_half, a_other, b_other,
             a_own, a_mate, b_own, b_mate, out_ref):
        rounded = [
            (density[...] + RELAXATION * (half[...].astype(jnp.float32)
                                          + other[...].astype(jnp.float32))).astype(jnp.bfloat16)
            for density, half, other in (
                (a_density, a_half, a_other), (b_density, b_half, b_other))
        ]

        def met(value, panel):
            return lax.dot_general(
                value, panel[...], (((1,), (1,)), ((), ())), preferred_element_type=jnp.float32
            )

        out_ref[:, 0, :] = met(rounded[0], a_own) + met(rounded[1], b_own)
        out_ref[:, 1, :] = met(rounded[0], a_mate)
        out_ref[:, 2, :] = met(rounded[1], b_mate)

    vmem = pl.BlockSpec(memory_space=pltpu.VMEM)
    return pl.pallas_call(
        body,
        out_shape=jax.ShapeDtypeStruct((excitations, len(MATES), targets), jnp.float32),
        in_specs=[vmem] * 10,
        out_specs=vmem,
        compiler_params=pltpu.CompilerParams(vmem_limit_bytes=VMEM_BYTES),
        name="potential",
    )(*densities, *halves, *mates, *panels)


def trace_spots(trace_count, trace_cell, targets, shape):
    _, cols, vols, _, by, bz = shape
    counts = trace_count[0]
    offsets = jnp.cumsum(counts) - counts
    slot_ids = jnp.arange(trace_cell.shape[2], dtype=jnp.int32)
    live = slot_ids[None, :] < counts[:, None]
    owner = jnp.where(live, offsets[:, None] + slot_ids[None, :], -1)
    cell = trace_cell[0]
    block_ids = jnp.arange(cols * vols, dtype=jnp.int32)[:, None]
    line = (block_ids % vols) * (cols * by) + (block_ids // vols) * by + (cell // bz) % by
    code = ((cell // (by * bz)) * (cols * vols * by) + line) * bz + cell % bz
    match = owner[:, :, None] == jnp.arange(targets, dtype=jnp.int32)
    code = jnp.sum(jnp.where(match, code[:, :, None], 0), axis=(0, 1))
    line = code // bz
    span = cols * vols * by
    return jnp.stack([line // span, line % span, code % bz])


def split_by_excitation(panel, density, source, class_index, class_values, trace_count, trace_cell):
    rows, cols, vols = (lax.axis_size(a) for a in ALL)
    blocks = cols * vols
    excitations, bx, by, bz = source.shape
    targets, nodes = panel.shape
    width = nodes // rows
    here = lax.axis_index("row")
    low, high = here & 1, here >> 1
    place = jnp.stack([lax.axis_index(a) for a in ALL]).astype(jnp.int32)
    shape = (rows, cols, vols, bx, by, bz)

    def columns(array, place):
        return lax.dynamic_slice_in_dim(array, place * width, width, 1)

    kinds = class_index.reshape(bx * by, bz).astype(jnp.bfloat16)
    kinds = stacked(kinds, "vol").reshape(vols * bx * by, bz)
    spots = trace_spots(trace_count, trace_cell, targets, shape).astype(jnp.bfloat16)
    spots = jnp.pad(spots, ((0, SPOT_ROWS - spots.shape[0]), (0, 0)))
    known = jnp.concatenate([kinds, spots])[None]
    known = jnp.concatenate([known, mated(known, "row", 1)])
    known = jnp.concatenate([known, mated(known, "row", 2)])
    spots = known[:, vols * bx * by:]
    kinds = stacked(known[:, :vols * bx * by], "col")
    kinds = kinds.reshape(cols, rows, vols, bx * by, bz)

    slab = gather_call(density, panel, source.reshape(excitations, bx * by, bz))
    slab = lax.all_to_all(slab, ALL, 0, 0, tiled=True)
    slab = slab.reshape(rows, blocks, bx * by + PART_ROWS, bz)

    panels = [columns(panel, low), None, columns(panel, 2 + high), None]
    panels[1] = mated(columns(panel, low ^ 1), "row", 1)
    panels[3] = mated(columns(panel, 2 + (high ^ 1)), "row", 2)
    densities = [columns(density, low), columns(density, 2 + high)]

    ratio, inverse, hit, lane = prepare_call(shape, place, class_values, kinds, spots)
    volume, flux = slab_call(shape, True, slab, ratio, inverse, hit, lane)
    flux = flux.reshape(excitations, len(MATES), targets)
    flux = lax.all_to_all(flux, ALL, 0, 0, tiled=True)
    halves = update_call(flux, panels)
    mates = [mated(halves[0], "row", 2), mated(halves[1], "row", 1)]
    parts = potential_call(densities, halves, mates, panels)
    parts = lax.all_to_all(parts, ALL, 0, 0, tiled=True)
    parts = parts.reshape(rows, blocks, len(MATES), targets)
    volume, flux = slab_call(shape, False, slab, ratio, inverse, hit, lane, parts, volume)
    flux = flux.reshape(excitations, len(MATES), targets)
    flux = lax.all_to_all(flux, ALL, 0, 0, tiled=True)
    volume = volume.reshape(excitations, bx, by, bz)
    volume = lax.all_to_all(volume, ALL, 0, 0, tiled=True)
    ends = update_call(flux, panels)
    end_mates = [mated(ends[0], "row", 2), mated(ends[1], "row", 1)]
    totals = []
    for group in zip(halves, mates, ends, end_mates):
        a, b, c, d = (value.astype(jnp.float32) for value in group)
        totals.append((RELAXATION * ((a + b) + (c + d))).astype(jnp.bfloat16))
    moved = [mated(totals[0], "row", 1), mated(totals[1], "row", 2)]
    change = [
        jnp.where(low == 0, totals[0], moved[0]), jnp.where(low == 0, moved[0], totals[0]),
        jnp.where(high == 0, totals[1], moved[1]), jnp.where(high == 0, moved[1], totals[1]),
    ]
    return (density + jnp.concatenate(change, axis=1).astype(jnp.float32), volume)


def padded_2(value, sides, width):
    for axis, dim in sides:
        size, length = (lax.axis_size(axis), value.shape[dim])
        up = [(i, (i + 1) % size) for i in range(size - 1)]
        down = [(j, i) for i, j in up]
        last = lax.slice_in_dim(value, length - width, length, axis=dim)
        first = lax.slice_in_dim(value, 0, width, axis=dim)
        before = lax.ppermute(last, axis, up)
        after = lax.ppermute(first, axis, down)
        value = jnp.concatenate([before, value, after], axis=dim)
    return value


def neighbours(padded):
    center = padded[..., 1:-1, 1:-1, 1:-1]
    beside_all = padded[..., 2:, 1:-1, 1:-1] + padded[..., :-2, 1:-1, 1:-1]
    beside_all = beside_all + padded[..., 1:-1, 2:, 1:-1] + padded[..., 1:-1, :-2, 1:-1]
    beside_all = beside_all + padded[..., 1:-1, 1:-1, 2:] + padded[..., 1:-1, 1:-1, :-2]
    return (center, beside_all)


def split_by_block(panel, density, source, class_index, class_values, trace_count, trace_cell):
    factors = relax_factors(SWEEPS)
    conduct = conduct_of(class_index, class_values)
    diagonal = MASS_TERM + 6.0 * conduct
    counts = trace_count[0]
    block_index = lax.axis_index(("col", "vol"))
    offsets = jnp.cumsum(counts) - counts
    target_rows = panel.shape[0]
    slot_count = trace_cell.shape[2]
    slot_ids = jnp.arange(slot_count, dtype=jnp.int32)
    target_ids = jnp.arange(target_rows, dtype=jnp.int32)
    own_count = lax.dynamic_index_in_dim(counts, block_index, keepdims=False)
    first_target = lax.dynamic_index_in_dim(offsets, block_index, keepdims=False)
    cell_ids = lax.dynamic_index_in_dim(trace_cell[0], block_index, keepdims=False)
    live_slots = slot_ids < own_count
    select = (
        ((first_target + slot_ids)[:, None] == target_ids[None, :]) & live_slots[:, None]
    ).astype(jnp.float32)
    volume = jnp.zeros(source.shape, jnp.float32)
    field_shape = volume.shape
    share_width = density.shape[1] // lax.axis_size("row")
    share_state = lax.dynamic_slice_in_dim(
        density, lax.axis_index("row") * share_width, share_width, 1
    )
    rounded = density.astype(jnp.bfloat16)
    lead = field_shape[0]
    for iteration in range(OUTER):
        partial_value = lax.dot_general(
            rounded, panel, (((1,), (1,)), ((), ())), preferred_element_type=jnp.float32
        )
        potential = lax.psum(partial_value, ("col", "vol"))
        slot_values = jnp.dot(potential, select.T, precision=lax.Precision.HIGHEST)
        right_side = source.reshape(lead, -1).at[:, cell_ids].add(slot_values).reshape(field_shape)
        relax_volume = volume
        for factor in factors:
            padded = padded_2(relax_volume, (("row", 1), ("col", 2), ("vol", 3)), 1)
            center, beside_all = neighbours(padded)
            relax_volume = (
                center + factor * (right_side - diagonal * center + conduct * beside_all) / diagonal
            )
        volume = relax_volume
        mismatch = volume.reshape(lead, -1)[:, cell_ids] - slot_values
        own_fluxes = jnp.dot(mismatch, select, precision=lax.Precision.HIGHEST)
        fluxes = lax.psum(own_fluxes, ("col", "vol"))
        update = jnp.dot(fluxes.astype(jnp.bfloat16), panel, preferred_element_type=jnp.float32)
        share_state = share_state + RELAXATION * lax.psum_scatter(
            update, "row", scatter_dimension=1, tiled=True
        )
        if iteration + 1 < OUTER:
            rounded = lax.all_gather(share_state.astype(jnp.bfloat16), "row", axis=1, tiled=True)
    density = lax.all_gather(share_state, "row", axis=1, tiled=True)
    return (density, volume)


def local(*args):
    sizes = [lax.axis_size(a) for a in ALL]
    if whole_slabs(sizes, args[0].shape[0], args[2].shape):
        return split_by_excitation(*args)
    return split_by_block(*args)


def whole_slabs(sizes, targets, block):
    fits = math.prod(sizes) == block[0] and sizes[0] == 4 and targets == block[3]
    return fits and all(size & (size - 1) == 0 for size in sizes)


def solution(mesh):
    placed = (
        P("row", ("col", "vol")),
        P(None, ("col", "vol")),
        P(None, "row", "col", "vol"),
        P("row", "col", "vol"),
        P(),
        P("row", None),
        P("row", None, None),
    )
    return jax.shard_map(
        local,
        mesh=mesh,
        in_specs=placed,
        out_specs=(P(None, ("col", "vol")), P(None, "row", "col", "vol")),
        check_vma=False,
    )
```

```python
import math

import jax
import jax.numpy as jnp
from jax import lax
from jax.experimental import pallas as pl
from jax.experimental.pallas import tpu as pltpu
from jax.sharding import PartitionSpec as P


SWEEPS = 4
OUTER = 2


MASS_TERM = 0.1
RELAXATION = 0.5
SPECTRUM_LOW = 0.1
SPECTRUM_HIGH = 2.0

ALL = ("row", "col", "vol")
GROUP = 8
SPOT_ROWS = 16
PART_ROWS = 8
VMEM_BYTES = 16 * 2 ** 20


def relax_factors(count):
    middle = (SPECTRUM_HIGH + SPECTRUM_LOW) / 2.0
    spread = (SPECTRUM_HIGH - SPECTRUM_LOW) / 2.0
    return [
        1.0 / (middle + spread * math.cos(math.pi * (2 * order + 1) / (2 * count)))
        for order in range(count)
    ]


def conduct_of(class_index, class_values):
    classes = jnp.arange(class_values.shape[0], dtype=jnp.int32)
    return jnp.sum(
        jnp.where(
            class_index[None] == classes[:, None, None, None],
            class_values[:, None, None, None],
            jnp.float32(0.0),
        ),
        axis=0,
    )


MATES = (0, 1, 2)


def mated(value, axis, mate):
    return lax.ppermute(value, axis, [(i, i ^ mate) for i in range(lax.axis_size(axis))])


def stacked(value, axis):
    size = lax.axis_size(axis)
    return jnp.stack([value] + [mated(value, axis, k) for k in range(1, size)])


def gather_call(density, panel, source):
    excitations, lines, bz = source.shape
    targets, nodes = panel.shape
    steps = math.gcd(excitations, 8)
    width, few = nodes // steps, excitations // steps

    def body(density_ref, panel_ref, source_ref, out_ref, part_ref):
        index = pl.program_id(0)
        part = lax.dot_general(
            density_ref[...].astype(jnp.bfloat16), panel_ref[...], (((1,), (1,)), ((), ())),
            preferred_element_type=jnp.float32,
        )

        @pl.when(index == 0)
        def _():
            part_ref[...] = part

        @pl.when(index > 0)
        def _():
            part_ref[...] += part

        out_ref[pl.ds(index * few, few), 0:lines] = source_ref[...]

        @pl.when(index == steps - 1)
        def _():
            for i in range(excitations):
                out_ref[i, lines:lines + PART_ROWS] = jnp.broadcast_to(
                    part_ref[i:i + 1], (PART_ROWS, targets)
                )

    return pl.pallas_call(
        body,
        grid=(steps,),
        out_shape=jax.ShapeDtypeStruct((excitations, lines + PART_ROWS, bz), jnp.float32),
        in_specs=[
            pl.BlockSpec((excitations, width), lambda i: (0, i)),
            pl.BlockSpec((targets, width), lambda i: (0, i)),
            pl.BlockSpec((few, lines, bz), lambda i: (i, 0, 0)),
        ],
        out_specs=pl.BlockSpec((excitations, lines + PART_ROWS, bz), lambda i: (0, 0, 0)),
        scratch_shapes=[pltpu.VMEM((excitations, targets), jnp.float32)],
        name="gather",
    )(density, panel, source)


def prepare_call(shape, place, values, kinds, spots):
    rows, cols, vols, bx, by, bz = shape
    blocks = cols * vols
    height = bx * blocks * by
    targets = spots.shape[-1]

    def body(place_ref, values_ref, kinds_ref, spots_ref, inverse_ref, hit_ref, lane_ref):
        r0, c0, v0 = place_ref[0], place_ref[1], place_ref[2]
        count = values_ref.shape[0]
        row_ids = lax.broadcasted_iota(jnp.int32, (height, targets), 0)
        lane_ids = lax.broadcasted_iota(jnp.int32, (bz, targets), 0)
        for r in range(rows):
            spot = spots_ref[r ^ r0].astype(jnp.float32).astype(jnp.int32)
            line = spot[0:1] * (blocks * by) + spot[1:2]
            hit_ref[r] = (row_ids == line).astype(jnp.bfloat16)
            lane_ref[r] = (lane_ids == spot[2:3]).astype(jnp.bfloat16)

        def block(index, carry):
            r, rest = index // blocks, index % blocks
            c, v = rest // vols, rest % vols
            kind = kinds_ref[c ^ c0, r ^ r0, v ^ v0].astype(jnp.float32)
            conduct = jnp.zeros((bx * by, bz), jnp.float32)
            for i in range(count):
                conduct = jnp.where(kind == float(i), values_ref[i], conduct)
            inverse = 1.0 / (MASS_TERM + 6.0 * conduct)
            start = pl.multiple_of(c * by, by)
            inverse_ref[pl.ds(r * bx, bx), v, pl.ds(start, by)] = inverse.reshape(bx, by, bz)
            return carry

        lax.fori_loop(0, rows * blocks, block, 0)

    planes = (rows * bx, vols, cols * by, bz)
    vmem = pl.BlockSpec(memory_space=pltpu.VMEM)
    smem = pl.BlockSpec(memory_space=pltpu.SMEM)
    return pl.pallas_call(
        body,
        out_shape=[
            jax.ShapeDtypeStruct(planes, jnp.float32),
            jax.ShapeDtypeStruct((rows, height, targets), jnp.bfloat16),
            jax.ShapeDtypeStruct((rows, bz, targets), jnp.bfloat16),
        ],
        in_specs=[smem, smem, vmem, vmem],
        out_specs=[vmem] * 3,
        name="prepare",
    )(place, values, kinds, spots)


def parts_of(value, count):
    pieces = []
    for _ in range(count):
        piece = value.astype(jnp.bfloat16)
        pieces.append(piece)
        value = value - piece.astype(jnp.float32)
    return pieces


def slab_call(shape, first, source, inverse, hit, lane, parts=None, start=None):
    rows, cols, vols, bx, by, bz = shape
    blocks = cols * vols
    targets = lane.shape[-1]
    height = bx * blocks * by
    depth = rows * bx
    planes = (depth, vols, cols * by, bz)
    padded = (depth + 2, vols, cols * by, bz)
    factors = relax_factors(SWEEPS)

    lines = bx * by

    def body(source_ref, inverse_ref, hit_ref, lane_ref, *rest):
        if first:
            out_ref, flux_ref, other_ref, scaled_ref, ratio_ref = rest
            volume_ref = None
        else:
            parts_ref, start_ref, volume_ref, flux_ref, out_ref, other_ref, scaled_ref, ratio_ref = rest
        sub = lax.broadcasted_iota(jnp.int32, (by, bz), 0)
        lan = lax.broadcasted_iota(jnp.int32, (by, bz), 1)
        for ref in (out_ref, other_ref):
            ref[0] = jnp.zeros(planes[1:], jnp.float32)
            ref[depth + 1] = jnp.zeros(planes[1:], jnp.float32)
        here = other_ref if first else start_ref
        potentials = []
        for r in range(rows):
            if first:
                potential = sum(source_ref[r, j, lines:lines + 1] for j in range(blocks))
            else:
                potential = sum(
                    jnp.sum(parts_ref[r ^ mate, :, k, :], axis=0, keepdims=True)
                    for k, mate in enumerate(MATES)
                )
            potentials.append(potential)
            weights = [
                lane_ref[r] * piece.astype(jnp.bfloat16) for piece in parts_of(potential, 3)
            ]
            added = lax.dot_general(
                hit_ref[r], jnp.concatenate(weights, axis=0), (((1,), (1,)), ((), ())),
                preferred_element_type=jnp.float32,
            )
            added = added[:, :bz] + added[:, bz:2 * bz] + added[:, 2 * bz:]
            added = added.reshape(bx, vols, cols, by, bz)
            for j in range(blocks):
                c, v = j // vols, j % vols
                span = (slice(r * bx, (r + 1) * bx), v, slice(c * by, (c + 1) * by))
                scaled = source_ref[r, j, 0:lines].reshape(bx, by, bz) + added[:, v, c]
                inverse = inverse_ref[span]
                scaled = scaled * inverse
                ratio_ref[span] = (1.0 - MASS_TERM * inverse) * (1.0 / 6.0)
                scaled_ref[span] = scaled
                if first:
                    here[1 + r * bx:1 + (r + 1) * bx, v, c * by:(c + 1) * by] = factors[0] * scaled

        sweeps = factors[1:] if first else factors
        for order, factor in enumerate(sweeps):
            last = order + 1 == len(sweeps)
            there = out_ref if (len(sweeps) - order) % 2 == 1 else other_ref

            def step(index, carry, here=here, there=there, last=last, factor=factor):
                for x in (GROUP * index + i for i in range(GROUP)):
                    tile = [here[x + 1, j % vols, (j // vols) * by:(j // vols + 1) * by]
                            for j in range(blocks)]
                    up = [pltpu.roll(t, 1, 1) for t in tile]
                    down = [pltpu.roll(t, bz - 1, 1) for t in tile]
                    for j in range(blocks):
                        c, v = j // vols, j % vols
                        own = slice(c * by, (c + 1) * by)
                        around = here[x, v, own] + here[x + 2, v, own]
                        if c > 0:
                            around += here[x + 1, v, c * by - 1:(c + 1) * by - 1]
                        else:
                            around += jnp.where(sub == 0, 0.0, pltpu.roll(tile[j], 1, 0))
                        if c < cols - 1:
                            around += here[x + 1, v, c * by + 1:(c + 1) * by + 1]
                        else:
                            around += jnp.where(sub == by - 1, 0.0, pltpu.roll(tile[j], by - 1, 0))
                        around += jnp.where(lan == 0, up[j - 1] if v > 0 else 0.0, up[j])
                        around += jnp.where(
                            lan == bz - 1, down[j + 1] if v < vols - 1 else 0.0, down[j]
                        )
                        value = (1.0 - factor) * tile[j] + factor * (
                            scaled_ref[x, v, own] + ratio_ref[x, v, own] * around
                        )
                        there[x + 1, v, own] = value
                        if last and not first:
                            volume_ref[x // bx, j, x % bx] = value
                return carry

            lax.fori_loop(0, depth // GROUP, step, 0)
            here = there

        for r in range(rows):
            part = here[1 + r * bx:1 + (r + 1) * bx].reshape(height, bz)
            met = sum(
                jnp.dot(piece, lane_ref[r], preferred_element_type=jnp.float32)
                for piece in parts_of(part, 2)
            )
            value = jnp.sum(met * hit_ref[r].astype(jnp.float32), axis=0, keepdims=True)
            value = value - potentials[r]
            for k, mate in enumerate(MATES):
                flux_ref[r ^ mate, :, k, :] = jnp.broadcast_to(value, (blocks, targets))

    vmem = pl.BlockSpec(memory_space=pltpu.VMEM)
    operands = [source, inverse, hit, lane] + ([] if first else [parts, start])
    fluxes = jax.ShapeDtypeStruct((rows, blocks, len(MATES), targets), jnp.float32)
    field = padded if first else (rows, blocks, bx, by, bz)
    field = jax.ShapeDtypeStruct(field, jnp.float32)
    scratch = [pltpu.VMEM(padded, jnp.float32)] * (1 if first else 2)
    return pl.pallas_call(
        body,
        out_shape=[field, fluxes],
        in_specs=[vmem] * len(operands),
        out_specs=[vmem, vmem],
        scratch_shapes=scratch + [pltpu.VMEM(planes, jnp.float32)] * 2,
        name="slab_first" if first else "slab_last",
    )(*operands)


def update_call(flux, panels):
    excitations, width = flux.shape[0], panels[0].shape[1]

    def body(flux_ref, a_own, a_mate, b_own, b_mate, a_ref, b_ref):
        fluxes = [flux_ref[:, k, :].astype(jnp.bfloat16) for k in range(len(MATES))]
        for out, own, mate, k in ((a_ref, a_own, a_mate, 1), (b_ref, b_own, b_mate, 2)):
            value = jnp.dot(fluxes[0], own[...], preferred_element_type=jnp.float32)
            value += jnp.dot(fluxes[k], mate[...], preferred_element_type=jnp.float32)
            out[...] = value.astype(jnp.bfloat16)

    vmem = pl.BlockSpec(memory_space=pltpu.VMEM)
    return pl.pallas_call(
        body,
        out_shape=[jax.ShapeDtypeStruct((excitations, width), jnp.bfloat16)] * 2,
        in_specs=[vmem] * 5,
        out_specs=[vmem] * 2,
        compiler_params=pltpu.CompilerParams(vmem_limit_bytes=VMEM_BYTES),
        name="update",
    )(flux, *panels)


def potential_call(densities, halves, mates, panels):
    excitations = densities[0].shape[0]
    targets = panels[0].shape[0]

    def body(a_density, b_density, a_half, b_half, a_other, b_other,
             a_own, a_mate, b_own, b_mate, out_ref):
        rounded = [
            (density[...] + RELAXATION * (half[...].astype(jnp.float32)
                                          + other[...].astype(jnp.float32))).astype(jnp.bfloat16)
            for density, half, other in (
                (a_density, a_half, a_other), (b_density, b_half, b_other))
        ]

        def met(value, panel):
            return lax.dot_general(
                value, panel[...], (((1,), (1,)), ((), ())), preferred_element_type=jnp.float32
            )

        out_ref[:, 0, :] = met(rounded[0], a_own) + met(rounded[1], b_own)
        out_ref[:, 1, :] = met(rounded[0], a_mate)
        out_ref[:, 2, :] = met(rounded[1], b_mate)

    vmem = pl.BlockSpec(memory_space=pltpu.VMEM)
    return pl.pallas_call(
        body,
        out_shape=jax.ShapeDtypeStruct((excitations, len(MATES), targets), jnp.float32),
        in_specs=[vmem] * 10,
        out_specs=vmem,
        compiler_params=pltpu.CompilerParams(vmem_limit_bytes=VMEM_BYTES),
        name="potential",
    )(*densities, *halves, *mates, *panels)


def trace_spots(trace_count, trace_cell, targets, shape):
    _, cols, vols, _, by, bz = shape
    counts = trace_count[0]
    offsets = jnp.cumsum(counts) - counts
    slot_ids = jnp.arange(trace_cell.shape[2], dtype=jnp.int32)
    live = slot_ids[None, :] < counts[:, None]
    owner = jnp.where(live, offsets[:, None] + slot_ids[None, :], -1)
    cell = trace_cell[0]
    block_ids = jnp.arange(cols * vols, dtype=jnp.int32)[:, None]
    line = (block_ids % vols) * (cols * by) + (block_ids // vols) * by + (cell // bz) % by
    code = ((cell // (by * bz)) * (cols * vols * by) + line) * bz + cell % bz
    match = owner[:, :, None] == jnp.arange(targets, dtype=jnp.int32)
    code = jnp.sum(jnp.where(match, code[:, :, None], 0), axis=(0, 1))
    line = code // bz
    span = cols * vols * by
    return jnp.stack([line // span, line % span, code % bz])


def split_by_excitation(panel, density, source, class_index, class_values, trace_count, trace_cell):
    rows, cols, vols = (lax.axis_size(a) for a in ALL)
    blocks = cols * vols
    excitations, bx, by, bz = source.shape
    targets, nodes = panel.shape
    width = nodes // rows
    here = lax.axis_index("row")
    low, high = here & 1, here >> 1
    place = jnp.stack([lax.axis_index(a) for a in ALL]).astype(jnp.int32)
    shape = (rows, cols, vols, bx, by, bz)

    def columns(array, place):
        return lax.dynamic_slice_in_dim(array, place * width, width, 1)

    kinds = class_index.reshape(bx * by, bz).astype(jnp.bfloat16)
    kinds = stacked(kinds, "vol").reshape(vols * bx * by, bz)
    spots = trace_spots(trace_count, trace_cell, targets, shape).astype(jnp.bfloat16)
    spots = jnp.pad(spots, ((0, SPOT_ROWS - spots.shape[0]), (0, 0)))
    known = jnp.concatenate([kinds, spots])[None]
    known = jnp.concatenate([known, mated(known, "row", 1)])
    known = jnp.concatenate([known, mated(known, "row", 2)])
    spots = known[:, vols * bx * by:]
    kinds = stacked(known[:, :vols * bx * by], "col")
    kinds = kinds.reshape(cols, rows, vols, bx * by, bz)

    slab = gather_call(density, panel, source.reshape(excitations, bx * by, bz))
    slab = lax.all_to_all(slab, ALL, 0, 0, tiled=True)
    slab = slab.reshape(rows, blocks, bx * by + PART_ROWS, bz)

    panels = [columns(panel, low), None, columns(panel, 2 + high), None]
    panels[1] = mated(columns(panel, low ^ 1), "row", 1)
    panels[3] = mated(columns(panel, 2 + (high ^ 1)), "row", 2)
    densities = [columns(density, low), columns(density, 2 + high)]

    inverse, hit, lane = prepare_call(shape, place, class_values, kinds, spots)
    volume, flux = slab_call(shape, True, slab, inverse, hit, lane)
    flux = flux.reshape(excitations, len(MATES), targets)
    flux = lax.all_to_all(flux, ALL, 0, 0, tiled=True)
    halves = update_call(flux, panels)
    mates = [mated(halves[0], "row", 2), mated(halves[1], "row", 1)]
    parts = potential_call(densities, halves, mates, panels)
    parts = lax.all_to_all(parts, ALL, 0, 0, tiled=True)
    parts = parts.reshape(rows, blocks, len(MATES), targets)
    volume, flux = slab_call(shape, False, slab, inverse, hit, lane, parts, volume)
    flux = flux.reshape(excitations, len(MATES), targets)
    flux = lax.all_to_all(flux, ALL, 0, 0, tiled=True)
    volume = volume.reshape(excitations, bx, by, bz)
    volume = lax.all_to_all(volume, ALL, 0, 0, tiled=True)
    ends = update_call(flux, panels)
    end_mates = [mated(ends[0], "row", 2), mated(ends[1], "row", 1)]
    totals = []
    for group in zip(halves, mates, ends, end_mates):
        a, b, c, d = (value.astype(jnp.float32) for value in group)
        totals.append((RELAXATION * ((a + b) + (c + d))).astype(jnp.bfloat16))
    moved = [mated(totals[0], "row", 1), mated(totals[1], "row", 2)]
    change = [
        jnp.where(low == 0, totals[0], moved[0]), jnp.where(low == 0, moved[0], totals[0]),
        jnp.where(high == 0, totals[1], moved[1]), jnp.where(high == 0, moved[1], totals[1]),
    ]
    return (density + jnp.concatenate(change, axis=1).astype(jnp.float32), volume)


def padded_2(value, sides, width):
    for axis, dim in sides:
        size, length = (lax.axis_size(axis), value.shape[dim])
        up = [(i, (i + 1) % size) for i in range(size - 1)]
        down = [(j, i) for i, j in up]
        last = lax.slice_in_dim(value, length - width, length, axis=dim)
        first = lax.slice_in_dim(value, 0, width, axis=dim)
        before = lax.ppermute(last, axis, up)
        after = lax.ppermute(first, axis, down)
        value = jnp.concatenate([before, value, after], axis=dim)
    return value


def neighbours(padded):
    center = padded[..., 1:-1, 1:-1, 1:-1]
    beside_all = padded[..., 2:, 1:-1, 1:-1] + padded[..., :-2, 1:-1, 1:-1]
    beside_all = beside_all + padded[..., 1:-1, 2:, 1:-1] + padded[..., 1:-1, :-2, 1:-1]
    beside_all = beside_all + padded[..., 1:-1, 1:-1, 2:] + padded[..., 1:-1, 1:-1, :-2]
    return (center, beside_all)


def split_by_block(panel, density, source, class_index, class_values, trace_count, trace_cell):
    factors = relax_factors(SWEEPS)
    conduct = conduct_of(class_index, class_values)
    diagonal = MASS_TERM + 6.0 * conduct
    counts = trace_count[0]
    block_index = lax.axis_index(("col", "vol"))
    offsets = jnp.cumsum(counts) - counts
    target_rows = panel.shape[0]
    slot_count = trace_cell.shape[2]
    slot_ids = jnp.arange(slot_count, dtype=jnp.int32)
    target_ids = jnp.arange(target_rows, dtype=jnp.int32)
    own_count = lax.dynamic_index_in_dim(counts, block_index, keepdims=False)
    first_target = lax.dynamic_index_in_dim(offsets, block_index, keepdims=False)
    cell_ids = lax.dynamic_index_in_dim(trace_cell[0], block_index, keepdims=False)
    live_slots = slot_ids < own_count
    select = (
        ((first_target + slot_ids)[:, None] == target_ids[None, :]) & live_slots[:, None]
    ).astype(jnp.float32)
    volume = jnp.zeros(source.shape, jnp.float32)
    field_shape = volume.shape
    share_width = density.shape[1] // lax.axis_size("row")
    share_state = lax.dynamic_slice_in_dim(
        density, lax.axis_index("row") * share_width, share_width, 1
    )
    rounded = density.astype(jnp.bfloat16)
    lead = field_shape[0]
    for iteration in range(OUTER):
        partial_value = lax.dot_general(
            rounded, panel, (((1,), (1,)), ((), ())), preferred_element_type=jnp.float32
        )
        potential = lax.psum(partial_value, ("col", "vol"))
        slot_values = jnp.dot(potential, select.T, precision=lax.Precision.HIGHEST)
        right_side = source.reshape(lead, -1).at[:, cell_ids].add(slot_values).reshape(field_shape)
        relax_volume = volume
        for factor in factors:
            padded = padded_2(relax_volume, (("row", 1), ("col", 2), ("vol", 3)), 1)
            center, beside_all = neighbours(padded)
            relax_volume = (
                center + factor * (right_side - diagonal * center + conduct * beside_all) / diagonal
            )
        volume = relax_volume
        mismatch = volume.reshape(lead, -1)[:, cell_ids] - slot_values
        own_fluxes = jnp.dot(mismatch, select, precision=lax.Precision.HIGHEST)
        fluxes = lax.psum(own_fluxes, ("col", "vol"))
        update = jnp.dot(fluxes.astype(jnp.bfloat16), panel, preferred_element_type=jnp.float32)
        share_state = share_state + RELAXATION * lax.psum_scatter(
            update, "row", scatter_dimension=1, tiled=True
        )
        if iteration + 1 < OUTER:
            rounded = lax.all_gather(share_state.astype(jnp.bfloat16), "row", axis=1, tiled=True)
    density = lax.all_gather(share_state, "row", axis=1, tiled=True)
    return (density, volume)


def local(*args):
    sizes = [lax.axis_size(a) for a in ALL]
    if whole_slabs(sizes, args[0].shape[0], args[2].shape):
        return split_by_excitation(*args)
    return split_by_block(*args)


def whole_slabs(sizes, targets, block):
    fits = math.prod(sizes) == block[0] and sizes[0] == 4 and targets == block[3]
    return fits and all(size & (size - 1) == 0 for size in sizes)


def solution(mesh):
    placed = (
        P("row", ("col", "vol")),
        P(None, ("col", "vol")),
        P(None, "row", "col", "vol"),
        P("row", "col", "vol"),
        P(),
        P("row", None),
        P("row", None, None),
    )
    return jax.shard_map(
        local,
        mesh=mesh,
        in_specs=placed,
        out_specs=(P(None, ("col", "vol")), P(None, "row", "col", "vol")),
        check_vma=False,
    )
```

```python
import math

import jax
import jax.numpy as jnp
from jax import lax
from jax.experimental import pallas as pl
from jax.experimental.pallas import tpu as pltpu
from jax.sharding import PartitionSpec as P


SWEEPS = 4
OUTER = 2


MASS_TERM = 0.1
RELAXATION = 0.5
SPECTRUM_LOW = 0.1
SPECTRUM_HIGH = 2.0

ALL = ("row", "col", "vol")
SPOT_ROWS = 16
VMEM_BYTES = 16 * 2 ** 20


def relax_factors(count):
    middle = (SPECTRUM_HIGH + SPECTRUM_LOW) / 2.0
    spread = (SPECTRUM_HIGH - SPECTRUM_LOW) / 2.0
    return [
        1.0 / (middle + spread * math.cos(math.pi * (2 * order + 1) / (2 * count)))
        for order in range(count)
    ]


def conduct_of(class_index, class_values):
    classes = jnp.arange(class_values.shape[0], dtype=jnp.int32)
    return jnp.sum(
        jnp.where(
            class_index[None] == classes[:, None, None, None],
            class_values[:, None, None, None],
            jnp.float32(0.0),
        ),
        axis=0,
    )


MATES = (0, 1, 2)


def mated(value, axis, mate):
    return lax.ppermute(value, axis, [(i, i ^ mate) for i in range(lax.axis_size(axis))])


def start_call(density, panel, shape):
    rows, cols, vols = shape[:3]
    excitations, nodes = density.shape
    targets = panel.shape[0]
    width = nodes // rows

    def body(density_ref, panel_ref, part_ref, *rest):
        quarters = rest[:rows]
        nodes_ref, panel_buf, total_ref, sems = rest[rows:]
        r0, c0, v0 = (lax.axis_index(a) for a in ALL)
        low, high = r0 & 1, r0 >> 1
        loads = []
        for q in range(rows):
            span = pl.ds(q * width, width)
            loads.append((
                pltpu.make_async_copy(panel_ref.at[:, span], panel_buf.at[q], sems.at[q]),
                pltpu.make_async_copy(density_ref.at[:, span], nodes_ref.at[q], sems.at[rows + q]),
            ))
        for pair in loads:
            for copy in pair:
                copy.start()
        total = jnp.zeros((targets, excitations), jnp.float32)
        for q in range(rows):
            for copy in loads[q]:
                copy.wait()
            total += lax.dot_general(
                panel_buf[q], nodes_ref[q].astype(jnp.bfloat16), (((1,), (1,)), ((), ())),
                preferred_element_type=jnp.float32,
            )
        sources = (low, low ^ 1, 2 + high, 2 + (high ^ 1))
        stores = [
            pltpu.make_async_copy(panel_buf.at[source], quarter, sems.at[q])
            for q, (source, quarter) in enumerate(zip(sources, quarters))
        ]
        for copy in stores:
            copy.start()
        total_ref[...] = total.T
        for kc in range(cols):
            for kr in range(rows):
                for kv in range(vols):
                    owner = ((r0 ^ kr) * cols + (c0 ^ kc)) * vols + (v0 ^ kv)
                    part_ref[kc, kr, kv:kv + 1] = total_ref[pl.ds(owner, 1)]
        for copy in stores:
            copy.wait()

    hbm = pl.BlockSpec(memory_space=pltpu.HBM)
    return pl.pallas_call(
        body,
        out_shape=[jax.ShapeDtypeStruct((cols, rows, vols, targets), jnp.float32)]
        + [jax.ShapeDtypeStruct((targets, width), panel.dtype)] * rows,
        in_specs=[hbm, hbm],
        out_specs=[pl.BlockSpec(memory_space=pltpu.VMEM)] + [hbm] * rows,
        scratch_shapes=[
            pltpu.VMEM((rows, excitations, width), jnp.float32),
            pltpu.VMEM((rows, targets, width), panel.dtype),
            pltpu.VMEM((excitations, targets), jnp.float32),
            pltpu.SemaphoreType.DMA((2 * rows,)),
        ],
        name="start",
    )(density, panel)


def prepare_call(shape, values, known, other):
    rows, cols, vols, bx, by, bz = shape
    blocks = cols * vols
    height = bx * blocks * by
    lines = bx * by
    targets = known[0].shape[-1]

    def body(values_ref, *refs):
        known_refs, other_refs = refs[:rows], refs[rows:2 * rows]
        inverse_ref, hit_ref, lane_ref = refs[2 * rows:]
        r0, c0, v0 = (lax.axis_index(a) for a in ALL)
        count = values_ref.shape[0]
        row_ids = lax.broadcasted_iota(jnp.int32, (height, targets), 0)
        lane_ids = lax.broadcasted_iota(jnp.int32, (bz, targets), 0)
        for k in range(rows):
            spot = known_refs[k][vols * lines:].astype(jnp.float32).astype(jnp.int32)
            line = spot[0:1] * (blocks * by) + spot[1:2]
            hit_ref[k ^ r0] = (row_ids == line).astype(jnp.bfloat16)
            lane_ref[k ^ r0] = (lane_ids == spot[2:3]).astype(jnp.bfloat16)
        for k in range(rows):
            for kc, refs_of in enumerate((known_refs, other_refs)):
                start = pl.multiple_of((kc ^ c0) * by, by)

                def plane(kv, carry, source=refs_of[k], start=start, k=k):
                    kind = source[pl.ds(pl.multiple_of(kv * lines, lines), lines)].astype(jnp.float32)
                    conduct = jnp.zeros((lines, bz), jnp.float32)
                    for i in range(count):
                        conduct = jnp.where(kind == float(i), values_ref[i], conduct)
                    inverse = 1.0 / (MASS_TERM + 6.0 * conduct)
                    place = (pl.ds((k ^ r0) * bx, bx), kv ^ v0, pl.ds(start, by))
                    inverse_ref[place] = inverse.reshape(bx, by, bz)
                    return carry

                lax.fori_loop(0, vols, plane, 0)

    vmem = pl.BlockSpec(memory_space=pltpu.VMEM)
    return pl.pallas_call(
        body,
        out_shape=[
            jax.ShapeDtypeStruct((rows * bx, vols, cols * by, bz), jnp.float32),
            jax.ShapeDtypeStruct((rows, height, targets), jnp.bfloat16),
            jax.ShapeDtypeStruct((rows, bz, targets), jnp.bfloat16),
        ],
        in_specs=[pl.BlockSpec(memory_space=pltpu.SMEM)] + [vmem] * (2 * rows),
        out_specs=[vmem] * 3,
        name="prepare",
    )(values, *known, *other)


def parts_of(value, count):
    pieces = []
    for _ in range(count):
        piece = value.astype(jnp.bfloat16)
        pieces.append(piece)
        value = value - piece.astype(jnp.float32)
    return pieces


def slab_call(shape, first, source, inverse, hit, lane, parts, start=None):
    rows, cols, vols, bx, by, bz = shape
    blocks = cols * vols
    targets = lane.shape[-1]
    height = bx * blocks * by
    depth = rows * bx
    planes = (depth, vols, cols * by, bz)
    padded = (depth + 2, vols, cols * by, bz)
    factors = relax_factors(SWEEPS)

    def body(source_ref, inverse_ref, hit_ref, lane_ref, *rest):
        if first:
            *part_refs, out_ref, flux_ref, other_ref, scaled_ref, ratio_ref = rest
            volume_ref = None
        else:
            parts_ref, start_ref, volume_ref, flux_ref, out_ref, other_ref, scaled_ref, ratio_ref = rest
        sub = lax.broadcasted_iota(jnp.int32, (by, bz), 0)
        lan = lax.broadcasted_iota(jnp.int32, (by, bz), 1)
        for ref in (out_ref, other_ref):
            ref[0] = jnp.zeros(planes[1:], jnp.float32)
            ref[depth + 1] = jnp.zeros(planes[1:], jnp.float32)
        here = other_ref if first else start_ref
        potentials = []
        for r in range(rows):
            if first:
                place = pl.ds(r ^ lax.axis_index("row"), 1)
                potential = sum(part[place, :] for part in part_refs)
            else:
                potential = sum(
                    jnp.sum(parts_ref[r ^ mate, :, k, :], axis=0, keepdims=True)
                    for k, mate in enumerate(MATES)
                )
            potentials.append(potential)
            weights = [
                lane_ref[r] * piece.astype(jnp.bfloat16) for piece in parts_of(potential, 3)
            ]
            added = lax.dot_general(
                hit_ref[r], jnp.concatenate(weights, axis=0), (((1,), (1,)), ((), ())),
                preferred_element_type=jnp.float32,
            )
            added = added[:, :bz] + added[:, bz:2 * bz] + added[:, 2 * bz:]
            added = added.reshape(bx, vols, cols, by, bz)
            for j in range(blocks):
                c, v = j // vols, j % vols
                span = (slice(r * bx, (r + 1) * bx), v, slice(c * by, (c + 1) * by))
                scaled = source_ref[r, j] + added[:, v, c]
                inverse = inverse_ref[span]
                scaled = scaled * inverse
                ratio_ref[span] = (1.0 - MASS_TERM * inverse) * (1.0 / 6.0)
                scaled_ref[span] = scaled
                if first:
                    here[1 + r * bx:1 + (r + 1) * bx, v, c * by:(c + 1) * by] = factors[0] * scaled

        sweeps = factors[1:] if first else factors
        for order, factor in enumerate(sweeps):
            last = order + 1 == len(sweeps)
            there = out_ref if (len(sweeps) - order) % 2 == 1 else other_ref

            def step(index, carry, here=here, there=there, last=last, factor=factor):
                for x in (index,):
                    tile = [here[x + 1, j % vols, (j // vols) * by:(j // vols + 1) * by]
                            for j in range(blocks)]
                    up = [pltpu.roll(t, 1, 1) for t in tile]
                    down = [pltpu.roll(t, bz - 1, 1) for t in tile]
                    for j in range(blocks):
                        c, v = j // vols, j % vols
                        own = slice(c * by, (c + 1) * by)
                        around = here[x, v, own] + here[x + 2, v, own]
                        if c > 0:
                            around += here[x + 1, v, c * by - 1:(c + 1) * by - 1]
                        else:
                            around += jnp.where(sub == 0, 0.0, pltpu.roll(tile[j], 1, 0))
                        if c < cols - 1:
                            around += here[x + 1, v, c * by + 1:(c + 1) * by + 1]
                        else:
                            around += jnp.where(sub == by - 1, 0.0, pltpu.roll(tile[j], by - 1, 0))
                        around += jnp.where(lan == 0, up[j - 1] if v > 0 else 0.0, up[j])
                        around += jnp.where(
                            lan == bz - 1, down[j + 1] if v < vols - 1 else 0.0, down[j]
                        )
                        value = (1.0 - factor) * tile[j] + factor * (
                            scaled_ref[x, v, own] + ratio_ref[x, v, own] * around
                        )
                        there[x + 1, v, own] = value
                        if last and not first:
                            volume_ref[x // bx, j, x % bx] = value
                return carry

            for index in range(depth):
                step(index, 0)
            here = there

        for r in range(rows):
            part = here[1 + r * bx:1 + (r + 1) * bx].reshape(height, bz)
            met = sum(
                jnp.dot(piece, lane_ref[r], preferred_element_type=jnp.float32)
                for piece in parts_of(part, 2)
            )
            value = jnp.sum(met * hit_ref[r].astype(jnp.float32), axis=0, keepdims=True)
            value = value - potentials[r]
            for k, mate in enumerate(MATES):
                flux_ref[r ^ mate, :, k, :] = jnp.broadcast_to(value, (blocks, targets))

    vmem = pl.BlockSpec(memory_space=pltpu.VMEM)
    operands = [source, inverse, hit, lane] + (list(parts) if first else [parts, start])
    fluxes = jax.ShapeDtypeStruct((rows, blocks, len(MATES), targets), jnp.float32)
    field = padded if first else (rows, blocks, bx, by, bz)
    field = jax.ShapeDtypeStruct(field, jnp.float32)
    scratch = [pltpu.VMEM(padded, jnp.float32)] * (1 if first else 2)
    return pl.pallas_call(
        body,
        out_shape=[field, fluxes],
        in_specs=[vmem] * len(operands),
        out_specs=[vmem, vmem],
        scratch_shapes=scratch + [pltpu.VMEM(planes, jnp.float32)] * 2,
        name="slab_first" if first else "slab_last",
    )(*operands)


def update_call(flux, panels):
    excitations, width = flux.shape[0], panels[0].shape[1]

    def body(flux_ref, a_own, a_mate, b_own, b_mate, a_ref, b_ref):
        fluxes = [flux_ref[:, k, :].astype(jnp.bfloat16) for k in range(len(MATES))]
        for out, own, mate, k in ((a_ref, a_own, a_mate, 1), (b_ref, b_own, b_mate, 2)):
            value = jnp.dot(fluxes[0], own[...], preferred_element_type=jnp.float32)
            value += jnp.dot(fluxes[k], mate[...], preferred_element_type=jnp.float32)
            out[...] = value.astype(jnp.bfloat16)

    vmem = pl.BlockSpec(memory_space=pltpu.VMEM)
    return pl.pallas_call(
        body,
        out_shape=[jax.ShapeDtypeStruct((excitations, width), jnp.bfloat16)] * 2,
        in_specs=[vmem] * 5,
        out_specs=[vmem] * 2,
        compiler_params=pltpu.CompilerParams(vmem_limit_bytes=VMEM_BYTES),
        name="update",
    )(flux, *panels)


def potential_call(densities, halves, mates, panels):
    excitations = densities[0].shape[0]
    targets = panels[0].shape[0]

    def body(a_density, b_density, a_half, b_half, a_other, b_other,
             a_own, a_mate, b_own, b_mate, out_ref):
        rounded = [
            (density[...] + RELAXATION * (half[...].astype(jnp.float32)
                                          + other[...].astype(jnp.float32))).astype(jnp.bfloat16)
            for density, half, other in (
                (a_density, a_half, a_other), (b_density, b_half, b_other))
        ]

        def met(value, panel):
            return lax.dot_general(
                value, panel[...], (((1,), (1,)), ((), ())), preferred_element_type=jnp.float32
            )

        out_ref[:, 0, :] = met(rounded[0], a_own) + met(rounded[1], b_own)
        out_ref[:, 1, :] = met(rounded[0], a_mate)
        out_ref[:, 2, :] = met(rounded[1], b_mate)

    vmem = pl.BlockSpec(memory_space=pltpu.VMEM)
    return pl.pallas_call(
        body,
        out_shape=jax.ShapeDtypeStruct((excitations, len(MATES), targets), jnp.float32),
        in_specs=[vmem] * 10,
        out_specs=vmem,
        compiler_params=pltpu.CompilerParams(vmem_limit_bytes=VMEM_BYTES),
        name="potential",
    )(*densities, *halves, *mates, *panels)


def trace_spots(trace_count, trace_cell, targets, shape):
    _, cols, vols, _, by, bz = shape
    counts = trace_count[0]
    offsets = jnp.cumsum(counts) - counts
    slot_ids = jnp.arange(trace_cell.shape[2], dtype=jnp.int32)
    live = slot_ids[None, :] < counts[:, None]
    owner = jnp.where(live, offsets[:, None] + slot_ids[None, :], -1)
    cell = trace_cell[0]
    block_ids = jnp.arange(cols * vols, dtype=jnp.int32)[:, None]
    line = (block_ids % vols) * (cols * by) + (block_ids // vols) * by + (cell // bz) % by
    code = ((cell // (by * bz)) * (cols * vols * by) + line) * bz + cell % bz
    match = owner[:, :, None] == jnp.arange(targets, dtype=jnp.int32)
    code = jnp.sum(jnp.where(match, code[:, :, None], 0), axis=(0, 1))
    line = code // bz
    span = cols * vols * by
    return jnp.stack([line // span, line % span, code % bz])


def split_by_excitation(panel, density, source, class_index, class_values, trace_count, trace_cell):
    rows, cols, vols = (lax.axis_size(a) for a in ALL)
    blocks = cols * vols
    excitations, bx, by, bz = source.shape
    targets, nodes = panel.shape
    width = nodes // rows
    here = lax.axis_index("row")
    low, high = here & 1, here >> 1
    shape = (rows, cols, vols, bx, by, bz)

    def columns(array, place):
        return lax.dynamic_slice_in_dim(array, place * width, width, 1)

    def around_axis(pieces, axis):
        return [pieces[0]] + [mated(piece, axis, k) for k, piece in enumerate(pieces) if k > 0]

    parts, *quarters = start_call(density, panel, shape)

    kinds = class_index.reshape(bx * by, bz).astype(jnp.bfloat16)
    kinds = around_axis([kinds] * vols, "vol")
    parts = parts[0] + mated(parts[1], "col", 1)
    slab = lax.all_to_all(source, ALL, 0, 0, tiled=True)
    slab = slab.reshape(rows, blocks, bx, by, bz)
    parts = jnp.stack(around_axis([parts[k] for k in range(rows)], "row"))
    spots = trace_spots(trace_count, trace_cell, targets, shape).astype(jnp.bfloat16)
    spots = jnp.pad(spots, ((0, SPOT_ROWS - spots.shape[0]), (0, 0)))
    known = jnp.concatenate(kinds + [spots])
    known = around_axis([known] * rows, "row")
    parts = around_axis([parts[:, k] for k in range(vols)], "vol")
    other = [mated(piece, "col", 1) for piece in known]

    panels = [quarters[0], None, quarters[2], None]
    panels[1] = mated(quarters[1], "row", 1)
    panels[3] = mated(quarters[3], "row", 2)
    densities = [columns(density, low), columns(density, 2 + high)]

    inverse, hit, lane = prepare_call(shape, class_values, known, other)
    volume, flux = slab_call(shape, True, slab, inverse, hit, lane, parts)
    flux = flux.reshape(excitations, len(MATES), targets)
    flux = lax.all_to_all(flux, ALL, 0, 0, tiled=True)
    halves = update_call(flux, panels)
    mates = [mated(halves[0], "row", 2), mated(halves[1], "row", 1)]
    parts = potential_call(densities, halves, mates, panels)
    parts = lax.all_to_all(parts, ALL, 0, 0, tiled=True)
    parts = parts.reshape(rows, blocks, len(MATES), targets)
    volume, flux = slab_call(shape, False, slab, inverse, hit, lane, parts, volume)
    flux = flux.reshape(excitations, len(MATES), targets)
    flux = lax.all_to_all(flux, ALL, 0, 0, tiled=True)
    volume = volume.reshape(excitations, bx, by, bz)
    volume = lax.all_to_all(volume, ALL, 0, 0, tiled=True)
    ends = update_call(flux, panels)
    end_mates = [mated(ends[0], "row", 2), mated(ends[1], "row", 1)]
    totals = []
    for group in zip(halves, mates, ends, end_mates):
        a, b, c, d = (value.astype(jnp.float32) for value in group)
        totals.append((RELAXATION * ((a + b) + (c + d))).astype(jnp.bfloat16))
    moved = [mated(totals[0], "row", 1), mated(totals[1], "row", 2)]
    change = [
        jnp.where(low == 0, totals[0], moved[0]), jnp.where(low == 0, moved[0], totals[0]),
        jnp.where(high == 0, totals[1], moved[1]), jnp.where(high == 0, moved[1], totals[1]),
    ]
    density = density + jnp.concatenate(change, axis=1).astype(jnp.float32)
    return (density, volume)


def padded_2(value, sides, width):
    for axis, dim in sides:
        size, length = (lax.axis_size(axis), value.shape[dim])
        up = [(i, (i + 1) % size) for i in range(size - 1)]
        down = [(j, i) for i, j in up]
        last = lax.slice_in_dim(value, length - width, length, axis=dim)
        first = lax.slice_in_dim(value, 0, width, axis=dim)
        before = lax.ppermute(last, axis, up)
        after = lax.ppermute(first, axis, down)
        value = jnp.concatenate([before, value, after], axis=dim)
    return value


def neighbours(padded):
    center = padded[..., 1:-1, 1:-1, 1:-1]
    beside_all = padded[..., 2:, 1:-1, 1:-1] + padded[..., :-2, 1:-1, 1:-1]
    beside_all = beside_all + padded[..., 1:-1, 2:, 1:-1] + padded[..., 1:-1, :-2, 1:-1]
    beside_all = beside_all + padded[..., 1:-1, 1:-1, 2:] + padded[..., 1:-1, 1:-1, :-2]
    return (center, beside_all)


def split_by_block(panel, density, source, class_index, class_values, trace_count, trace_cell):
    factors = relax_factors(SWEEPS)
    conduct = conduct_of(class_index, class_values)
    diagonal = MASS_TERM + 6.0 * conduct
    counts = trace_count[0]
    block_index = lax.axis_index(("col", "vol"))
    offsets = jnp.cumsum(counts) - counts
    target_rows = panel.shape[0]
    slot_count = trace_cell.shape[2]
    slot_ids = jnp.arange(slot_count, dtype=jnp.int32)
    target_ids = jnp.arange(target_rows, dtype=jnp.int32)
    own_count = lax.dynamic_index_in_dim(counts, block_index, keepdims=False)
    first_target = lax.dynamic_index_in_dim(offsets, block_index, keepdims=False)
    cell_ids = lax.dynamic_index_in_dim(trace_cell[0], block_index, keepdims=False)
    live_slots = slot_ids < own_count
    select = (
        ((first_target + slot_ids)[:, None] == target_ids[None, :]) & live_slots[:, None]
    ).astype(jnp.float32)
    volume = jnp.zeros(source.shape, jnp.float32)
    field_shape = volume.shape
    share_width = density.shape[1] // lax.axis_size("row")
    share_state = lax.dynamic_slice_in_dim(
        density, lax.axis_index("row") * share_width, share_width, 1
    )
    rounded = density.astype(jnp.bfloat16)
    lead = field_shape[0]
    for iteration in range(OUTER):
        partial_value = lax.dot_general(
            rounded, panel, (((1,), (1,)), ((), ())), preferred_element_type=jnp.float32
        )
        potential = lax.psum(partial_value, ("col", "vol"))
        slot_values = jnp.dot(potential, select.T, precision=lax.Precision.HIGHEST)
        right_side = source.reshape(lead, -1).at[:, cell_ids].add(slot_values).reshape(field_shape)
        relax_volume = volume
        for factor in factors:
            padded = padded_2(relax_volume, (("row", 1), ("col", 2), ("vol", 3)), 1)
            center, beside_all = neighbours(padded)
            relax_volume = (
                center + factor * (right_side - diagonal * center + conduct * beside_all) / diagonal
            )
        volume = relax_volume
        mismatch = volume.reshape(lead, -1)[:, cell_ids] - slot_values
        own_fluxes = jnp.dot(mismatch, select, precision=lax.Precision.HIGHEST)
        fluxes = lax.psum(own_fluxes, ("col", "vol"))
        update = jnp.dot(fluxes.astype(jnp.bfloat16), panel, preferred_element_type=jnp.float32)
        share_state = share_state + RELAXATION * lax.psum_scatter(
            update, "row", scatter_dimension=1, tiled=True
        )
        if iteration + 1 < OUTER:
            rounded = lax.all_gather(share_state.astype(jnp.bfloat16), "row", axis=1, tiled=True)
    density = lax.all_gather(share_state, "row", axis=1, tiled=True)
    return (density, volume)


def local(*args):
    sizes = [lax.axis_size(a) for a in ALL]
    if whole_slabs(sizes, args[0].shape[0], args[2].shape):
        return split_by_excitation(*args)
    return split_by_block(*args)


def whole_slabs(sizes, targets, block):
    fits = math.prod(sizes) == block[0] and sizes[0] == 4 and targets == block[3]
    return fits and all(size & (size - 1) == 0 for size in sizes)


def solution(mesh):
    placed = (
        P("row", ("col", "vol")),
        P(None, ("col", "vol")),
        P(None, "row", "col", "vol"),
        P("row", "col", "vol"),
        P(),
        P("row", None),
        P("row", None, None),
    )
    return jax.shard_map(
        local,
        mesh=mesh,
        in_specs=placed,
        out_specs=(P(None, ("col", "vol")), P(None, "row", "col", "vol")),
        check_vma=False,
    )
```

```python
import math

import jax
import jax.numpy as jnp
from jax import lax
from jax.experimental import pallas as pl
from jax.experimental.pallas import tpu as pltpu
from jax.sharding import PartitionSpec as P


SWEEPS = 4
OUTER = 2


MASS_TERM = 0.1
RELAXATION = 0.5
SPECTRUM_LOW = 0.1
SPECTRUM_HIGH = 2.0

ALL = ("row", "col", "vol")
SPOT_ROWS = 16
VMEM_BYTES = 16 * 2 ** 20


def relax_factors(count):
    middle = (SPECTRUM_HIGH + SPECTRUM_LOW) / 2.0
    spread = (SPECTRUM_HIGH - SPECTRUM_LOW) / 2.0
    return [
        1.0 / (middle + spread * math.cos(math.pi * (2 * order + 1) / (2 * count)))
        for order in range(count)
    ]


def conduct_of(class_index, class_values):
    classes = jnp.arange(class_values.shape[0], dtype=jnp.int32)
    return jnp.sum(
        jnp.where(
            class_index[None] == classes[:, None, None, None],
            class_values[:, None, None, None],
            jnp.float32(0.0),
        ),
        axis=0,
    )


MATES = (0, 1, 2)


def mated(value, axis, mate):
    return lax.ppermute(value, axis, [(i, i ^ mate) for i in range(lax.axis_size(axis))])


def start_call(density, panel, shape):
    rows, cols, vols = shape[:3]
    excitations, nodes = density.shape
    targets = panel.shape[0]
    width = nodes // rows

    def body(density_ref, panel_ref, part_ref, *rest):
        quarters = rest[:rows]
        nodes_ref, panel_buf, total_ref, sems = rest[rows:]
        r0, c0, v0 = (lax.axis_index(a) for a in ALL)
        low, high = r0 & 1, r0 >> 1
        sources = (low, low ^ 1, 2 + high, 2 + (high ^ 1))
        order = (1, 3, 0, 2)
        loads, stores = [], []
        for q in order:
            span = pl.ds(pl.multiple_of(sources[q] * width, width), width)
            pair = (
                pltpu.make_async_copy(panel_ref.at[:, span], panel_buf.at[q], sems.at[q]),
                pltpu.make_async_copy(density_ref.at[:, span], nodes_ref.at[q], sems.at[rows + q]),
            )
            for copy in pair:
                copy.start()
            loads.append(pair)
        total = jnp.zeros((targets, excitations), jnp.float32)
        for q, pair in zip(order, loads):
            for copy in pair:
                copy.wait()
            store = pltpu.make_async_copy(panel_buf.at[q], quarters[q], sems.at[2 * rows + q])
            store.start()
            stores.append(store)
            total += lax.dot_general(
                panel_buf[q], nodes_ref[q].astype(jnp.bfloat16), (((1,), (1,)), ((), ())),
                preferred_element_type=jnp.float32,
            )
        total_ref[...] = total.T
        for kc in range(cols):
            for kr in range(rows):
                for kv in range(vols):
                    owner = ((r0 ^ kr) * cols + (c0 ^ kc)) * vols + (v0 ^ kv)
                    part_ref[kc, kr, kv:kv + 1] = total_ref[pl.ds(owner, 1)]
        for copy in stores:
            copy.wait()

    hbm = pl.BlockSpec(memory_space=pltpu.HBM)
    return pl.pallas_call(
        body,
        out_shape=[jax.ShapeDtypeStruct((cols, rows, vols, targets), jnp.float32)]
        + [jax.ShapeDtypeStruct((targets, width), panel.dtype)] * rows,
        in_specs=[hbm, hbm],
        out_specs=[pl.BlockSpec(memory_space=pltpu.VMEM)] + [hbm] * rows,
        scratch_shapes=[
            pltpu.VMEM((rows, excitations, width), jnp.float32),
            pltpu.VMEM((rows, targets, width), panel.dtype),
            pltpu.VMEM((excitations, targets), jnp.float32),
            pltpu.SemaphoreType.DMA((3 * rows,)),
        ],
        name="start",
    )(density, panel)


def prepare_call(shape, values, known, other):
    rows, cols, vols, bx, by, bz = shape
    blocks = cols * vols
    height = bx * blocks * by
    lines = bx * by
    targets = known[0].shape[-1]

    def body(values_ref, *refs):
        known_refs, other_refs = refs[:rows], refs[rows:2 * rows]
        inverse_ref, hit_ref, lane_ref = refs[2 * rows:]
        r0, c0, v0 = (lax.axis_index(a) for a in ALL)
        count = values_ref.shape[0]
        row_ids = lax.broadcasted_iota(jnp.int32, (height, targets), 0)
        lane_ids = lax.broadcasted_iota(jnp.int32, (bz, targets), 0)
        for k in range(rows):
            spot = known_refs[k][vols * lines:].astype(jnp.float32).astype(jnp.int32)
            line = spot[0:1] * (blocks * by) + spot[1:2]
            hit_ref[k ^ r0] = (row_ids == line).astype(jnp.bfloat16)
            lane_ref[k ^ r0] = (lane_ids == spot[2:3]).astype(jnp.bfloat16)
        for k in range(rows):
            for kc, refs_of in enumerate((known_refs, other_refs)):
                start = pl.multiple_of((kc ^ c0) * by, by)

                def plane(kv, carry, source=refs_of[k], start=start, k=k):
                    kind = source[pl.ds(pl.multiple_of(kv * lines, lines), lines)].astype(jnp.float32)
                    conduct = jnp.zeros((lines, bz), jnp.float32)
                    for i in range(count):
                        conduct = jnp.where(kind == float(i), values_ref[i], conduct)
                    inverse = 1.0 / (MASS_TERM + 6.0 * conduct)
                    place = (pl.ds((k ^ r0) * bx, bx), kv ^ v0, pl.ds(start, by))
                    inverse_ref[place] = inverse.reshape(bx, by, bz)
                    return carry

                lax.fori_loop(0, vols, plane, 0)

    vmem = pl.BlockSpec(memory_space=pltpu.VMEM)
    return pl.pallas_call(
        body,
        out_shape=[
            jax.ShapeDtypeStruct((rows * bx, vols, cols * by, bz), jnp.float32),
            jax.ShapeDtypeStruct((rows, height, targets), jnp.bfloat16),
            jax.ShapeDtypeStruct((rows, bz, targets), jnp.bfloat16),
        ],
        in_specs=[pl.BlockSpec(memory_space=pltpu.SMEM)] + [vmem] * (2 * rows),
        out_specs=[vmem] * 3,
        name="prepare",
    )(values, *known, *other)


def landed_call(volume):
    excitations = volume.shape[0]
    few = math.gcd(excitations, 8)
    block = pl.BlockSpec((few,) + volume.shape[1:], lambda i: (i, 0, 0, 0))

    def body(in_ref, out_ref):
        out_ref[...] = in_ref[...]

    return pl.pallas_call(
        body,
        grid=(excitations // few,),
        out_shape=jax.ShapeDtypeStruct(volume.shape, volume.dtype),
        in_specs=[block],
        out_specs=block,
        name="landed",
    )(volume)


def parts_of(value, count):
    pieces = []
    for _ in range(count):
        piece = value.astype(jnp.bfloat16)
        pieces.append(piece)
        value = value - piece.astype(jnp.float32)
    return pieces


def slab_call(shape, first, source, inverse, hit, lane, parts, start=None):
    rows, cols, vols, bx, by, bz = shape
    blocks = cols * vols
    targets = lane.shape[-1]
    height = bx * blocks * by
    depth = rows * bx
    planes = (depth, vols, cols * by, bz)
    padded = (depth + 2, vols, cols * by, bz)
    factors = relax_factors(SWEEPS)

    def body(source_ref, inverse_ref, hit_ref, lane_ref, *rest):
        if first:
            *part_refs, out_ref, flux_ref, other_ref, scaled_ref, ratio_ref = rest
            volume_ref = None
        else:
            parts_ref, start_ref, volume_ref, flux_ref, out_ref, other_ref, scaled_ref, ratio_ref = rest
        sub = lax.broadcasted_iota(jnp.int32, (by, bz), 0)
        lan = lax.broadcasted_iota(jnp.int32, (by, bz), 1)
        for ref in (out_ref, other_ref):
            ref[0] = jnp.zeros(planes[1:], jnp.float32)
            ref[depth + 1] = jnp.zeros(planes[1:], jnp.float32)
        here = other_ref if first else start_ref
        potentials = []
        for r in range(rows):
            if first:
                place = pl.ds(r ^ lax.axis_index("row"), 1)
                potential = sum(part[place, :] for part in part_refs)
            else:
                potential = sum(
                    jnp.sum(parts_ref[r ^ mate, :, k, :], axis=0, keepdims=True)
                    for k, mate in enumerate(MATES)
                )
            potentials.append(potential)
            weights = [
                lane_ref[r] * piece.astype(jnp.bfloat16) for piece in parts_of(potential, 3)
            ]
            added = lax.dot_general(
                hit_ref[r], jnp.concatenate(weights, axis=0), (((1,), (1,)), ((), ())),
                preferred_element_type=jnp.float32,
            )
            added = added[:, :bz] + added[:, bz:2 * bz] + added[:, 2 * bz:]
            added = added.reshape(bx, vols, cols, by, bz)
            for j in range(blocks):
                c, v = j // vols, j % vols
                span = (slice(r * bx, (r + 1) * bx), v, slice(c * by, (c + 1) * by))
                scaled = source_ref[r, j] + added[:, v, c]
                inverse = inverse_ref[span]
                scaled = scaled * inverse
                ratio_ref[span] = (1.0 - MASS_TERM * inverse) * (1.0 / 6.0)
                scaled_ref[span] = scaled
                if first:
                    here[1 + r * bx:1 + (r + 1) * bx, v, c * by:(c + 1) * by] = factors[0] * scaled

        sweeps = factors[1:] if first else factors
        for order, factor in enumerate(sweeps):
            last = order + 1 == len(sweeps)
            there = out_ref if (len(sweeps) - order) % 2 == 1 else other_ref

            def step(index, carry, here=here, there=there, last=last, factor=factor):
                for x in (index,):
                    tile = [here[x + 1, j % vols, (j // vols) * by:(j // vols + 1) * by]
                            for j in range(blocks)]
                    up = [pltpu.roll(t, 1, 1) for t in tile]
                    down = [pltpu.roll(t, bz - 1, 1) for t in tile]
                    for j in range(blocks):
                        c, v = j // vols, j % vols
                        own = slice(c * by, (c + 1) * by)
                        around = here[x, v, own] + here[x + 2, v, own]
                        if c > 0:
                            around += here[x + 1, v, c * by - 1:(c + 1) * by - 1]
                        else:
                            around += jnp.where(sub == 0, 0.0, pltpu.roll(tile[j], 1, 0))
                        if c < cols - 1:
                            around += here[x + 1, v, c * by + 1:(c + 1) * by + 1]
                        else:
                            around += jnp.where(sub == by - 1, 0.0, pltpu.roll(tile[j], by - 1, 0))
                        around += jnp.where(lan == 0, up[j - 1] if v > 0 else 0.0, up[j])
                        around += jnp.where(
                            lan == bz - 1, down[j + 1] if v < vols - 1 else 0.0, down[j]
                        )
                        value = (1.0 - factor) * tile[j] + factor * (
                            scaled_ref[x, v, own] + ratio_ref[x, v, own] * around
                        )
                        there[x + 1, v, own] = value
                        if last and not first:
                            volume_ref[x // bx, j, x % bx] = value
                return carry

            for index in range(depth):
                step(index, 0)
            here = there

        for r in range(rows):
            part = here[1 + r * bx:1 + (r + 1) * bx].reshape(height, bz)
            met = sum(
                jnp.dot(piece, lane_ref[r], preferred_element_type=jnp.float32)
                for piece in parts_of(part, 2)
            )
            value = jnp.sum(met * hit_ref[r].astype(jnp.float32), axis=0, keepdims=True)
            value = value - potentials[r]
            for k, mate in enumerate(MATES):
                flux_ref[r ^ mate, :, k, :] = jnp.broadcast_to(value, (blocks, targets))

    vmem = pl.BlockSpec(memory_space=pltpu.VMEM)
    operands = [source, inverse, hit, lane] + (list(parts) if first else [parts, start])
    fluxes = jax.ShapeDtypeStruct((rows, blocks, len(MATES), targets), jnp.float32)
    field = padded if first else (rows, blocks, bx, by, bz)
    field = jax.ShapeDtypeStruct(field, jnp.float32)
    scratch = [pltpu.VMEM(padded, jnp.float32)] * (1 if first else 2)
    return pl.pallas_call(
        body,
        out_shape=[field, fluxes],
        in_specs=[vmem] * len(operands),
        out_specs=[vmem, vmem],
        scratch_shapes=scratch + [pltpu.VMEM(planes, jnp.float32)] * 2,
        name="slab_first" if first else "slab_last",
    )(*operands)


def update_call(flux, panels):
    excitations, width = flux.shape[0], panels[0].shape[1]

    def body(flux_ref, a_own, a_mate, b_own, b_mate, a_ref, b_ref):
        fluxes = [flux_ref[:, k, :].astype(jnp.bfloat16) for k in range(len(MATES))]
        for out, own, mate, k in ((a_ref, a_own, a_mate, 1), (b_ref, b_own, b_mate, 2)):
            value = jnp.dot(fluxes[0], own[...], preferred_element_type=jnp.float32)
            value += jnp.dot(fluxes[k], mate[...], preferred_element_type=jnp.float32)
            out[...] = value.astype(jnp.bfloat16)

    vmem = pl.BlockSpec(memory_space=pltpu.VMEM)
    return pl.pallas_call(
        body,
        out_shape=[jax.ShapeDtypeStruct((excitations, width), jnp.bfloat16)] * 2,
        in_specs=[vmem] * 5,
        out_specs=[vmem] * 2,
        compiler_params=pltpu.CompilerParams(vmem_limit_bytes=VMEM_BYTES),
        name="update",
    )(flux, *panels)


def potential_call(densities, halves, mates, panels):
    excitations = densities[0].shape[0]
    targets = panels[0].shape[0]

    def body(a_density, b_density, a_half, b_half, a_other, b_other,
             a_own, a_mate, b_own, b_mate, out_ref):
        rounded = [
            (density[...] + RELAXATION * (half[...].astype(jnp.float32)
                                          + other[...].astype(jnp.float32))).astype(jnp.bfloat16)
            for density, half, other in (
                (a_density, a_half, a_other), (b_density, b_half, b_other))
        ]

        def met(value, panel):
            return lax.dot_general(
                value, panel[...], (((1,), (1,)), ((), ())), preferred_element_type=jnp.float32
            )

        out_ref[:, 0, :] = met(rounded[0], a_own) + met(rounded[1], b_own)
        out_ref[:, 1, :] = met(rounded[0], a_mate)
        out_ref[:, 2, :] = met(rounded[1], b_mate)

    vmem = pl.BlockSpec(memory_space=pltpu.VMEM)
    return pl.pallas_call(
        body,
        out_shape=jax.ShapeDtypeStruct((excitations, len(MATES), targets), jnp.float32),
        in_specs=[vmem] * 10,
        out_specs=vmem,
        compiler_params=pltpu.CompilerParams(vmem_limit_bytes=VMEM_BYTES),
        name="potential",
    )(*densities, *halves, *mates, *panels)


def trace_spots(trace_count, trace_cell, targets, shape):
    _, cols, vols, _, by, bz = shape
    counts = trace_count[0]
    offsets = jnp.cumsum(counts) - counts
    slot_ids = jnp.arange(trace_cell.shape[2], dtype=jnp.int32)
    live = slot_ids[None, :] < counts[:, None]
    owner = jnp.where(live, offsets[:, None] + slot_ids[None, :], -1)
    cell = trace_cell[0]
    block_ids = jnp.arange(cols * vols, dtype=jnp.int32)[:, None]
    line = (block_ids % vols) * (cols * by) + (block_ids // vols) * by + (cell // bz) % by
    code = ((cell // (by * bz)) * (cols * vols * by) + line) * bz + cell % bz
    match = owner[:, :, None] == jnp.arange(targets, dtype=jnp.int32)
    code = jnp.sum(jnp.where(match, code[:, :, None], 0), axis=(0, 1))
    line = code // bz
    span = cols * vols * by
    return jnp.stack([line // span, line % span, code % bz])


def split_by_excitation(panel, density, source, class_index, class_values, trace_count, trace_cell):
    rows, cols, vols = (lax.axis_size(a) for a in ALL)
    blocks = cols * vols
    excitations, bx, by, bz = source.shape
    targets, nodes = panel.shape
    width = nodes // rows
    here = lax.axis_index("row")
    low, high = here & 1, here >> 1
    shape = (rows, cols, vols, bx, by, bz)

    def columns(array, place):
        return lax.dynamic_slice_in_dim(array, place * width, width, 1)

    def around_axis(pieces, axis):
        return [pieces[0]] + [mated(piece, axis, k) for k, piece in enumerate(pieces) if k > 0]

    parts, *quarters = start_call(density, panel, shape)

    kinds = class_index.reshape(bx * by, bz).astype(jnp.bfloat16)
    kinds = around_axis([kinds] * vols, "vol")
    parts = parts[0] + mated(parts[1], "col", 1)
    slab = lax.all_to_all(source, ALL, 0, 0, tiled=True)
    slab = slab.reshape(rows, blocks, bx, by, bz)
    parts = jnp.stack(around_axis([parts[k] for k in range(rows)], "row"))
    spots = trace_spots(trace_count, trace_cell, targets, shape).astype(jnp.bfloat16)
    spots = jnp.pad(spots, ((0, SPOT_ROWS - spots.shape[0]), (0, 0)))
    known = jnp.concatenate(kinds + [spots])
    known = around_axis([known] * rows, "row")
    parts = around_axis([parts[:, k] for k in range(vols)], "vol")
    other = [mated(piece, "col", 1) for piece in known]

    panels = [quarters[0], None, quarters[2], None]
    panels[1] = mated(quarters[1], "row", 1)
    panels[3] = mated(quarters[3], "row", 2)
    densities = [columns(density, low), columns(density, 2 + high)]

    inverse, hit, lane = prepare_call(shape, class_values, known, other)
    volume, flux = slab_call(shape, True, slab, inverse, hit, lane, parts)
    flux = flux.reshape(excitations, len(MATES), targets)
    flux = lax.all_to_all(flux, ALL, 0, 0, tiled=True)
    halves = update_call(flux, panels)
    mates = [mated(halves[0], "row", 2), mated(halves[1], "row", 1)]
    parts = potential_call(densities, halves, mates, panels)
    parts = lax.all_to_all(parts, ALL, 0, 0, tiled=True)
    parts = parts.reshape(rows, blocks, len(MATES), targets)
    volume, flux = slab_call(shape, False, slab, inverse, hit, lane, parts, volume)
    flux = flux.reshape(excitations, len(MATES), targets)
    flux = lax.all_to_all(flux, ALL, 0, 0, tiled=True)
    volume = volume.reshape(excitations, bx, by, bz)
    volume = lax.all_to_all(volume, ALL, 0, 0, tiled=True)
    volume = landed_call(volume)
    ends = update_call(flux, panels)
    end_mates = [mated(ends[0], "row", 2), mated(ends[1], "row", 1)]
    totals = []
    for group in zip(halves, mates, ends, end_mates):
        a, b, c, d = (value.astype(jnp.float32) for value in group)
        totals.append((RELAXATION * ((a + b) + (c + d))).astype(jnp.bfloat16))
    moved = [mated(totals[0], "row", 1), mated(totals[1], "row", 2)]
    change = [
        jnp.where(low == 0, totals[0], moved[0]), jnp.where(low == 0, moved[0], totals[0]),
        jnp.where(high == 0, totals[1], moved[1]), jnp.where(high == 0, moved[1], totals[1]),
    ]
    density = density + jnp.concatenate(change, axis=1).astype(jnp.float32)
    return (density, volume)


def padded_2(value, sides, width):
    for axis, dim in sides:
        size, length = (lax.axis_size(axis), value.shape[dim])
        up = [(i, (i + 1) % size) for i in range(size - 1)]
        down = [(j, i) for i, j in up]
        last = lax.slice_in_dim(value, length - width, length, axis=dim)
        first = lax.slice_in_dim(value, 0, width, axis=dim)
        before = lax.ppermute(last, axis, up)
        after = lax.ppermute(first, axis, down)
        value = jnp.concatenate([before, value, after], axis=dim)
    return value


def neighbours(padded):
    center = padded[..., 1:-1, 1:-1, 1:-1]
    beside_all = padded[..., 2:, 1:-1, 1:-1] + padded[..., :-2, 1:-1, 1:-1]
    beside_all = beside_all + padded[..., 1:-1, 2:, 1:-1] + padded[..., 1:-1, :-2, 1:-1]
    beside_all = beside_all + padded[..., 1:-1, 1:-1, 2:] + padded[..., 1:-1, 1:-1, :-2]
    return (center, beside_all)


def split_by_block(panel, density, source, class_index, class_values, trace_count, trace_cell):
    factors = relax_factors(SWEEPS)
    conduct = conduct_of(class_index, class_values)
    diagonal = MASS_TERM + 6.0 * conduct
    counts = trace_count[0]
    block_index = lax.axis_index(("col", "vol"))
    offsets = jnp.cumsum(counts) - counts
    target_rows = panel.shape[0]
    slot_count = trace_cell.shape[2]
    slot_ids = jnp.arange(slot_count, dtype=jnp.int32)
    target_ids = jnp.arange(target_rows, dtype=jnp.int32)
    own_count = lax.dynamic_index_in_dim(counts, block_index, keepdims=False)
    first_target = lax.dynamic_index_in_dim(offsets, block_index, keepdims=False)
    cell_ids = lax.dynamic_index_in_dim(trace_cell[0], block_index, keepdims=False)
    live_slots = slot_ids < own_count
    select = (
        ((first_target + slot_ids)[:, None] == target_ids[None, :]) & live_slots[:, None]
    ).astype(jnp.float32)
    volume = jnp.zeros(source.shape, jnp.float32)
    field_shape = volume.shape
    share_width = density.shape[1] // lax.axis_size("row")
    share_state = lax.dynamic_slice_in_dim(
        density, lax.axis_index("row") * share_width, share_width, 1
    )
    rounded = density.astype(jnp.bfloat16)
    lead = field_shape[0]
    for iteration in range(OUTER):
        partial_value = lax.dot_general(
            rounded, panel, (((1,), (1,)), ((), ())), preferred_element_type=jnp.float32
        )
        potential = lax.psum(partial_value, ("col", "vol"))
        slot_values = jnp.dot(potential, select.T, precision=lax.Precision.HIGHEST)
        right_side = source.reshape(lead, -1).at[:, cell_ids].add(slot_values).reshape(field_shape)
        relax_volume = volume
        for factor in factors:
            padded = padded_2(relax_volume, (("row", 1), ("col", 2), ("vol", 3)), 1)
            center, beside_all = neighbours(padded)
            relax_volume = (
                center + factor * (right_side - diagonal * center + conduct * beside_all) / diagonal
            )
        volume = relax_volume
        mismatch = volume.reshape(lead, -1)[:, cell_ids] - slot_values
        own_fluxes = jnp.dot(mismatch, select, precision=lax.Precision.HIGHEST)
        fluxes = lax.psum(own_fluxes, ("col", "vol"))
        update = jnp.dot(fluxes.astype(jnp.bfloat16), panel, preferred_element_type=jnp.float32)
        share_state = share_state + RELAXATION * lax.psum_scatter(
            update, "row", scatter_dimension=1, tiled=True
        )
        if iteration + 1 < OUTER:
            rounded = lax.all_gather(share_state.astype(jnp.bfloat16), "row", axis=1, tiled=True)
    density = lax.all_gather(share_state, "row", axis=1, tiled=True)
    return (density, volume)


def local(*args):
    sizes = [lax.axis_size(a) for a in ALL]
    if whole_slabs(sizes, args[0].shape[0], args[2].shape):
        return split_by_excitation(*args)
    return split_by_block(*args)


def whole_slabs(sizes, targets, block):
    fits = math.prod(sizes) == block[0] and sizes[0] == 4 and targets == block[3]
    return fits and all(size & (size - 1) == 0 for size in sizes)


def solution(mesh):
    placed = (
        P("row", ("col", "vol")),
        P(None, ("col", "vol")),
        P(None, "row", "col", "vol"),
        P("row", "col", "vol"),
        P(),
        P("row", None),
        P("row", None, None),
    )
    return jax.shard_map(
        local,
        mesh=mesh,
        in_specs=placed,
        out_specs=(P(None, ("col", "vol")), P(None, "row", "col", "vol")),
        check_vma=False,
    )
```

```python
import math

import jax
import jax.numpy as jnp
from jax import lax
from jax.experimental import pallas as pl
from jax.experimental.pallas import tpu as pltpu
from jax.sharding import PartitionSpec as P


SWEEPS = 4
OUTER = 2


MASS_TERM = 0.1
RELAXATION = 0.5
SPECTRUM_LOW = 0.1
SPECTRUM_HIGH = 2.0

ALL = ("row", "col", "vol")
SPOT_ROWS = 16
PARTS = 2
VMEM_BYTES = 16 * 2 ** 20


def relax_factors(count):
    middle = (SPECTRUM_HIGH + SPECTRUM_LOW) / 2.0
    spread = (SPECTRUM_HIGH - SPECTRUM_LOW) / 2.0
    return [
        1.0 / (middle + spread * math.cos(math.pi * (2 * order + 1) / (2 * count)))
        for order in range(count)
    ]


def conduct_of(class_index, class_values):
    classes = jnp.arange(class_values.shape[0], dtype=jnp.int32)
    return jnp.sum(
        jnp.where(
            class_index[None] == classes[:, None, None, None],
            class_values[:, None, None, None],
            jnp.float32(0.0),
        ),
        axis=0,
    )


MATES = (0, 1, 2)


def mated(value, axis, mate):
    return lax.ppermute(value, axis, [(i, i ^ mate) for i in range(lax.axis_size(axis))])


def start_call(density, panel, shape):
    rows, cols, vols = shape[:3]
    excitations, nodes = density.shape
    targets = panel.shape[0]
    width = nodes // rows

    def body(density_ref, panel_ref, *rest):
        part_refs, rest = rest[:cols], rest[cols:]
        quarters = rest[:rows]
        nodes_ref, panel_buf, total_ref, sems = rest[rows:]
        r0, c0, v0 = (lax.axis_index(a) for a in ALL)
        low, high = r0 & 1, r0 >> 1
        sources = (low, low ^ 1, 2 + high, 2 + (high ^ 1))
        order = (1, 3, 0, 2)
        loads, stores = [], []
        for q in order:
            span = pl.ds(pl.multiple_of(sources[q] * width, width), width)
            pair = (
                pltpu.make_async_copy(panel_ref.at[:, span], panel_buf.at[q], sems.at[q]),
                pltpu.make_async_copy(density_ref.at[:, span], nodes_ref.at[q], sems.at[rows + q]),
            )
            for copy in pair:
                copy.start()
            loads.append(pair)
        total = jnp.zeros((targets, excitations), jnp.float32)
        for q, pair in zip(order, loads):
            for copy in pair:
                copy.wait()
            store = pltpu.make_async_copy(panel_buf.at[q], quarters[q], sems.at[2 * rows + q])
            store.start()
            stores.append(store)
            total += lax.dot_general(
                panel_buf[q], nodes_ref[q].astype(jnp.bfloat16), (((1,), (1,)), ((), ())),
                preferred_element_type=jnp.float32,
            )
        total_ref[...] = total.T
        for kc in range(cols):
            for kr in range(rows):
                for kv in range(vols):
                    owner = ((r0 ^ kr) * cols + (c0 ^ kc)) * vols + (v0 ^ kv)
                    part_refs[kc][kr, kv:kv + 1] = total_ref[pl.ds(owner, 1)]
        for copy in stores:
            copy.wait()

    hbm = pl.BlockSpec(memory_space=pltpu.HBM)
    return pl.pallas_call(
        body,
        out_shape=[jax.ShapeDtypeStruct((rows, vols, targets), jnp.float32)] * cols
        + [jax.ShapeDtypeStruct((targets, width), panel.dtype)] * rows,
        in_specs=[hbm, hbm],
        out_specs=[pl.BlockSpec(memory_space=pltpu.VMEM)] * cols + [hbm] * rows,
        scratch_shapes=[
            pltpu.VMEM((rows, excitations, width), jnp.float32),
            pltpu.VMEM((rows, targets, width), panel.dtype),
            pltpu.VMEM((excitations, targets), jnp.float32),
            pltpu.SemaphoreType.DMA((3 * rows,)),
        ],
        name="start",
    )(density, panel)


def prepare_call(shape, values, known, other):
    rows, cols, vols, bx, by, bz = shape
    blocks = cols * vols
    height = bx * blocks * by
    lines = bx * by
    targets = known[0].shape[-1]

    def body(values_ref, *refs):
        known_refs, other_refs = refs[:rows], refs[rows:2 * rows]
        inverse_ref, hit_ref, lane_ref = refs[2 * rows:]
        r0, c0, v0 = (lax.axis_index(a) for a in ALL)
        count = values_ref.shape[0]
        row_ids = lax.broadcasted_iota(jnp.int32, (height, targets), 0)
        lane_ids = lax.broadcasted_iota(jnp.int32, (bz, targets), 0)
        for k in range(rows):
            spot = known_refs[k][vols * lines:].astype(jnp.float32).astype(jnp.int32)
            line = spot[0:1] * (blocks * by) + spot[1:2]
            hit_ref[k ^ r0] = (row_ids == line).astype(jnp.bfloat16)
            lane_ref[k ^ r0] = (lane_ids == spot[2:3]).astype(jnp.bfloat16)
        for k in range(rows):
            for kc, refs_of in enumerate((known_refs, other_refs)):
                start = pl.multiple_of((kc ^ c0) * by, by)

                def plane(kv, carry, source=refs_of[k], start=start, k=k):
                    kind = source[pl.ds(pl.multiple_of(kv * lines, lines), lines)].astype(jnp.float32)
                    conduct = jnp.zeros((lines, bz), jnp.float32)
                    for i in range(count):
                        conduct = jnp.where(kind == float(i), values_ref[i], conduct)
                    inverse = 1.0 / (MASS_TERM + 6.0 * conduct)
                    place = (pl.ds((k ^ r0) * bx, bx), kv ^ v0, pl.ds(start, by))
                    inverse_ref[place] = inverse.reshape(bx, by, bz)
                    return carry

                lax.fori_loop(0, vols, plane, 0)

    vmem = pl.BlockSpec(memory_space=pltpu.VMEM)
    return pl.pallas_call(
        body,
        out_shape=[
            jax.ShapeDtypeStruct((rows * bx, vols, cols * by, bz), jnp.float32),
            jax.ShapeDtypeStruct((rows, height, targets), jnp.bfloat16),
            jax.ShapeDtypeStruct((rows, bz, targets), jnp.bfloat16),
        ],
        in_specs=[pl.BlockSpec(memory_space=pltpu.SMEM)] + [vmem] * (2 * rows),
        out_specs=[vmem] * 3,
        name="prepare",
    )(values, *known, *other)


def landed_call(volume):
    excitations = volume.shape[0]
    few = math.gcd(excitations, 8)
    block = pl.BlockSpec((few,) + volume.shape[1:], lambda i: (i, 0, 0, 0))

    def body(in_ref, out_ref):
        out_ref[...] = in_ref[...]

    return pl.pallas_call(
        body,
        grid=(excitations // few,),
        out_shape=jax.ShapeDtypeStruct(volume.shape, volume.dtype),
        in_specs=[block],
        out_specs=block,
        name="landed",
    )(volume)


def parts_of(value, count):
    pieces = []
    for _ in range(count):
        piece = value.astype(jnp.bfloat16)
        pieces.append(piece)
        value = value - piece.astype(jnp.float32)
    return pieces


def slab_call(shape, first, source, inverse, hit, lane, parts, start=None):
    rows, cols, vols, bx, by, bz = shape
    blocks = cols * vols
    targets = lane.shape[-1]
    height = bx * blocks * by
    depth = rows * bx
    planes = (depth, vols, cols * by, bz)
    padded = (depth + 2, vols, cols * by, bz)
    factors = relax_factors(SWEEPS)

    def body(source_ref, inverse_ref, hit_ref, lane_ref, *rest):
        if first:
            *part_refs, out_ref, flux_ref, other_ref, scaled_ref, ratio_ref = rest
            volume_ref = None
        else:
            parts_ref, start_ref, volume_ref, flux_ref, out_ref, other_ref, scaled_ref, ratio_ref = rest
        sub = lax.broadcasted_iota(jnp.int32, (by, bz), 0)
        lan = lax.broadcasted_iota(jnp.int32, (by, bz), 1)
        for ref in (out_ref, other_ref):
            ref[0] = jnp.zeros(planes[1:], jnp.float32)
            ref[depth + 1] = jnp.zeros(planes[1:], jnp.float32)
        here = other_ref if first else start_ref
        potentials = []
        for r in range(rows):
            if first:
                place = pl.ds(r ^ lax.axis_index("row"), 1)
                potential = sum(part[place, :] for part in part_refs)
            else:
                potential = sum(
                    jnp.sum(parts_ref[r ^ mate, :, k, :], axis=0, keepdims=True)
                    for k, mate in enumerate(MATES)
                )
            potentials.append(potential)
            weights = [
                lane_ref[r] * piece.astype(jnp.bfloat16) for piece in parts_of(potential, 3)
            ]
            added = lax.dot_general(
                hit_ref[r], jnp.concatenate(weights, axis=0), (((1,), (1,)), ((), ())),
                preferred_element_type=jnp.float32,
            )
            added = added[:, :bz] + added[:, bz:2 * bz] + added[:, 2 * bz:]
            added = added.reshape(bx, vols, cols, by, bz)
            for j in range(blocks):
                c, v = j // vols, j % vols
                span = (slice(r * bx, (r + 1) * bx), v, slice(c * by, (c + 1) * by))
                scaled = source_ref[r, j] + added[:, v, c]
                inverse = inverse_ref[span]
                scaled = scaled * inverse
                ratio_ref[span] = (1.0 - MASS_TERM * inverse) * (1.0 / 6.0)
                scaled_ref[span] = scaled
                if first:
                    here[1 + r * bx:1 + (r + 1) * bx, v, c * by:(c + 1) * by] = factors[0] * scaled

        sweeps = factors[1:] if first else factors
        for order, factor in enumerate(sweeps):
            last = order + 1 == len(sweeps)
            there = out_ref if (len(sweeps) - order) % 2 == 1 else other_ref

            def step(index, carry, here=here, there=there, last=last, factor=factor):
                for x in (index,):
                    tile = [here[x + 1, j % vols, (j // vols) * by:(j // vols + 1) * by]
                            for j in range(blocks)]
                    up = [pltpu.roll(t, 1, 1) for t in tile]
                    down = [pltpu.roll(t, bz - 1, 1) for t in tile]
                    for j in range(blocks):
                        c, v = j // vols, j % vols
                        own = slice(c * by, (c + 1) * by)
                        around = here[x, v, own] + here[x + 2, v, own]
                        if c > 0:
                            around += here[x + 1, v, c * by - 1:(c + 1) * by - 1]
                        else:
                            around += jnp.where(sub == 0, 0.0, pltpu.roll(tile[j], 1, 0))
                        if c < cols - 1:
                            around += here[x + 1, v, c * by + 1:(c + 1) * by + 1]
                        else:
                            around += jnp.where(sub == by - 1, 0.0, pltpu.roll(tile[j], by - 1, 0))
                        around += jnp.where(lan == 0, up[j - 1] if v > 0 else 0.0, up[j])
                        around += jnp.where(
                            lan == bz - 1, down[j + 1] if v < vols - 1 else 0.0, down[j]
                        )
                        value = (1.0 - factor) * tile[j] + factor * (
                            scaled_ref[x, v, own] + ratio_ref[x, v, own] * around
                        )
                        there[x + 1, v, own] = value
                        if last and not first:
                            volume_ref[x // bx, j, x % bx] = value
                return carry

            for index in range(depth):
                step(index, 0)
            here = there

        for r in range(rows):
            part = here[1 + r * bx:1 + (r + 1) * bx].reshape(height, bz)
            met = sum(
                jnp.dot(piece, lane_ref[r], preferred_element_type=jnp.float32)
                for piece in parts_of(part, 2)
            )
            value = jnp.sum(met * hit_ref[r].astype(jnp.float32), axis=0, keepdims=True)
            value = value - potentials[r]
            for k, mate in enumerate(MATES):
                flux_ref[r ^ mate, :, k, :] = jnp.broadcast_to(value, (blocks, targets))

    vmem = pl.BlockSpec(memory_space=pltpu.VMEM)
    operands = [source, inverse, hit, lane] + (list(parts) if first else [parts, start])
    fluxes = jax.ShapeDtypeStruct((rows, blocks, len(MATES), targets), jnp.float32)
    field = padded if first else (rows, blocks, bx, by, bz)
    field = jax.ShapeDtypeStruct(field, jnp.float32)
    scratch = [pltpu.VMEM(padded, jnp.float32)] * (1 if first else 2)
    return pl.pallas_call(
        body,
        out_shape=[field, fluxes],
        in_specs=[vmem] * len(operands),
        out_specs=[vmem, vmem],
        scratch_shapes=scratch + [pltpu.VMEM(planes, jnp.float32)] * 2,
        name="slab_first" if first else "slab_last",
    )(*operands)


def update_call(flux, panels, part, parts):
    excitations, width = flux.shape[0], panels[0].shape[1] // parts
    span = slice(part * width, (part + 1) * width)

    def body(flux_ref, a_own, a_mate, b_own, b_mate, a_ref, b_ref):
        fluxes = [flux_ref[:, k, :].astype(jnp.bfloat16) for k in range(len(MATES))]
        for out, own, mate, k in ((a_ref, a_own, a_mate, 1), (b_ref, b_own, b_mate, 2)):
            value = jnp.dot(fluxes[0], own[:, span], preferred_element_type=jnp.float32)
            value += jnp.dot(fluxes[k], mate[:, span], preferred_element_type=jnp.float32)
            out[...] = value.astype(jnp.bfloat16)

    vmem = pl.BlockSpec(memory_space=pltpu.VMEM)
    return pl.pallas_call(
        body,
        out_shape=[jax.ShapeDtypeStruct((excitations, width), jnp.bfloat16)] * 2,
        in_specs=[vmem] * 5,
        out_specs=[vmem] * 2,
        compiler_params=pltpu.CompilerParams(vmem_limit_bytes=VMEM_BYTES),
        name="update",
    )(flux, *panels)


def potential_call(densities, halves, mates, panels, part, before):
    excitations = densities[0].shape[0]
    targets, width = panels[0].shape[0], panels[0].shape[1] // PARTS
    span = slice(part * width, (part + 1) * width)

    def body(a_density, b_density, a_half, b_half, a_other, b_other,
             a_own, a_mate, b_own, b_mate, *rest):
        out_ref = rest[-1]
        rounded = [
            (density[:, span] + RELAXATION * (half[...].astype(jnp.float32)
                                              + other[...].astype(jnp.float32))).astype(jnp.bfloat16)
            for density, half, other in (
                (a_density, a_half, a_other), (b_density, b_half, b_other))
        ]

        def met(value, panel):
            return lax.dot_general(
                value, panel[:, span], (((1,), (1,)), ((), ())), preferred_element_type=jnp.float32
            )

        sums = (
            met(rounded[0], a_own) + met(rounded[1], b_own),
            met(rounded[0], a_mate),
            met(rounded[1], b_mate),
        )
        for k, value in enumerate(sums):
            out_ref[:, k, :] = value + rest[0][:, k, :] if before is not None else value

    vmem = pl.BlockSpec(memory_space=pltpu.VMEM)
    operands = [*densities, *halves, *mates, *panels] + ([] if before is None else [before])
    return pl.pallas_call(
        body,
        out_shape=jax.ShapeDtypeStruct((excitations, len(MATES), targets), jnp.float32),
        in_specs=[vmem] * len(operands),
        out_specs=vmem,
        compiler_params=pltpu.CompilerParams(vmem_limit_bytes=VMEM_BYTES),
        name="potential",
    )(*operands)


def trace_spots(trace_count, trace_cell, targets, shape):
    _, cols, vols, _, by, bz = shape
    counts = trace_count[0]
    offsets = jnp.cumsum(counts) - counts
    slot_ids = jnp.arange(trace_cell.shape[2], dtype=jnp.int32)
    live = slot_ids[None, :] < counts[:, None]
    owner = jnp.where(live, offsets[:, None] + slot_ids[None, :], -1)
    cell = trace_cell[0]
    block_ids = jnp.arange(cols * vols, dtype=jnp.int32)[:, None]
    line = (block_ids % vols) * (cols * by) + (block_ids // vols) * by + (cell // bz) % by
    code = ((cell // (by * bz)) * (cols * vols * by) + line) * bz + cell % bz
    match = owner[:, :, None] == jnp.arange(targets, dtype=jnp.int32)
    code = jnp.sum(jnp.where(match, code[:, :, None], 0), axis=(0, 1))
    line = code // bz
    span = cols * vols * by
    return jnp.stack([line // span, line % span, code % bz])


def split_by_excitation(panel, density, source, class_index, class_values, trace_count, trace_cell):
    rows, cols, vols = (lax.axis_size(a) for a in ALL)
    blocks = cols * vols
    excitations, bx, by, bz = source.shape
    targets, nodes = panel.shape
    width = nodes // rows
    here = lax.axis_index("row")
    low, high = here & 1, here >> 1
    shape = (rows, cols, vols, bx, by, bz)

    def columns(array, place):
        return lax.dynamic_slice_in_dim(array, place * width, width, 1)

    def around_axis(pieces, axis):
        return [pieces[0]] + [mated(piece, axis, k) for k, piece in enumerate(pieces) if k > 0]

    made = start_call(density, panel, shape)
    parts, quarters = made[:cols], made[cols:]

    kinds = class_index.reshape(bx * by, bz).astype(jnp.bfloat16)
    kinds = around_axis([kinds] * vols, "vol")
    parts = parts[0] + mated(parts[1], "col", 1)
    slab = lax.all_to_all(source, ALL, 0, 0, tiled=True)
    slab = slab.reshape(rows, blocks, bx, by, bz)
    parts = jnp.stack(around_axis([parts[k] for k in range(rows)], "row"))
    spots = trace_spots(trace_count, trace_cell, targets, shape).astype(jnp.bfloat16)
    spots = jnp.pad(spots, ((0, SPOT_ROWS - spots.shape[0]), (0, 0)))
    known = jnp.concatenate(kinds + [spots])
    known = around_axis([known] * rows, "row")
    parts = around_axis([parts[:, k] for k in range(vols)], "vol")
    other = [mated(piece, "col", 1) for piece in known]

    panels = [quarters[0], None, quarters[2], None]
    panels[1] = mated(quarters[1], "row", 1)
    panels[3] = mated(quarters[3], "row", 2)
    densities = [columns(density, low), columns(density, 2 + high)]

    inverse, hit, lane = prepare_call(shape, class_values, known, other)
    volume, flux = slab_call(shape, True, slab, inverse, hit, lane, parts)
    flux = flux.reshape(excitations, len(MATES), targets)
    flux = lax.all_to_all(flux, ALL, 0, 0, tiled=True)
    halves, mates, parts = [], [], None
    for part in range(PARTS):
        halves.append(update_call(flux, panels, part, PARTS))
        mates.append([mated(halves[part][0], "row", 2), mated(halves[part][1], "row", 1)])
    for part in range(PARTS):
        parts = potential_call(densities, halves[part], mates[part], panels, part, parts)
    parts = lax.all_to_all(parts, ALL, 0, 0, tiled=True)
    parts = parts.reshape(rows, blocks, len(MATES), targets)
    volume, flux = slab_call(shape, False, slab, inverse, hit, lane, parts, volume)
    flux = flux.reshape(excitations, len(MATES), targets)
    flux = lax.all_to_all(flux, ALL, 0, 0, tiled=True)
    volume = volume.reshape(excitations, bx, by, bz)
    volume = lax.all_to_all(volume, ALL, 0, 0, tiled=True)
    volume = landed_call(volume)
    ends = update_call(flux, panels, 0, 1)
    end_mates = [mated(ends[0], "row", 2), mated(ends[1], "row", 1)]
    totals = []
    for group in range(2):
        firsts = [
            jnp.concatenate([pair[group] for pair in pairs], axis=1) for pairs in (halves, mates)
        ]
        a, b, c, d = (
            value.astype(jnp.float32) for value in (*firsts, ends[group], end_mates[group])
        )
        totals.append((RELAXATION * ((a + b) + (c + d))).astype(jnp.bfloat16))
    moved = [mated(totals[0], "row", 1), mated(totals[1], "row", 2)]
    change = [
        jnp.where(low == 0, totals[0], moved[0]), jnp.where(low == 0, moved[0], totals[0]),
        jnp.where(high == 0, totals[1], moved[1]), jnp.where(high == 0, moved[1], totals[1]),
    ]
    density = density + jnp.concatenate(change, axis=1).astype(jnp.float32)
    return (density, volume)


def padded_2(value, sides, width):
    for axis, dim in sides:
        size, length = (lax.axis_size(axis), value.shape[dim])
        up = [(i, (i + 1) % size) for i in range(size - 1)]
        down = [(j, i) for i, j in up]
        last = lax.slice_in_dim(value, length - width, length, axis=dim)
        first = lax.slice_in_dim(value, 0, width, axis=dim)
        before = lax.ppermute(last, axis, up)
        after = lax.ppermute(first, axis, down)
        value = jnp.concatenate([before, value, after], axis=dim)
    return value


def neighbours(padded):
    center = padded[..., 1:-1, 1:-1, 1:-1]
    beside_all = padded[..., 2:, 1:-1, 1:-1] + padded[..., :-2, 1:-1, 1:-1]
    beside_all = beside_all + padded[..., 1:-1, 2:, 1:-1] + padded[..., 1:-1, :-2, 1:-1]
    beside_all = beside_all + padded[..., 1:-1, 1:-1, 2:] + padded[..., 1:-1, 1:-1, :-2]
    return (center, beside_all)


def split_by_block(panel, density, source, class_index, class_values, trace_count, trace_cell):
    factors = relax_factors(SWEEPS)
    conduct = conduct_of(class_index, class_values)
    diagonal = MASS_TERM + 6.0 * conduct
    counts = trace_count[0]
    block_index = lax.axis_index(("col", "vol"))
    offsets = jnp.cumsum(counts) - counts
    target_rows = panel.shape[0]
    slot_count = trace_cell.shape[2]
    slot_ids = jnp.arange(slot_count, dtype=jnp.int32)
    target_ids = jnp.arange(target_rows, dtype=jnp.int32)
    own_count = lax.dynamic_index_in_dim(counts, block_index, keepdims=False)
    first_target = lax.dynamic_index_in_dim(offsets, block_index, keepdims=False)
    cell_ids = lax.dynamic_index_in_dim(trace_cell[0], block_index, keepdims=False)
    live_slots = slot_ids < own_count
    select = (
        ((first_target + slot_ids)[:, None] == target_ids[None, :]) & live_slots[:, None]
    ).astype(jnp.float32)
    volume = jnp.zeros(source.shape, jnp.float32)
    field_shape = volume.shape
    share_width = density.shape[1] // lax.axis_size("row")
    share_state = lax.dynamic_slice_in_dim(
        density, lax.axis_index("row") * share_width, share_width, 1
    )
    rounded = density.astype(jnp.bfloat16)
    lead = field_shape[0]
    for iteration in range(OUTER):
        partial_value = lax.dot_general(
            rounded, panel, (((1,), (1,)), ((), ())), preferred_element_type=jnp.float32
        )
        potential = lax.psum(partial_value, ("col", "vol"))
        slot_values = jnp.dot(potential, select.T, precision=lax.Precision.HIGHEST)
        right_side = source.reshape(lead, -1).at[:, cell_ids].add(slot_values).reshape(field_shape)
        relax_volume = volume
        for factor in factors:
            padded = padded_2(relax_volume, (("row", 1), ("col", 2), ("vol", 3)), 1)
            center, beside_all = neighbours(padded)
            relax_volume = (
                center + factor * (right_side - diagonal * center + conduct * beside_all) / diagonal
            )
        volume = relax_volume
        mismatch = volume.reshape(lead, -1)[:, cell_ids] - slot_values
        own_fluxes = jnp.dot(mismatch, select, precision=lax.Precision.HIGHEST)
        fluxes = lax.psum(own_fluxes, ("col", "vol"))
        update = jnp.dot(fluxes.astype(jnp.bfloat16), panel, preferred_element_type=jnp.float32)
        share_state = share_state + RELAXATION * lax.psum_scatter(
            update, "row", scatter_dimension=1, tiled=True
        )
        if iteration + 1 < OUTER:
            rounded = lax.all_gather(share_state.astype(jnp.bfloat16), "row", axis=1, tiled=True)
    density = lax.all_gather(share_state, "row", axis=1, tiled=True)
    return (density, volume)


def local(*args):
    sizes = [lax.axis_size(a) for a in ALL]
    if whole_slabs(sizes, args[0].shape[0], args[2].shape):
        return split_by_excitation(*args)
    return split_by_block(*args)


def whole_slabs(sizes, targets, block):
    fits = math.prod(sizes) == block[0] and sizes[0] == 4 and targets == block[3]
    return fits and all(size & (size - 1) == 0 for size in sizes)


def solution(mesh):
    placed = (
        P("row", ("col", "vol")),
        P(None, ("col", "vol")),
        P(None, "row", "col", "vol"),
        P("row", "col", "vol"),
        P(),
        P("row", None),
        P("row", None, None),
    )
    return jax.shard_map(
        local,
        mesh=mesh,
        in_specs=placed,
        out_specs=(P(None, ("col", "vol")), P(None, "row", "col", "vol")),
        check_vma=False,
    )
```

```python
import math

import jax
import jax.numpy as jnp
from jax import lax
from jax.experimental import pallas as pl
from jax.experimental.pallas import tpu as pltpu
from jax.sharding import PartitionSpec as P


SWEEPS = 4
OUTER = 2


MASS_TERM = 0.1
RELAXATION = 0.5
SPECTRUM_LOW = 0.1
SPECTRUM_HIGH = 2.0

ALL = ("row", "col", "vol")
SPOT_ROWS = 32
PARTS = 2
VMEM_BYTES = 16 * 2 ** 20


def relax_factors(count):
    middle = (SPECTRUM_HIGH + SPECTRUM_LOW) / 2.0
    spread = (SPECTRUM_HIGH - SPECTRUM_LOW) / 2.0
    return [
        1.0 / (middle + spread * math.cos(math.pi * (2 * order + 1) / (2 * count)))
        for order in range(count)
    ]


def conduct_of(class_index, class_values):
    classes = jnp.arange(class_values.shape[0], dtype=jnp.int32)
    return jnp.sum(
        jnp.where(
            class_index[None] == classes[:, None, None, None],
            class_values[:, None, None, None],
            jnp.float32(0.0),
        ),
        axis=0,
    )


MATES = (0, 1, 2)


def mated(value, axis, mate):
    return lax.ppermute(value, axis, [(i, i ^ mate) for i in range(lax.axis_size(axis))])


def start_call(density, panel, known, shape):
    rows, cols, vols = shape[:3]
    excitations, nodes = density.shape
    targets = panel.shape[0]
    width = nodes // rows
    lines = known.shape[0]
    owners = cols * vols

    def body(density_ref, panel_ref, known_ref, *rest):
        sent, rest = rest[:rows], rest[rows:]
        quarters = rest[:rows]
        nodes_ref, panel_buf, total_ref, picked_ref, sems = rest[rows:]
        r0, c0, v0 = (lax.axis_index(a) for a in ALL)
        low, high = r0 & 1, r0 >> 1
        sources = (low, low ^ 1, 2 + high, 2 + (high ^ 1))
        order = (1, 3, 0, 2)
        loads, stores = [], []
        for q in order:
            span = pl.ds(pl.multiple_of(sources[q] * width, width), width)
            pair = (
                pltpu.make_async_copy(panel_ref.at[:, span], panel_buf.at[q], sems.at[q]),
                pltpu.make_async_copy(density_ref.at[:, span], nodes_ref.at[q], sems.at[rows + q]),
            )
            for copy in pair:
                copy.start()
            loads.append(pair)
        for k in range(rows):
            sent[k][0:lines] = known_ref[...]
        total = jnp.zeros((targets, excitations), jnp.float32)
        for q, pair in zip(order, loads):
            for copy in pair:
                copy.wait()
            store = pltpu.make_async_copy(panel_buf.at[q], quarters[q], sems.at[2 * rows + q])
            store.start()
            stores.append(store)
            total += lax.dot_general(
                panel_buf[q], nodes_ref[q].astype(jnp.bfloat16), (((1,), (1,)), ((), ())),
                preferred_element_type=jnp.float32,
            )
        total_ref[...] = total.T
        for kr in range(rows):
            for kc in range(cols):
                for kv in range(vols):
                    owner = ((r0 ^ kr) * cols + (c0 ^ kc)) * vols + (v0 ^ kv)
                    place = kc * vols + kv
                    picked_ref[kr, place:place + 1] = total_ref[pl.ds(owner, 1)]
            pieces = [piece.astype(jnp.float32) for piece in parts_of(picked_ref[kr], 3)]
            pieces.append(jnp.zeros((owners, targets), jnp.float32))
            sent[kr][lines:] = jnp.concatenate(pieces).astype(jnp.bfloat16)
        for copy in stores:
            copy.wait()

    hbm = pl.BlockSpec(memory_space=pltpu.HBM)
    vmem = pl.BlockSpec(memory_space=pltpu.VMEM)
    return pl.pallas_call(
        body,
        out_shape=[jax.ShapeDtypeStruct((lines + 4 * owners, targets), known.dtype)] * rows
        + [jax.ShapeDtypeStruct((targets, width), panel.dtype)] * rows,
        in_specs=[hbm, hbm, vmem],
        out_specs=[vmem] * rows + [hbm] * rows,
        scratch_shapes=[
            pltpu.VMEM((rows, excitations, width), jnp.float32),
            pltpu.VMEM((rows, targets, width), panel.dtype),
            pltpu.VMEM((excitations, targets), jnp.float32),
            pltpu.VMEM((rows, owners, targets), jnp.float32),
            pltpu.SemaphoreType.DMA((3 * rows,)),
        ],
        name="start",
    )(density, panel, known)


def collect_call(shape, lines, known, other):
    rows, cols, vols = shape[:3]
    targets = known[0].shape[1]
    owners = cols * vols
    height = 4 * owners

    def body(*refs):
        ins, outs = refs[:2 * rows], refs[2 * rows:]
        for k in range(rows):
            own, mate = (ins[k + side * rows][...].astype(jnp.float32) for side in range(2))
            total = jnp.zeros((vols, targets), jnp.float32)
            for p in (2, 1, 0):
                total += own[p * owners:p * owners + vols] + mate[p * owners + vols:(p + 1) * owners]
            for v in range(vols):
                outs[v][k:k + 1] = total[v:v + 1]

    block = pl.BlockSpec((height, targets), lambda i: (lines // height, 0))
    whole = pl.BlockSpec((rows, targets), lambda i: (0, 0))
    return pl.pallas_call(
        body,
        grid=(1,),
        out_shape=[jax.ShapeDtypeStruct((rows, targets), jnp.float32)] * vols,
        in_specs=[block] * (2 * rows),
        out_specs=[whole] * vols,
        name="collect",
    )(*known, *other)


def prepare_call(shape, values, known, other):
    rows, cols, vols, bx, by, bz = shape
    blocks = cols * vols
    height = bx * blocks * by
    lines = bx * by
    targets = known[0].shape[-1]

    def body(values_ref, *refs):
        known_refs, other_refs = refs[:rows], refs[rows:2 * rows]
        inverse_ref, hit_ref, lane_ref = refs[2 * rows:]
        r0, c0, v0 = (lax.axis_index(a) for a in ALL)
        count = values_ref.shape[0]
        row_ids = lax.broadcasted_iota(jnp.int32, (height, targets), 0)
        lane_ids = lax.broadcasted_iota(jnp.int32, (bz, targets), 0)
        for k in range(rows):
            spot = known_refs[k][vols * lines:vols * lines + SPOT_ROWS].astype(jnp.float32)
            spot = spot.astype(jnp.int32)
            line = spot[0:1] * (blocks * by) + spot[1:2]
            hit_ref[k ^ r0] = (row_ids == line).astype(jnp.bfloat16)
            lane_ref[k ^ r0] = (lane_ids == spot[2:3]).astype(jnp.bfloat16)
        for k in range(rows):
            for kc, refs_of in enumerate((known_refs, other_refs)):
                start = pl.multiple_of((kc ^ c0) * by, by)

                def plane(kv, carry, source=refs_of[k], start=start, k=k):
                    kind = source[pl.ds(pl.multiple_of(kv * lines, lines), lines)].astype(jnp.float32)
                    kind = kind.astype(jnp.int32)
                    choices, bit = [values_ref[i] for i in range(count)], 1
                    while len(choices) > 1:
                        odd = (kind & bit) != 0
                        merged = [jnp.where(odd, two, one)
                                  for one, two in zip(choices[0::2], choices[1::2])]
                        choices, bit = merged + choices[len(merged) * 2:], bit * 2
                    inverse = jnp.broadcast_to(choices[0], (lines, bz))
                    place = (pl.ds((k ^ r0) * bx, bx), kv ^ v0, pl.ds(start, by))
                    inverse_ref[place] = inverse.reshape(bx, by, bz)
                    return carry

                lax.fori_loop(0, vols, plane, 0)

    vmem = pl.BlockSpec(memory_space=pltpu.VMEM)
    return pl.pallas_call(
        body,
        out_shape=[
            jax.ShapeDtypeStruct((rows * bx, vols, cols * by, bz), jnp.float32),
            jax.ShapeDtypeStruct((rows, height, targets), jnp.bfloat16),
            jax.ShapeDtypeStruct((rows, bz, targets), jnp.bfloat16),
        ],
        in_specs=[pl.BlockSpec(memory_space=pltpu.SMEM)] + [vmem] * (2 * rows),
        out_specs=[vmem] * 3,
        name="prepare",
    )(values, *known, *other)


def landed_call(volume):
    pieces = 4
    few = volume.shape[0] // pieces

    def body(in_ref, out_ref, held_ref, sems):
        loads, stores = [], []
        for i in range(pieces):
            span = pl.ds(i * few, few)
            loads.append(pltpu.make_async_copy(in_ref.at[span], held_ref.at[span], sems.at[i]))
            stores.append(pltpu.make_async_copy(held_ref.at[span], out_ref.at[span], sems.at[pieces + i]))
            loads[i].start()
        for load, store in zip(loads, stores):
            load.wait()
            store.start()
        for store in stores:
            store.wait()

    hbm = pl.BlockSpec(memory_space=pltpu.HBM)
    return pl.pallas_call(
        body,
        out_shape=jax.ShapeDtypeStruct(volume.shape, volume.dtype),
        in_specs=[hbm],
        out_specs=hbm,
        scratch_shapes=[
            pltpu.VMEM(volume.shape, volume.dtype), pltpu.SemaphoreType.DMA((2 * pieces,))
        ],
        name="landed",
    )(volume)


def parts_of(value, count):
    pieces = []
    for _ in range(count):
        piece = value.astype(jnp.bfloat16)
        pieces.append(piece)
        value = value - piece.astype(jnp.float32)
    return pieces


def slab_call(shape, first, source, inverse, hit, lane, parts, start=None):
    rows, cols, vols, bx, by, bz = shape
    blocks = cols * vols
    targets = lane.shape[-1]
    height = bx * blocks * by
    depth = rows * bx
    planes = (depth, vols, cols * by, bz)
    padded = (depth + 2, vols, cols * by, bz)
    factors = relax_factors(SWEEPS)

    def body(source_ref, inverse_ref, hit_ref, lane_ref, *rest):
        if first:
            *part_refs, out_ref, flux_ref, other_ref, scaled_ref, ratio_ref = rest
            volume_ref = None
        else:
            parts_ref, start_ref, volume_ref, flux_ref, out_ref, other_ref, scaled_ref, ratio_ref = rest
        sub = lax.broadcasted_iota(jnp.int32, (by, bz), 0)
        lan = lax.broadcasted_iota(jnp.int32, (by, bz), 1)
        for ref in (out_ref, other_ref):
            ref[0] = jnp.zeros(planes[1:], jnp.float32)
            ref[depth + 1] = jnp.zeros(planes[1:], jnp.float32)
        here = other_ref if first else start_ref
        potentials = []
        for r in range(rows):
            if first:
                place = pl.ds(r ^ lax.axis_index("row"), 1)
                potential = sum(part[place, :] for part in part_refs)
            else:
                potential = sum(
                    jnp.sum(parts_ref[r ^ mate, :, k, :], axis=0, keepdims=True)
                    for k, mate in enumerate(MATES)
                )
            potentials.append(potential)
            weights = [
                lane_ref[r] * piece.astype(jnp.bfloat16) for piece in parts_of(potential, 3)
            ]
            added = lax.dot_general(
                hit_ref[r], jnp.concatenate(weights, axis=0), (((1,), (1,)), ((), ())),
                preferred_element_type=jnp.float32,
            )
            added = added[:, :bz] + added[:, bz:2 * bz] + added[:, 2 * bz:]
            added = added.reshape(bx, vols, cols, by, bz)
            for j in range(blocks):
                c, v = j // vols, j % vols
                span = (slice(r * bx, (r + 1) * bx), v, slice(c * by, (c + 1) * by))
                scaled = source_ref[r, j] + added[:, v, c]
                inverse = inverse_ref[span]
                scaled = scaled * inverse
                ratio_ref[span] = (1.0 - MASS_TERM * inverse) * (1.0 / 6.0)
                scaled_ref[span] = scaled
                if first:
                    here[1 + r * bx:1 + (r + 1) * bx, v, c * by:(c + 1) * by] = factors[0] * scaled

        sweeps = factors[1:] if first else factors
        for order, factor in enumerate(sweeps):
            last = order + 1 == len(sweeps)
            there = out_ref if (len(sweeps) - order) % 2 == 1 else other_ref

            def step(index, carry, here=here, there=there, last=last, factor=factor):
                for x in (index,):
                    tile = [here[x + 1, j % vols, (j // vols) * by:(j // vols + 1) * by]
                            for j in range(blocks)]
                    up = [pltpu.roll(t, 1, 1) for t in tile]
                    down = [pltpu.roll(t, bz - 1, 1) for t in tile]
                    for j in range(blocks):
                        c, v = j // vols, j % vols
                        own = slice(c * by, (c + 1) * by)
                        around = here[x, v, own] + here[x + 2, v, own]
                        if c > 0:
                            around += here[x + 1, v, c * by - 1:(c + 1) * by - 1]
                        else:
                            around += jnp.where(sub == 0, 0.0, pltpu.roll(tile[j], 1, 0))
                        if c < cols - 1:
                            around += here[x + 1, v, c * by + 1:(c + 1) * by + 1]
                        else:
                            around += jnp.where(sub == by - 1, 0.0, pltpu.roll(tile[j], by - 1, 0))
                        around += jnp.where(lan == 0, up[j - 1] if v > 0 else 0.0, up[j])
                        around += jnp.where(
                            lan == bz - 1, down[j + 1] if v < vols - 1 else 0.0, down[j]
                        )
                        value = (1.0 - factor) * tile[j] + factor * (
                            scaled_ref[x, v, own] + ratio_ref[x, v, own] * around
                        )
                        there[x + 1, v, own] = value
                        if last and not first:
                            volume_ref[x // bx, j, x % bx] = value
                return carry

            for index in range(depth):
                step(index, 0)
            here = there

        for r in range(rows):
            part = here[1 + r * bx:1 + (r + 1) * bx].reshape(height, bz)
            met = sum(
                jnp.dot(piece, lane_ref[r], preferred_element_type=jnp.float32)
                for piece in parts_of(part, 2)
            )
            value = jnp.sum(met * hit_ref[r].astype(jnp.float32), axis=0, keepdims=True)
            value = value - potentials[r]
            for k, mate in enumerate(MATES):
                flux_ref[r ^ mate, :, k, :] = jnp.broadcast_to(value, (blocks, targets))

    vmem = pl.BlockSpec(memory_space=pltpu.VMEM)
    operands = [source, inverse, hit, lane] + (list(parts) if first else [parts, start])
    fluxes = jax.ShapeDtypeStruct((rows, blocks, len(MATES), targets), jnp.float32)
    field = padded if first else (rows, blocks, bx, by, bz)
    field = jax.ShapeDtypeStruct(field, jnp.float32)
    scratch = [pltpu.VMEM(padded, jnp.float32)] * (1 if first else 2)
    return pl.pallas_call(
        body,
        out_shape=[field, fluxes],
        in_specs=[vmem] * len(operands),
        out_specs=[vmem, vmem],
        scratch_shapes=scratch + [pltpu.VMEM(planes, jnp.float32)] * 2,
        name="slab_first" if first else "slab_last",
    )(*operands)


def update_call(flux, panels, part, parts):
    excitations, width = flux.shape[0], panels[0].shape[1] // parts
    span = slice(part * width, (part + 1) * width)

    def body(flux_ref, a_own, a_mate, b_own, b_mate, a_ref, b_ref):
        fluxes = [flux_ref[:, k, :].astype(jnp.bfloat16) for k in range(len(MATES))]
        for out, own, mate, k in ((a_ref, a_own, a_mate, 1), (b_ref, b_own, b_mate, 2)):
            value = jnp.dot(fluxes[0], own[:, span], preferred_element_type=jnp.float32)
            value += jnp.dot(fluxes[k], mate[:, span], preferred_element_type=jnp.float32)
            out[...] = value.astype(jnp.bfloat16)

    vmem = pl.BlockSpec(memory_space=pltpu.VMEM)
    return pl.pallas_call(
        body,
        out_shape=[jax.ShapeDtypeStruct((excitations, width), jnp.bfloat16)] * 2,
        in_specs=[vmem] * 5,
        out_specs=[vmem] * 2,
        compiler_params=pltpu.CompilerParams(vmem_limit_bytes=VMEM_BYTES),
        name="update",
    )(flux, *panels)


def potential_call(densities, halves, mates, panels, part, before):
    excitations = densities[0].shape[0]
    targets, width = panels[0].shape[0], panels[0].shape[1] // PARTS
    span = slice(part * width, (part + 1) * width)

    def body(a_density, b_density, a_half, b_half, a_other, b_other,
             a_own, a_mate, b_own, b_mate, *rest):
        out_ref = rest[-1]
        rounded = [
            (density[:, span] + RELAXATION * (half[...].astype(jnp.float32)
                                              + other[...].astype(jnp.float32))).astype(jnp.bfloat16)
            for density, half, other in (
                (a_density, a_half, a_other), (b_density, b_half, b_other))
        ]

        def met(value, panel):
            return lax.dot_general(
                panel[:, span], value, (((1,), (1,)), ((), ())), preferred_element_type=jnp.float32
            )

        sums = (
            met(rounded[0], a_own) + met(rounded[1], b_own),
            met(rounded[0], a_mate),
            met(rounded[1], b_mate),
        )
        for k, value in enumerate(sums):
            value = value.T
            out_ref[:, k, :] = value + rest[0][:, k, :] if before is not None else value

    vmem = pl.BlockSpec(memory_space=pltpu.VMEM)
    operands = [*densities, *halves, *mates, *panels] + ([] if before is None else [before])
    return pl.pallas_call(
        body,
        out_shape=jax.ShapeDtypeStruct((excitations, len(MATES), targets), jnp.float32),
        in_specs=[vmem] * len(operands),
        out_specs=vmem,
        compiler_params=pltpu.CompilerParams(vmem_limit_bytes=VMEM_BYTES),
        name="potential",
    )(*operands)


def trace_spots(trace_count, trace_cell, targets, shape):
    _, cols, vols, _, by, bz = shape
    counts = trace_count[0]
    offsets = jnp.cumsum(counts) - counts
    slot_ids = jnp.arange(trace_cell.shape[2], dtype=jnp.int32)
    live = slot_ids[None, :] < counts[:, None]
    owner = jnp.where(live, offsets[:, None] + slot_ids[None, :], -1)
    cell = trace_cell[0]
    block_ids = jnp.arange(cols * vols, dtype=jnp.int32)[:, None]
    line = (block_ids % vols) * (cols * by) + (block_ids // vols) * by + (cell // bz) % by
    code = ((cell // (by * bz)) * (cols * vols * by) + line) * bz + cell % bz
    match = owner[:, :, None] == jnp.arange(targets, dtype=jnp.int32)
    code = jnp.sum(jnp.where(match, code[:, :, None], 0), axis=(0, 1))
    line = code // bz
    span = cols * vols * by
    return jnp.stack([line // span, line % span, code % bz])


def split_by_excitation(panel, density, source, class_index, class_values, trace_count, trace_cell):
    rows, cols, vols = (lax.axis_size(a) for a in ALL)
    blocks = cols * vols
    excitations, bx, by, bz = source.shape
    targets, nodes = panel.shape
    width = nodes // rows
    here = lax.axis_index("row")
    low, high = here & 1, here >> 1
    shape = (rows, cols, vols, bx, by, bz)

    def columns(array, place):
        return lax.dynamic_slice_in_dim(array, place * width, width, 1)

    def around_axis(pieces, axis):
        return [pieces[0]] + [mated(piece, axis, k) for k, piece in enumerate(pieces) if k > 0]

    kinds = class_index.reshape(bx * by, bz).astype(jnp.bfloat16)
    kinds = around_axis([kinds] * vols, "vol")
    slab = lax.all_to_all(source, ALL, 0, 0, tiled=True)
    slab = slab.reshape(rows, blocks, bx, by, bz)
    spots = trace_spots(trace_count, trace_cell, targets, shape).astype(jnp.bfloat16)
    spots = jnp.pad(spots, ((0, SPOT_ROWS - spots.shape[0]), (0, 0)))
    known = jnp.concatenate(kinds + [spots])
    made = start_call(density, panel, known, shape)
    lines, quarters = known.shape[0], made[rows:]
    known = around_axis(made[:rows], "row")
    other = [mated(piece, "col", 1) for piece in known]
    parts = collect_call(shape, lines, known, other)
    parts = around_axis(parts, "vol")

    panels = [quarters[0], None, quarters[2], None]
    panels[1] = mated(quarters[1], "row", 1)
    panels[3] = mated(quarters[3], "row", 2)
    densities = [columns(density, low), columns(density, 2 + high)]

    inverses = 1.0 / (MASS_TERM + 6.0 * class_values)
    inverse, hit, lane = prepare_call(shape, inverses, known, other)
    volume, flux = slab_call(shape, True, slab, inverse, hit, lane, parts)
    flux = flux.reshape(excitations, len(MATES), targets)
    flux = lax.all_to_all(flux, ALL, 0, 0, tiled=True)
    halves, mates, parts = [], [], None
    for part in range(PARTS):
        halves.append(update_call(flux, panels, part, PARTS))
        mates.append([mated(halves[part][0], "row", 2), mated(halves[part][1], "row", 1)])
    for part in range(PARTS):
        parts = potential_call(densities, halves[part], mates[part], panels, part, parts)
    parts = lax.all_to_all(parts, ALL, 0, 0, tiled=True)
    parts = parts.reshape(rows, blocks, len(MATES), targets)
    volume, flux = slab_call(shape, False, slab, inverse, hit, lane, parts, volume)
    flux = flux.reshape(excitations, len(MATES), targets)
    flux = lax.all_to_all(flux, ALL, 0, 0, tiled=True)
    volume = volume.reshape(excitations, bx, by, bz)
    volume = lax.all_to_all(volume, ALL, 0, 0, tiled=True)
    volume = landed_call(volume)
    ends = update_call(flux, panels, 0, 1)
    end_mates = [mated(ends[0], "row", 2), mated(ends[1], "row", 1)]
    totals = []
    for group in range(2):
        firsts = [
            jnp.concatenate([pair[group] for pair in pairs], axis=1) for pairs in (halves, mates)
        ]
        a, b, c, d = (
            value.astype(jnp.float32) for value in (*firsts, ends[group], end_mates[group])
        )
        totals.append((RELAXATION * ((a + b) + (c + d))).astype(jnp.bfloat16))
    moved = [mated(totals[0], "row", 1), mated(totals[1], "row", 2)]
    change = [
        jnp.where(low == 0, totals[0], moved[0]), jnp.where(low == 0, moved[0], totals[0]),
        jnp.where(high == 0, totals[1], moved[1]), jnp.where(high == 0, moved[1], totals[1]),
    ]
    density = density + jnp.concatenate(change, axis=1).astype(jnp.float32)
    return (density, volume)


def padded_2(value, sides, width):
    for axis, dim in sides:
        size, length = (lax.axis_size(axis), value.shape[dim])
        up = [(i, (i + 1) % size) for i in range(size - 1)]
        down = [(j, i) for i, j in up]
        last = lax.slice_in_dim(value, length - width, length, axis=dim)
        first = lax.slice_in_dim(value, 0, width, axis=dim)
        before = lax.ppermute(last, axis, up)
        after = lax.ppermute(first, axis, down)
        value = jnp.concatenate([before, value, after], axis=dim)
    return value


def neighbours(padded):
    center = padded[..., 1:-1, 1:-1, 1:-1]
    beside_all = padded[..., 2:, 1:-1, 1:-1] + padded[..., :-2, 1:-1, 1:-1]
    beside_all = beside_all + padded[..., 1:-1, 2:, 1:-1] + padded[..., 1:-1, :-2, 1:-1]
    beside_all = beside_all + padded[..., 1:-1, 1:-1, 2:] + padded[..., 1:-1, 1:-1, :-2]
    return (center, beside_all)


def split_by_block(panel, density, source, class_index, class_values, trace_count, trace_cell):
    factors = relax_factors(SWEEPS)
    conduct = conduct_of(class_index, class_values)
    diagonal = MASS_TERM + 6.0 * conduct
    counts = trace_count[0]
    block_index = lax.axis_index(("col", "vol"))
    offsets = jnp.cumsum(counts) - counts
    target_rows = panel.shape[0]
    slot_count = trace_cell.shape[2]
    slot_ids = jnp.arange(slot_count, dtype=jnp.int32)
    target_ids = jnp.arange(target_rows, dtype=jnp.int32)
    own_count = lax.dynamic_index_in_dim(counts, block_index, keepdims=False)
    first_target = lax.dynamic_index_in_dim(offsets, block_index, keepdims=False)
    cell_ids = lax.dynamic_index_in_dim(trace_cell[0], block_index, keepdims=False)
    live_slots = slot_ids < own_count
    select = (
        ((first_target + slot_ids)[:, None] == target_ids[None, :]) & live_slots[:, None]
    ).astype(jnp.float32)
    volume = jnp.zeros(source.shape, jnp.float32)
    field_shape = volume.shape
    share_width = density.shape[1] // lax.axis_size("row")
    share_state = lax.dynamic_slice_in_dim(
        density, lax.axis_index("row") * share_width, share_width, 1
    )
    rounded = density.astype(jnp.bfloat16)
    lead = field_shape[0]
    for iteration in range(OUTER):
        partial_value = lax.dot_general(
            rounded, panel, (((1,), (1,)), ((), ())), preferred_element_type=jnp.float32
        )
        potential = lax.psum(partial_value, ("col", "vol"))
        slot_values = jnp.dot(potential, select.T, precision=lax.Precision.HIGHEST)
        right_side = source.reshape(lead, -1).at[:, cell_ids].add(slot_values).reshape(field_shape)
        relax_volume = volume
        for factor in factors:
            padded = padded_2(relax_volume, (("row", 1), ("col", 2), ("vol", 3)), 1)
            center, beside_all = neighbours(padded)
            relax_volume = (
                center + factor * (right_side - diagonal * center + conduct * beside_all) / diagonal
            )
        volume = relax_volume
        mismatch = volume.reshape(lead, -1)[:, cell_ids] - slot_values
        own_fluxes = jnp.dot(mismatch, select, precision=lax.Precision.HIGHEST)
        fluxes = lax.psum(own_fluxes, ("col", "vol"))
        update = jnp.dot(fluxes.astype(jnp.bfloat16), panel, preferred_element_type=jnp.float32)
        share_state = share_state + RELAXATION * lax.psum_scatter(
            update, "row", scatter_dimension=1, tiled=True
        )
        if iteration + 1 < OUTER:
            rounded = lax.all_gather(share_state.astype(jnp.bfloat16), "row", axis=1, tiled=True)
    density = lax.all_gather(share_state, "row", axis=1, tiled=True)
    return (density, volume)


def local(*args):
    sizes = [lax.axis_size(a) for a in ALL]
    if whole_slabs(sizes, args[0].shape[0], args[2].shape):
        return split_by_excitation(*args)
    return split_by_block(*args)


def whole_slabs(sizes, targets, block):
    fits = math.prod(sizes) == block[0] and sizes[:2] == [4, 2] and targets == block[3]
    return fits and all(size & (size - 1) == 0 for size in sizes)


def solution(mesh):
    placed = (
        P("row", ("col", "vol")),
        P(None, ("col", "vol")),
        P(None, "row", "col", "vol"),
        P("row", "col", "vol"),
        P(),
        P("row", None),
        P("row", None, None),
    )
    return jax.shard_map(
        local,
        mesh=mesh,
        in_specs=placed,
        out_specs=(P(None, ("col", "vol")), P(None, "row", "col", "vol")),
        check_vma=False,
    )
```

```python
import math

import jax
import jax.numpy as jnp
from jax import lax
from jax.experimental import pallas as pl
from jax.experimental.pallas import tpu as pltpu
from jax.sharding import PartitionSpec as P


SWEEPS = 4
OUTER = 2


MASS_TERM = 0.1
RELAXATION = 0.5
SPECTRUM_LOW = 0.1
SPECTRUM_HIGH = 2.0

ALL = ("row", "col", "vol")
SPOT_ROWS = 32
PARTS = 2
VMEM_BYTES = 16 * 2 ** 20
SLAB_BYTES = 40 * 2 ** 20


def relax_factors(count):
    middle = (SPECTRUM_HIGH + SPECTRUM_LOW) / 2.0
    spread = (SPECTRUM_HIGH - SPECTRUM_LOW) / 2.0
    return [
        1.0 / (middle + spread * math.cos(math.pi * (2 * order + 1) / (2 * count)))
        for order in range(count)
    ]


def conduct_of(class_index, class_values):
    classes = jnp.arange(class_values.shape[0], dtype=jnp.int32)
    return jnp.sum(
        jnp.where(
            class_index[None] == classes[:, None, None, None],
            class_values[:, None, None, None],
            jnp.float32(0.0),
        ),
        axis=0,
    )


MATES = (0, 1, 2)


def mated(value, axis, mate):
    return lax.ppermute(value, axis, [(i, i ^ mate) for i in range(lax.axis_size(axis))])


def start_call(density, panel, known, shape):
    rows, cols, vols = shape[:3]
    excitations, nodes = density.shape
    targets = panel.shape[0]
    width = nodes // rows
    lines = known.shape[0]
    owners = cols * vols

    def body(density_ref, panel_ref, known_ref, *rest):
        sent, rest = rest[:rows], rest[rows:]
        quarters = rest[:rows]
        nodes_ref, panel_buf, total_ref, picked_ref, sems = rest[rows:]
        r0, c0, v0 = (lax.axis_index(a) for a in ALL)
        low, high = r0 & 1, r0 >> 1
        sources = (low, low ^ 1, 2 + high, 2 + (high ^ 1))
        order = (1, 3, 0, 2)
        loads, stores = [], []
        for q in order:
            span = pl.ds(pl.multiple_of(sources[q] * width, width), width)
            pair = (
                pltpu.make_async_copy(panel_ref.at[:, span], panel_buf.at[q], sems.at[q]),
                pltpu.make_async_copy(density_ref.at[:, span], nodes_ref.at[q], sems.at[rows + q]),
            )
            for copy in pair:
                copy.start()
            loads.append(pair)
        for k in range(rows):
            sent[k][0:lines] = known_ref[...]
        total = jnp.zeros((targets, excitations), jnp.float32)
        for q, pair in zip(order, loads):
            for copy in pair:
                copy.wait()
            store = pltpu.make_async_copy(panel_buf.at[q], quarters[q], sems.at[2 * rows + q])
            store.start()
            stores.append(store)
            total += lax.dot_general(
                panel_buf[q], nodes_ref[q].astype(jnp.bfloat16), (((1,), (1,)), ((), ())),
                preferred_element_type=jnp.float32,
            )
        total_ref[...] = total.T
        for kr in range(rows):
            for kc in range(cols):
                for kv in range(vols):
                    owner = ((r0 ^ kr) * cols + (c0 ^ kc)) * vols + (v0 ^ kv)
                    place = kc * vols + kv
                    picked_ref[kr, place:place + 1] = total_ref[pl.ds(owner, 1)]
            pieces = [piece.astype(jnp.float32) for piece in parts_of(picked_ref[kr], 3)]
            pieces.append(jnp.zeros((owners, targets), jnp.float32))
            sent[kr][lines:] = jnp.concatenate(pieces).astype(jnp.bfloat16)
        for copy in stores:
            copy.wait()

    hbm = pl.BlockSpec(memory_space=pltpu.HBM)
    vmem = pl.BlockSpec(memory_space=pltpu.VMEM)
    return pl.pallas_call(
        body,
        out_shape=[jax.ShapeDtypeStruct((lines + 4 * owners, targets), known.dtype)] * rows
        + [jax.ShapeDtypeStruct((targets, width), panel.dtype)] * rows,
        in_specs=[hbm, hbm, vmem],
        out_specs=[vmem] * rows + [hbm] * rows,
        scratch_shapes=[
            pltpu.VMEM((rows, excitations, width), jnp.float32),
            pltpu.VMEM((rows, targets, width), panel.dtype),
            pltpu.VMEM((excitations, targets), jnp.float32),
            pltpu.VMEM((rows, owners, targets), jnp.float32),
            pltpu.SemaphoreType.DMA((3 * rows,)),
        ],
        name="start",
    )(density, panel, known)


def collect_call(shape, lines, known, other):
    rows, cols, vols = shape[:3]
    targets = known[0].shape[1]
    owners = cols * vols
    height = 4 * owners

    def body(*refs):
        ins, outs = refs[:2 * rows], refs[2 * rows:]
        for k in range(rows):
            own, mate = (ins[k + side * rows][...].astype(jnp.float32) for side in range(2))
            total = jnp.zeros((vols, targets), jnp.float32)
            for p in (2, 1, 0):
                total += own[p * owners:p * owners + vols] + mate[p * owners + vols:(p + 1) * owners]
            for v in range(vols):
                outs[v][k:k + 1] = total[v:v + 1]

    block = pl.BlockSpec((height, targets), lambda i: (lines // height, 0))
    whole = pl.BlockSpec((rows, targets), lambda i: (0, 0))
    return pl.pallas_call(
        body,
        grid=(1,),
        out_shape=[jax.ShapeDtypeStruct((rows, targets), jnp.float32)] * vols,
        in_specs=[block] * (2 * rows),
        out_specs=[whole] * vols,
        name="collect",
    )(*known, *other)


def prepare_call(shape, values, known, other):
    rows, cols, vols, bx, by, bz = shape
    blocks = cols * vols
    height = bx * blocks * by
    lines = bx * by
    targets = known[0].shape[-1]

    def body(values_ref, *refs):
        known_refs, other_refs = refs[:rows], refs[rows:2 * rows]
        inverse_ref, hit_ref, lane_ref = refs[2 * rows:]
        r0, c0, v0 = (lax.axis_index(a) for a in ALL)
        inverses = [
            1.0 / (MASS_TERM + 6.0 * jnp.full((by, bz), values_ref[i], jnp.float32))
            for i in range(values_ref.shape[0])
        ]
        row_ids = lax.broadcasted_iota(jnp.int32, (height, targets), 0)
        lane_ids = lax.broadcasted_iota(jnp.int32, (bz, targets), 0)
        for k in range(rows):
            spot = known_refs[k][vols * lines:vols * lines + SPOT_ROWS].astype(jnp.float32)
            spot = spot.astype(jnp.int32)
            line = spot[0:1] * (blocks * by) + spot[1:2]
            hit_ref[k ^ r0] = (row_ids == line).astype(jnp.bfloat16)
            lane_ref[k ^ r0] = (lane_ids == spot[2:3]).astype(jnp.bfloat16)
        for k in range(rows):
            for kc, refs_of in enumerate((known_refs, other_refs)):
                start = pl.multiple_of((kc ^ c0) * by, by)

                def plane(kv, carry, source=refs_of[k], start=start, k=k):
                    kind = source[pl.ds(pl.multiple_of(kv * lines, lines), lines)].astype(jnp.float32)
                    kind = kind.astype(jnp.int32).reshape(bx, by, bz)
                    choices, bit = [value[None] for value in inverses], 1
                    while len(choices) > 1:
                        odd = (kind & bit) != 0
                        merged = [jnp.where(odd, two, one)
                                  for one, two in zip(choices[0::2], choices[1::2])]
                        choices, bit = merged + choices[len(merged) * 2:], bit * 2
                    inverse = jnp.broadcast_to(choices[0], (bx, by, bz))
                    place = (pl.ds((k ^ r0) * bx, bx), kv ^ v0, pl.ds(start, by))
                    inverse_ref[place] = inverse
                    return carry

                lax.fori_loop(0, vols, plane, 0)

    vmem = pl.BlockSpec(memory_space=pltpu.VMEM)
    return pl.pallas_call(
        body,
        out_shape=[
            jax.ShapeDtypeStruct((rows * bx, vols, cols * by, bz), jnp.float32),
            jax.ShapeDtypeStruct((rows, height, targets), jnp.bfloat16),
            jax.ShapeDtypeStruct((rows, bz, targets), jnp.bfloat16),
        ],
        in_specs=[pl.BlockSpec(memory_space=pltpu.SMEM)] + [vmem] * (2 * rows),
        out_specs=[vmem] * 3,
        name="prepare",
    )(values, *known, *other)


def landed_call(volume):
    pieces = 4
    few = volume.shape[0] // pieces

    def body(in_ref, out_ref, held_ref, sems):
        loads, stores = [], []
        for i in range(pieces):
            span = pl.ds(i * few, few)
            loads.append(pltpu.make_async_copy(in_ref.at[span], held_ref.at[span], sems.at[i]))
            stores.append(pltpu.make_async_copy(held_ref.at[span], out_ref.at[span], sems.at[pieces + i]))
            loads[i].start()
        for load, store in zip(loads, stores):
            load.wait()
            store.start()
        for store in stores:
            store.wait()

    hbm = pl.BlockSpec(memory_space=pltpu.HBM)
    return pl.pallas_call(
        body,
        out_shape=jax.ShapeDtypeStruct(volume.shape, volume.dtype),
        in_specs=[hbm],
        out_specs=hbm,
        scratch_shapes=[
            pltpu.VMEM(volume.shape, volume.dtype), pltpu.SemaphoreType.DMA((2 * pieces,))
        ],
        name="landed",
    )(volume)


def parts_of(value, count):
    pieces = []
    for _ in range(count):
        piece = value.astype(jnp.bfloat16)
        pieces.append(piece)
        value = value - piece.astype(jnp.float32)
    return pieces


def slab_call(shape, first, source, inverse, hit, lane, parts, start=None):
    rows, cols, vols, bx, by, bz = shape
    blocks = cols * vols
    targets = lane.shape[-1]
    height = bx * blocks * by
    depth = rows * bx
    planes = (depth, vols, cols * by, bz)
    padded = (depth + 2, vols, cols * by, bz)
    factors = relax_factors(SWEEPS)

    def body(source_ref, inverse_ref, hit_ref, lane_ref, *rest):
        if first:
            *part_refs, far_ref, flux_ref, other_ref, scaled_ref, ratio_ref, sem = rest[:-6]
            out_ref, *held, load_sems = rest[-6:]
            fars = (lane_ref, hit_ref, source_ref, inverse_ref)
            lane_ref, hit_ref, source_ref, inverse_ref = held
            whole = [pltpu.make_async_copy(fars[i], held[i], load_sems.at[i]) for i in range(2)]
            chunks = []
            for r in range(rows):
                deep = pl.ds(r * bx, bx)
                chunks.append((
                    pltpu.make_async_copy(fars[2].at[r], held[2].at[r], load_sems.at[2 + 2 * r]),
                    pltpu.make_async_copy(fars[3].at[deep], held[3].at[deep], load_sems.at[3 + 2 * r]),
                ))
            for copy in whole + [copy for pair in chunks for copy in pair]:
                copy.start()
            result_ref = out_ref
        else:
            parts_ref, start_ref, far_ref, flux_ref, out_ref, *rest = rest
            other_ref, scaled_ref, ratio_ref, volume_ref, sem = rest
            result_ref = volume_ref
        sub = lax.broadcasted_iota(jnp.int32, (by, bz), 0)
        lan = lax.broadcasted_iota(jnp.int32, (by, bz), 1)
        for ref in (out_ref, other_ref):
            ref[0] = jnp.zeros(planes[1:], jnp.float32)
            ref[depth + 1] = jnp.zeros(planes[1:], jnp.float32)
        here = other_ref if first else start_ref
        potentials = []
        for r in range(rows):
            if first:
                place = pl.ds(r ^ lax.axis_index("row"), 1)
                potential = sum(part[place, :] for part in part_refs)
            else:
                potential = sum(
                    jnp.sum(parts_ref[r ^ mate, :, k, :], axis=0, keepdims=True)
                    for k, mate in enumerate(MATES)
                )
            potentials.append(potential)
            if first and r == 0:
                for copy in whole:
                    copy.wait()
            weights = [
                lane_ref[r] * piece.astype(jnp.bfloat16) for piece in parts_of(potential, 3)
            ]
            added = lax.dot_general(
                hit_ref[r], jnp.concatenate(weights, axis=0), (((1,), (1,)), ((), ())),
                preferred_element_type=jnp.float32,
            )
            added = added[:, :bz] + added[:, bz:2 * bz] + added[:, 2 * bz:]
            added = added.reshape(bx, vols, cols, by, bz)
            if first:
                for copy in chunks[r]:
                    copy.wait()
            for j in range(blocks):
                c, v = j // vols, j % vols
                span = (slice(r * bx, (r + 1) * bx), v, slice(c * by, (c + 1) * by))
                scaled = source_ref[r, j] + added[:, v, c]
                inverse = inverse_ref[span]
                scaled = scaled * inverse
                ratio_ref[span] = (1.0 - MASS_TERM * inverse) * (1.0 / 6.0)
                scaled_ref[span] = scaled
                if first:
                    here[1 + r * bx:1 + (r + 1) * bx, v, c * by:(c + 1) * by] = factors[0] * scaled

        sweeps = factors[1:] if first else factors
        for order, factor in enumerate(sweeps):
            last = order + 1 == len(sweeps)
            there = out_ref if (len(sweeps) - order) % 2 == 1 else other_ref

            def step(index, carry, here=here, there=there, last=last, factor=factor):
                for x in (index,):
                    tile = [here[x + 1, j % vols, (j // vols) * by:(j // vols + 1) * by]
                            for j in range(blocks)]
                    up = [pltpu.roll(t, 1, 1) for t in tile]
                    down = [pltpu.roll(t, bz - 1, 1) for t in tile]
                    for j in range(blocks):
                        c, v = j // vols, j % vols
                        own = slice(c * by, (c + 1) * by)
                        around = here[x, v, own] + here[x + 2, v, own]
                        if c > 0:
                            around += here[x + 1, v, c * by - 1:(c + 1) * by - 1]
                        else:
                            around += jnp.where(sub == 0, 0.0, pltpu.roll(tile[j], 1, 0))
                        if c < cols - 1:
                            around += here[x + 1, v, c * by + 1:(c + 1) * by + 1]
                        else:
                            around += jnp.where(sub == by - 1, 0.0, pltpu.roll(tile[j], by - 1, 0))
                        around += jnp.where(lan == 0, up[j - 1] if v > 0 else 0.0, up[j])
                        around += jnp.where(
                            lan == bz - 1, down[j + 1] if v < vols - 1 else 0.0, down[j]
                        )
                        value = (1.0 - factor) * tile[j] + factor * (
                            scaled_ref[x, v, own] + ratio_ref[x, v, own] * around
                        )
                        there[x + 1, v, own] = value
                        if last and not first:
                            volume_ref[x // bx, j, x % bx] = value
                return carry

            for index in range(depth):
                step(index, 0)
            here = there

        store = pltpu.make_async_copy(result_ref, far_ref, sem)
        store.start()
        for r in range(rows):
            part = here[1 + r * bx:1 + (r + 1) * bx].reshape(height, bz)
            met = sum(
                jnp.dot(piece, lane_ref[r], preferred_element_type=jnp.float32)
                for piece in parts_of(part, 2)
            )
            value = jnp.sum(met * hit_ref[r].astype(jnp.float32), axis=0, keepdims=True)
            value = value - potentials[r]
            for k, mate in enumerate(MATES):
                flux_ref[r ^ mate, :, k, :] = jnp.broadcast_to(value, (blocks, targets))
        store.wait()

    vmem = pl.BlockSpec(memory_space=pltpu.VMEM)
    operands = [source, inverse, hit, lane] + (list(parts) if first else [parts, start])
    fluxes = jax.ShapeDtypeStruct((rows, blocks, len(MATES), targets), jnp.float32)
    field = padded if first else (rows, blocks, bx, by, bz)
    field = jax.ShapeDtypeStruct(field, jnp.float32)
    hbm = pl.BlockSpec(memory_space=pltpu.HBM)
    work = [pltpu.VMEM(padded, jnp.float32)] + [pltpu.VMEM(planes, jnp.float32)] * 2
    done = pltpu.SemaphoreType.DMA(())
    if first:
        scratch = work + [done, pltpu.VMEM(padded, jnp.float32)]
        scratch += [pltpu.VMEM(value.shape, value.dtype) for value in (lane, hit, source, inverse)]
        scratch.append(pltpu.SemaphoreType.DMA((2 + 2 * rows,)))
    else:
        scratch = [pltpu.VMEM(padded, jnp.float32)] + work + [pltpu.VMEM(field.shape, jnp.float32), done]
    return pl.pallas_call(
        body,
        out_shape=[field, fluxes],
        in_specs=([hbm] * 4 if first else [vmem] * 4) + [vmem] * (len(operands) - 4),
        out_specs=[hbm, vmem],
        scratch_shapes=scratch,
        compiler_params=None if first else pltpu.CompilerParams(vmem_limit_bytes=SLAB_BYTES),
        name="slab_first" if first else "slab_last",
    )(*operands)


def update_call(flux, panels, part, parts):
    excitations, width = flux.shape[0], panels[0].shape[1] // parts
    span = slice(part * width, (part + 1) * width)

    def body(flux_ref, a_own, a_mate, b_own, b_far, a_ref, b_ref, b_mate, sem):
        load = pltpu.make_async_copy(b_far.at[:, span], b_mate, sem)
        load.start()
        fluxes = [flux_ref[:, k, :].astype(jnp.bfloat16) for k in range(len(MATES))]
        value = jnp.dot(fluxes[0], a_own[:, span], preferred_element_type=jnp.float32)
        value += jnp.dot(fluxes[1], a_mate[:, span], preferred_element_type=jnp.float32)
        a_ref[...] = value.astype(jnp.bfloat16)
        value = jnp.dot(fluxes[0], b_own[:, span], preferred_element_type=jnp.float32)
        load.wait()
        value += jnp.dot(fluxes[2], b_mate[...], preferred_element_type=jnp.float32)
        b_ref[...] = value.astype(jnp.bfloat16)

    vmem = pl.BlockSpec(memory_space=pltpu.VMEM)
    return pl.pallas_call(
        body,
        out_shape=[jax.ShapeDtypeStruct((excitations, width), jnp.bfloat16)] * 2,
        in_specs=[vmem] * 4 + [pl.BlockSpec(memory_space=pltpu.HBM)],
        out_specs=[vmem] * 2,
        scratch_shapes=[
            pltpu.VMEM((panels[0].shape[0], width), panels[0].dtype), pltpu.SemaphoreType.DMA(())
        ],
        compiler_params=pltpu.CompilerParams(vmem_limit_bytes=VMEM_BYTES),
        name="update",
    )(flux, *panels)


def potential_call(densities, halves, mates, panels, part, before):
    excitations = densities[0].shape[0]
    targets, width = panels[0].shape[0], panels[0].shape[1] // PARTS
    span = slice(part * width, (part + 1) * width)

    def body(a_density, b_density, a_half, b_half, a_other, b_other,
             a_own, a_mate, b_own, b_far, *rest):
        out_ref, b_mate, sem = rest[-3:]
        load = pltpu.make_async_copy(b_far.at[:, span], b_mate, sem)
        load.start()
        rounded = [
            (density[:, span] + RELAXATION * (half[...].astype(jnp.float32)
                                              + other[...].astype(jnp.float32))).astype(jnp.bfloat16)
            for density, half, other in (
                (a_density, a_half, a_other), (b_density, b_half, b_other))
        ]

        def met(value, panel):
            return lax.dot_general(
                panel, value, (((1,), (1,)), ((), ())), preferred_element_type=jnp.float32
            )

        def put(k, value):
            value = value.T
            out_ref[:, k, :] = value + rest[0][:, k, :] if before is not None else value

        put(0, met(rounded[0], a_own[:, span]) + met(rounded[1], b_own[:, span]))
        put(1, met(rounded[0], a_mate[:, span]))
        load.wait()
        put(2, met(rounded[1], b_mate[...]))

    vmem = pl.BlockSpec(memory_space=pltpu.VMEM)
    operands = [*densities, *halves, *mates, *panels] + ([] if before is None else [before])
    return pl.pallas_call(
        body,
        out_shape=jax.ShapeDtypeStruct((excitations, len(MATES), targets), jnp.float32),
        in_specs=[vmem] * 9 + [pl.BlockSpec(memory_space=pltpu.HBM)] + [vmem] * (len(operands) - 10),
        out_specs=vmem,
        scratch_shapes=[pltpu.VMEM((targets, width), panels[0].dtype), pltpu.SemaphoreType.DMA(())],
        compiler_params=pltpu.CompilerParams(vmem_limit_bytes=VMEM_BYTES),
        name="potential",
    )(*operands)


def trace_spots(trace_count, trace_cell, targets, shape):
    _, cols, vols, _, by, bz = shape
    counts = trace_count[0]
    offsets = jnp.cumsum(counts) - counts
    slot_ids = jnp.arange(trace_cell.shape[2], dtype=jnp.int32)
    live = slot_ids[None, :] < counts[:, None]
    owner = jnp.where(live, offsets[:, None] + slot_ids[None, :], -1)
    cell = trace_cell[0]
    block_ids = jnp.arange(cols * vols, dtype=jnp.int32)[:, None]
    line = (block_ids % vols) * (cols * by) + (block_ids // vols) * by + (cell // bz) % by
    code = ((cell // (by * bz)) * (cols * vols * by) + line) * bz + cell % bz
    match = owner[:, :, None] == jnp.arange(targets, dtype=jnp.int32)
    code = jnp.sum(jnp.where(match, code[:, :, None], 0), axis=(0, 1))
    line = code // bz
    span = cols * vols * by
    return jnp.stack([line // span, line % span, code % bz])


def split_by_excitation(panel, density, source, class_index, class_values, trace_count, trace_cell):
    rows, cols, vols = (lax.axis_size(a) for a in ALL)
    blocks = cols * vols
    excitations, bx, by, bz = source.shape
    targets, nodes = panel.shape
    width = nodes // rows
    here = lax.axis_index("row")
    low, high = here & 1, here >> 1
    shape = (rows, cols, vols, bx, by, bz)

    def columns(array, place):
        return lax.dynamic_slice_in_dim(array, place * width, width, 1)

    def around_axis(pieces, axis):
        return [pieces[0]] + [mated(piece, axis, k) for k, piece in enumerate(pieces) if k > 0]

    kinds = class_index.reshape(bx * by, bz).astype(jnp.bfloat16)
    kinds = around_axis([kinds] * vols, "vol")
    slab = lax.all_to_all(source, ALL, 0, 0, tiled=True)
    slab = slab.reshape(rows, blocks, bx, by, bz)
    spots = trace_spots(trace_count, trace_cell, targets, shape).astype(jnp.bfloat16)
    spots = jnp.pad(spots, ((0, SPOT_ROWS - spots.shape[0]), (0, 0)))
    known = jnp.concatenate(kinds + [spots])
    made = start_call(density, panel, known, shape)
    lines, quarters = known.shape[0], made[rows:]
    known = around_axis(made[:rows], "row")
    other = [mated(piece, "col", 1) for piece in known]
    parts = list(collect_call(shape, lines, known, other))
    for k in range(1, vols):
        parts[k] = mated(parts[k], "vol", k)

    panels = [quarters[0], None, quarters[2], None]
    panels[1] = mated(quarters[1], "row", 1)
    panels[3] = mated(quarters[3], "row", 2)
    densities = [columns(density, low), columns(density, 2 + high)]

    inverse, hit, lane = prepare_call(shape, class_values, known, other)
    volume, flux = slab_call(shape, True, slab, inverse, hit, lane, parts)
    flux = flux.reshape(excitations, len(MATES), targets)
    flux = lax.all_to_all(flux, ALL, 0, 0, tiled=True)
    halves, mates, parts = [], [], None
    for part in range(PARTS):
        halves.append(update_call(flux, panels, part, PARTS))
        mates.append([mated(halves[part][0], "row", 2), mated(halves[part][1], "row", 1)])
    for part in range(PARTS):
        parts = potential_call(densities, halves[part], mates[part], panels, part, parts)
    parts = lax.all_to_all(parts, ALL, 0, 0, tiled=True)
    parts = parts.reshape(rows, blocks, len(MATES), targets)
    volume, flux = slab_call(shape, False, slab, inverse, hit, lane, parts, volume)
    flux = flux.reshape(excitations, len(MATES), targets)
    flux = lax.all_to_all(flux, ALL, 0, 0, tiled=True)
    volume = volume.reshape(excitations, bx, by, bz)
    volume = lax.all_to_all(volume, ALL, 0, 0, tiled=True)
    volume = landed_call(volume)
    ends = update_call(flux, panels, 0, 1)
    end_mates = [mated(ends[0], "row", 2), mated(ends[1], "row", 1)]
    totals = []
    for group in range(2):
        firsts = [
            jnp.concatenate([pair[group] for pair in pairs], axis=1) for pairs in (halves, mates)
        ]
        a, b, c, d = (
            value.astype(jnp.float32) for value in (*firsts, ends[group], end_mates[group])
        )
        totals.append((RELAXATION * ((a + b) + (c + d))).astype(jnp.bfloat16))
    moved = [mated(totals[0], "row", 1), mated(totals[1], "row", 2)]
    change = [
        jnp.where(low == 0, totals[0], moved[0]), jnp.where(low == 0, moved[0], totals[0]),
        jnp.where(high == 0, totals[1], moved[1]), jnp.where(high == 0, moved[1], totals[1]),
    ]
    density = density + jnp.concatenate(change, axis=1).astype(jnp.float32)
    return (density, volume)


def padded_2(value, sides, width):
    for axis, dim in sides:
        size, length = (lax.axis_size(axis), value.shape[dim])
        up = [(i, (i + 1) % size) for i in range(size - 1)]
        down = [(j, i) for i, j in up]
        last = lax.slice_in_dim(value, length - width, length, axis=dim)
        first = lax.slice_in_dim(value, 0, width, axis=dim)
        before = lax.ppermute(last, axis, up)
        after = lax.ppermute(first, axis, down)
        value = jnp.concatenate([before, value, after], axis=dim)
    return value


def neighbours(padded):
    center = padded[..., 1:-1, 1:-1, 1:-1]
    beside_all = padded[..., 2:, 1:-1, 1:-1] + padded[..., :-2, 1:-1, 1:-1]
    beside_all = beside_all + padded[..., 1:-1, 2:, 1:-1] + padded[..., 1:-1, :-2, 1:-1]
    beside_all = beside_all + padded[..., 1:-1, 1:-1, 2:] + padded[..., 1:-1, 1:-1, :-2]
    return (center, beside_all)


def split_by_block(panel, density, source, class_index, class_values, trace_count, trace_cell):
    factors = relax_factors(SWEEPS)
    conduct = conduct_of(class_index, class_values)
    diagonal = MASS_TERM + 6.0 * conduct
    counts = trace_count[0]
    block_index = lax.axis_index(("col", "vol"))
    offsets = jnp.cumsum(counts) - counts
    target_rows = panel.shape[0]
    slot_count = trace_cell.shape[2]
    slot_ids = jnp.arange(slot_count, dtype=jnp.int32)
    target_ids = jnp.arange(target_rows, dtype=jnp.int32)
    own_count = lax.dynamic_index_in_dim(counts, block_index, keepdims=False)
    first_target = lax.dynamic_index_in_dim(offsets, block_index, keepdims=False)
    cell_ids = lax.dynamic_index_in_dim(trace_cell[0], block_index, keepdims=False)
    live_slots = slot_ids < own_count
    select = (
        ((first_target + slot_ids)[:, None] == target_ids[None, :]) & live_slots[:, None]
    ).astype(jnp.float32)
    volume = jnp.zeros(source.shape, jnp.float32)
    field_shape = volume.shape
    share_width = density.shape[1] // lax.axis_size("row")
    share_state = lax.dynamic_slice_in_dim(
        density, lax.axis_index("row") * share_width, share_width, 1
    )
    rounded = density.astype(jnp.bfloat16)
    lead = field_shape[0]
    for iteration in range(OUTER):
        partial_value = lax.dot_general(
            rounded, panel, (((1,), (1,)), ((), ())), preferred_element_type=jnp.float32
        )
        potential = lax.psum(partial_value, ("col", "vol"))
        slot_values = jnp.dot(potential, select.T, precision=lax.Precision.HIGHEST)
        right_side = source.reshape(lead, -1).at[:, cell_ids].add(slot_values).reshape(field_shape)
        relax_volume = volume
        for factor in factors:
            padded = padded_2(relax_volume, (("row", 1), ("col", 2), ("vol", 3)), 1)
            center, beside_all = neighbours(padded)
            relax_volume = (
                center + factor * (right_side - diagonal * center + conduct * beside_all) / diagonal
            )
        volume = relax_volume
        mismatch = volume.reshape(lead, -1)[:, cell_ids] - slot_values
        own_fluxes = jnp.dot(mismatch, select, precision=lax.Precision.HIGHEST)
        fluxes = lax.psum(own_fluxes, ("col", "vol"))
        update = jnp.dot(fluxes.astype(jnp.bfloat16), panel, preferred_element_type=jnp.float32)
        share_state = share_state + RELAXATION * lax.psum_scatter(
            update, "row", scatter_dimension=1, tiled=True
        )
        if iteration + 1 < OUTER:
            rounded = lax.all_gather(share_state.astype(jnp.bfloat16), "row", axis=1, tiled=True)
    density = lax.all_gather(share_state, "row", axis=1, tiled=True)
    return (density, volume)


def local(*args):
    sizes = [lax.axis_size(a) for a in ALL]
    if whole_slabs(sizes, args[0].shape[0], args[2].shape):
        return split_by_excitation(*args)
    return split_by_block(*args)


def whole_slabs(sizes, targets, block):
    return math.prod(sizes) == block[0] and sizes == [4, 2, 4] and targets == block[3]


def solution(mesh):
    placed = (
        P("row", ("col", "vol")),
        P(None, ("col", "vol")),
        P(None, "row", "col", "vol"),
        P("row", "col", "vol"),
        P(),
        P("row", None),
        P("row", None, None),
    )
    return jax.shard_map(
        local,
        mesh=mesh,
        in_specs=placed,
        out_specs=(P(None, ("col", "vol")), P(None, "row", "col", "vol")),
        check_vma=False,
    )
```

```python
import math

import jax
import jax.numpy as jnp
from jax import lax
from jax.experimental import pallas as pl
from jax.experimental.pallas import tpu as pltpu
from jax.sharding import PartitionSpec as P


SWEEPS = 4
OUTER = 2


MASS_TERM = 0.1
RELAXATION = 0.5
SPECTRUM_LOW = 0.1
SPECTRUM_HIGH = 2.0

ALL = ("row", "col", "vol")
SPOT_ROWS = 32
PARTS = 2
VMEM_BYTES = 16 * 2 ** 20
SLAB_BYTES = 40 * 2 ** 20


def relax_factors(count):
    middle = (SPECTRUM_HIGH + SPECTRUM_LOW) / 2.0
    spread = (SPECTRUM_HIGH - SPECTRUM_LOW) / 2.0
    return [
        1.0 / (middle + spread * math.cos(math.pi * (2 * order + 1) / (2 * count)))
        for order in range(count)
    ]


def conduct_of(class_index, class_values):
    classes = jnp.arange(class_values.shape[0], dtype=jnp.int32)
    return jnp.sum(
        jnp.where(
            class_index[None] == classes[:, None, None, None],
            class_values[:, None, None, None],
            jnp.float32(0.0),
        ),
        axis=0,
    )


MATES = (0, 1, 2)


def mated(value, axis, mate):
    return lax.ppermute(value, axis, [(i, i ^ mate) for i in range(lax.axis_size(axis))])


def start_call(density, panel, known, shape):
    rows, cols, vols = shape[:3]
    excitations, nodes = density.shape
    targets = panel.shape[0]
    width = nodes // rows
    lines = known.shape[0]
    owners = cols * vols

    def body(density_ref, panel_ref, known_ref, *rest):
        sent, rest = rest[:rows], rest[rows:]
        quarters = rest[:rows]
        nodes_ref, panel_buf, total_ref, picked_ref, sems = rest[rows:]
        r0, c0, v0 = (lax.axis_index(a) for a in ALL)
        low, high = r0 & 1, r0 >> 1
        sources = (low, low ^ 1, 2 + high, 2 + (high ^ 1))
        order = (1, 3, 0, 2)
        loads, stores = [], []
        for q in order:
            span = pl.ds(pl.multiple_of(sources[q] * width, width), width)
            pair = (
                pltpu.make_async_copy(panel_ref.at[:, span], panel_buf.at[q], sems.at[q]),
                pltpu.make_async_copy(density_ref.at[:, span], nodes_ref.at[q], sems.at[rows + q]),
            )
            for copy in pair:
                copy.start()
            loads.append(pair)
        for k in range(rows):
            sent[k][0:lines] = known_ref[...]
        total = jnp.zeros((targets, excitations), jnp.float32)
        for q, pair in zip(order, loads):
            for copy in pair:
                copy.wait()
            store = pltpu.make_async_copy(panel_buf.at[q], quarters[q], sems.at[2 * rows + q])
            store.start()
            stores.append(store)
            total += lax.dot_general(
                panel_buf[q], nodes_ref[q].astype(jnp.bfloat16), (((1,), (1,)), ((), ())),
                preferred_element_type=jnp.float32,
            )
        total_ref[...] = total.T
        for kr in range(rows):
            for kc in range(cols):
                for kv in range(vols):
                    owner = ((r0 ^ kr) * cols + (c0 ^ kc)) * vols + (v0 ^ kv)
                    place = kc * vols + kv
                    picked_ref[kr, place:place + 1] = total_ref[pl.ds(owner, 1)]
            pieces = [piece.astype(jnp.float32) for piece in parts_of(picked_ref[kr], 3)]
            pieces.append(jnp.zeros((owners, targets), jnp.float32))
            sent[kr][lines:] = jnp.concatenate(pieces).astype(jnp.bfloat16)
        for copy in stores:
            copy.wait()

    hbm = pl.BlockSpec(memory_space=pltpu.HBM)
    vmem = pl.BlockSpec(memory_space=pltpu.VMEM)
    return pl.pallas_call(
        body,
        out_shape=[jax.ShapeDtypeStruct((lines + 4 * owners, targets), known.dtype)] * rows
        + [jax.ShapeDtypeStruct((targets, width), panel.dtype)] * rows,
        in_specs=[hbm, hbm, vmem],
        out_specs=[vmem] * rows + [hbm] * rows,
        scratch_shapes=[
            pltpu.VMEM((rows, excitations, width), jnp.float32),
            pltpu.VMEM((rows, targets, width), panel.dtype),
            pltpu.VMEM((excitations, targets), jnp.float32),
            pltpu.VMEM((rows, owners, targets), jnp.float32),
            pltpu.SemaphoreType.DMA((3 * rows,)),
        ],
        name="start",
    )(density, panel, known)


def collect_call(shape, lines, known, other):
    rows, cols, vols = shape[:3]
    targets = known[0].shape[1]
    owners = cols * vols
    height = 4 * owners

    def body(*refs):
        ins, outs = refs[:2 * rows], refs[2 * rows:]
        for k in range(rows):
            own, mate = (ins[k + side * rows][...].astype(jnp.float32) for side in range(2))
            total = jnp.zeros((vols, targets), jnp.float32)
            for p in (2, 1, 0):
                total += own[p * owners:p * owners + vols] + mate[p * owners + vols:(p + 1) * owners]
            for v in range(vols):
                outs[v][k:k + 1] = total[v:v + 1]

    block = pl.BlockSpec((height, targets), lambda i: (lines // height, 0))
    whole = pl.BlockSpec((rows, targets), lambda i: (0, 0))
    return pl.pallas_call(
        body,
        grid=(1,),
        out_shape=[jax.ShapeDtypeStruct((rows, targets), jnp.float32)] * vols,
        in_specs=[block] * (2 * rows),
        out_specs=[whole] * vols,
        name="collect",
    )(*known, *other)


def prepare_call(shape, values, known, other):
    rows, cols, vols, bx, by, bz = shape
    blocks = cols * vols
    height = bx * blocks * by
    lines = bx * by
    targets = known[0].shape[-1]

    def body(values_ref, *refs):
        known_refs, other_refs = refs[:rows], refs[rows:2 * rows]
        inverse_ref, hit_ref, lane_ref = refs[2 * rows:]
        r0, c0, v0 = (lax.axis_index(a) for a in ALL)
        inverses = [
            1.0 / (MASS_TERM + 6.0 * jnp.full((by, bz), values_ref[i], jnp.float32))
            for i in range(values_ref.shape[0])
        ]
        row_ids = lax.broadcasted_iota(jnp.int32, (height, targets), 0)
        lane_ids = lax.broadcasted_iota(jnp.int32, (bz, targets), 0)
        for k in range(rows):
            spot = known_refs[k][vols * lines:vols * lines + SPOT_ROWS].astype(jnp.float32)
            spot = spot.astype(jnp.int32)
            line = spot[0:1] * (blocks * by) + spot[1:2]
            hit_ref[k ^ r0] = (row_ids == line).astype(jnp.bfloat16)
            lane_ref[k ^ r0] = (lane_ids == spot[2:3]).astype(jnp.bfloat16)
        for k in range(rows):
            for kc, refs_of in enumerate((known_refs, other_refs)):
                start = pl.multiple_of((kc ^ c0) * by, by)

                def plane(kv, carry, source=refs_of[k], start=start, k=k):
                    kind = source[pl.ds(pl.multiple_of(kv * lines, lines), lines)].astype(jnp.float32)
                    kind = kind.astype(jnp.int32).reshape(bx, by, bz)
                    choices, bit = [value[None] for value in inverses], 1
                    while len(choices) > 1:
                        odd = (kind & bit) != 0
                        merged = [jnp.where(odd, two, one)
                                  for one, two in zip(choices[0::2], choices[1::2])]
                        choices, bit = merged + choices[len(merged) * 2:], bit * 2
                    inverse = jnp.broadcast_to(choices[0], (bx, by, bz))
                    place = (pl.ds((k ^ r0) * bx, bx), kv ^ v0, pl.ds(start, by))
                    inverse_ref[place] = inverse
                    return carry

                lax.fori_loop(0, vols, plane, 0)

    vmem = pl.BlockSpec(memory_space=pltpu.VMEM)
    return pl.pallas_call(
        body,
        out_shape=[
            jax.ShapeDtypeStruct((rows * bx, vols, cols * by, bz), jnp.float32),
            jax.ShapeDtypeStruct((rows, height, targets), jnp.bfloat16),
            jax.ShapeDtypeStruct((rows, bz, targets), jnp.bfloat16),
        ],
        in_specs=[pl.BlockSpec(memory_space=pltpu.SMEM)] + [vmem] * (2 * rows),
        out_specs=[vmem] * 3,
        name="prepare",
    )(values, *known, *other)


def landed_call(volume):
    pieces = 4
    few = volume.shape[0] // pieces

    def body(in_ref, out_ref, held_ref, sems):
        loads, stores = [], []
        for i in range(pieces):
            span = pl.ds(i * few, few)
            loads.append(pltpu.make_async_copy(in_ref.at[span], held_ref.at[span], sems.at[i]))
            stores.append(pltpu.make_async_copy(held_ref.at[span], out_ref.at[span], sems.at[pieces + i]))
            loads[i].start()
        for load, store in zip(loads, stores):
            load.wait()
            store.start()
        for store in stores:
            store.wait()

    hbm = pl.BlockSpec(memory_space=pltpu.HBM)
    return pl.pallas_call(
        body,
        out_shape=jax.ShapeDtypeStruct(volume.shape, volume.dtype),
        in_specs=[hbm],
        out_specs=hbm,
        scratch_shapes=[
            pltpu.VMEM(volume.shape, volume.dtype), pltpu.SemaphoreType.DMA((2 * pieces,))
        ],
        name="landed",
    )(volume)


def parts_of(value, count):
    pieces = []
    for _ in range(count):
        piece = value.astype(jnp.bfloat16)
        pieces.append(piece)
        value = value - piece.astype(jnp.float32)
    return pieces


def slab_call(shape, first, source, inverse, hit, lane, parts, start=None):
    rows, cols, vols, bx, by, bz = shape
    blocks = cols * vols
    targets = lane.shape[-1]
    height = bx * blocks * by
    depth = rows * bx
    planes = (depth, vols, cols * by, bz)
    padded = (depth + 2, vols, cols * by, bz)
    factors = relax_factors(SWEEPS)

    def body(source_ref, inverse_ref, hit_ref, lane_ref, *rest):
        if first:
            *part_refs, out_ref, flux_ref, other_ref, scaled_ref, ratio_ref = rest
        else:
            parts_ref, start_ref, far_ref, flux_ref, out_ref, *rest = rest
            other_ref, scaled_ref, ratio_ref, volume_ref, sem = rest
        sub = lax.broadcasted_iota(jnp.int32, (by, bz), 0)
        lan = lax.broadcasted_iota(jnp.int32, (by, bz), 1)
        for ref in (out_ref, other_ref):
            ref[0] = jnp.zeros(planes[1:], jnp.float32)
            ref[depth + 1] = jnp.zeros(planes[1:], jnp.float32)
        here = other_ref if first else start_ref
        potentials = []
        for r in range(rows):
            if first:
                place = pl.ds(r ^ lax.axis_index("row"), 1)
                potential = sum(part[place, :] for part in part_refs)
            else:
                potential = sum(
                    jnp.sum(parts_ref[r ^ mate, :, k, :], axis=0, keepdims=True)
                    for k, mate in enumerate(MATES)
                )
            potentials.append(potential)
            weights = [
                lane_ref[r] * piece.astype(jnp.bfloat16) for piece in parts_of(potential, 3)
            ]
            added = lax.dot_general(
                hit_ref[r], jnp.concatenate(weights, axis=0), (((1,), (1,)), ((), ())),
                preferred_element_type=jnp.float32,
            )
            added = added[:, :bz] + added[:, bz:2 * bz] + added[:, 2 * bz:]
            added = added.reshape(bx, vols, cols, by, bz)
            for j in range(blocks):
                c, v = j // vols, j % vols
                span = (slice(r * bx, (r + 1) * bx), v, slice(c * by, (c + 1) * by))
                scaled = source_ref[r, j] + added[:, v, c]
                inverse = inverse_ref[span]
                scaled = scaled * inverse
                ratio_ref[span] = (1.0 - MASS_TERM * inverse) * (1.0 / 6.0)
                scaled_ref[span] = scaled
                if first:
                    here[1 + r * bx:1 + (r + 1) * bx, v, c * by:(c + 1) * by] = factors[0] * scaled

        sweeps = factors[1:] if first else factors
        for order, factor in enumerate(sweeps):
            last = order + 1 == len(sweeps)
            there = out_ref if (len(sweeps) - order) % 2 == 1 else other_ref

            def step(index, carry, here=here, there=there, last=last, factor=factor):
                for x in (index,):
                    tile = [here[x + 1, j % vols, (j // vols) * by:(j // vols + 1) * by]
                            for j in range(blocks)]
                    up = [pltpu.roll(t, 1, 1) for t in tile]
                    down = [pltpu.roll(t, bz - 1, 1) for t in tile]
                    for j in range(blocks):
                        c, v = j // vols, j % vols
                        own = slice(c * by, (c + 1) * by)
                        around = here[x, v, own] + here[x + 2, v, own]
                        if c > 0:
                            around += here[x + 1, v, c * by - 1:(c + 1) * by - 1]
                        else:
                            around += jnp.where(sub == 0, 0.0, pltpu.roll(tile[j], 1, 0))
                        if c < cols - 1:
                            around += here[x + 1, v, c * by + 1:(c + 1) * by + 1]
                        else:
                            around += jnp.where(sub == by - 1, 0.0, pltpu.roll(tile[j], by - 1, 0))
                        around += jnp.where(lan == 0, up[j - 1] if v > 0 else 0.0, up[j])
                        around += jnp.where(
                            lan == bz - 1, down[j + 1] if v < vols - 1 else 0.0, down[j]
                        )
                        value = (1.0 - factor) * tile[j] + factor * (
                            scaled_ref[x, v, own] + ratio_ref[x, v, own] * around
                        )
                        there[x + 1, v, own] = value
                        if last and not first:
                            volume_ref[x // bx, j, x % bx] = value
                return carry

            for index in range(depth):
                step(index, 0)
            here = there

        if not first:
            store = pltpu.make_async_copy(volume_ref, far_ref, sem)
            store.start()
        for r in range(rows):
            part = here[1 + r * bx:1 + (r + 1) * bx].reshape(height, bz)
            met = sum(
                jnp.dot(piece, lane_ref[r], preferred_element_type=jnp.float32)
                for piece in parts_of(part, 2)
            )
            value = jnp.sum(met * hit_ref[r].astype(jnp.float32), axis=0, keepdims=True)
            value = value - potentials[r]
            for k, mate in enumerate(MATES):
                flux_ref[r ^ mate, :, k, :] = jnp.broadcast_to(value, (blocks, targets))
        if not first:
            store.wait()

    vmem = pl.BlockSpec(memory_space=pltpu.VMEM)
    operands = [source, inverse, hit, lane] + (list(parts) if first else [parts, start])
    fluxes = jax.ShapeDtypeStruct((rows, blocks, len(MATES), targets), jnp.float32)
    field = padded if first else (rows, blocks, bx, by, bz)
    field = jax.ShapeDtypeStruct(field, jnp.float32)
    scratch = [pltpu.VMEM(padded, jnp.float32)] + [pltpu.VMEM(planes, jnp.float32)] * 2
    if not first:
        scratch = [pltpu.VMEM(padded, jnp.float32)] + scratch
        scratch += [pltpu.VMEM(field.shape, jnp.float32), pltpu.SemaphoreType.DMA(())]
    return pl.pallas_call(
        body,
        out_shape=[field, fluxes],
        in_specs=[vmem] * len(operands),
        out_specs=[vmem if first else pl.BlockSpec(memory_space=pltpu.HBM), vmem],
        scratch_shapes=scratch,
        compiler_params=None if first else pltpu.CompilerParams(vmem_limit_bytes=SLAB_BYTES),
        name="slab_first" if first else "slab_last",
    )(*operands)


def update_call(flux, panels, part, parts, keep):
    excitations, width = flux.shape[0], panels[0].shape[1] // parts
    span = slice(part * width, (part + 1) * width)
    far = jax.ShapeDtypeStruct((panels[3].shape[0], width), panels[3].dtype)

    def body(flux_ref, a_own, a_mate, b_own, b_far, a_ref, b_ref, b_mate, sem):
        load = pltpu.make_async_copy(b_far.at[:, span], b_mate, sem)
        load.start()
        fluxes = [flux_ref[:, k, :].astype(jnp.bfloat16) for k in range(len(MATES))]
        value = jnp.dot(fluxes[0], a_own[:, span], preferred_element_type=jnp.float32)
        value += jnp.dot(fluxes[1], a_mate[:, span], preferred_element_type=jnp.float32)
        a_ref[...] = value.astype(jnp.bfloat16)
        value = jnp.dot(fluxes[0], b_own[:, span], preferred_element_type=jnp.float32)
        load.wait()
        value += jnp.dot(fluxes[2], b_mate[...], preferred_element_type=jnp.float32)
        b_ref[...] = value.astype(jnp.bfloat16)

    vmem = pl.BlockSpec(memory_space=pltpu.VMEM)
    return pl.pallas_call(
        body,
        out_shape=[jax.ShapeDtypeStruct((excitations, width), jnp.bfloat16)] * 2 + ([far] if keep else []),
        in_specs=[vmem] * 4 + [pl.BlockSpec(memory_space=pltpu.HBM)],
        out_specs=[vmem] * (3 if keep else 2),
        scratch_shapes=([] if keep else [pltpu.VMEM(far.shape, far.dtype)]) + [pltpu.SemaphoreType.DMA(())],
        compiler_params=pltpu.CompilerParams(vmem_limit_bytes=VMEM_BYTES),
        name="update",
    )(flux, *panels)


def potential_call(densities, halves, mates, panels, part, before):
    excitations = densities[0].shape[0]
    targets, width = panels[0].shape[0], panels[0].shape[1] // PARTS
    span = slice(part * width, (part + 1) * width)

    def body(a_density, b_density, a_half, b_half, a_other, b_other,
             a_own, a_mate, b_own, b_mate, *rest):
        out_ref = rest[-1]
        rounded = [
            (density[:, span] + RELAXATION * (half[...].astype(jnp.float32)
                                              + other[...].astype(jnp.float32))).astype(jnp.bfloat16)
            for density, half, other in (
                (a_density, a_half, a_other), (b_density, b_half, b_other))
        ]

        def met(value, panel):
            return lax.dot_general(
                panel, value, (((1,), (1,)), ((), ())), preferred_element_type=jnp.float32
            )

        def put(k, value):
            value = value.T
            out_ref[:, k, :] = value + rest[0][:, k, :] if before is not None else value

        put(0, met(rounded[0], a_own[:, span]) + met(rounded[1], b_own[:, span]))
        put(1, met(rounded[0], a_mate[:, span]))
        put(2, met(rounded[1], b_mate[...]))

    vmem = pl.BlockSpec(memory_space=pltpu.VMEM)
    operands = [*densities, *halves, *mates, *panels] + ([] if before is None else [before])
    return pl.pallas_call(
        body,
        out_shape=jax.ShapeDtypeStruct((excitations, len(MATES), targets), jnp.float32),
        in_specs=[vmem] * len(operands),
        out_specs=vmem,
        compiler_params=pltpu.CompilerParams(vmem_limit_bytes=VMEM_BYTES),
        name="potential",
    )(*operands)


def totals_call(firsts, ends):
    groups = len(ends)
    width = firsts[0][0][0].shape[1]

    def body(*refs):
        outs, rest = refs[-groups:], list(refs[:-groups])
        first_refs = [[[rest.pop(0) for _ in pair] for pair in parts] for parts in firsts]
        end_refs = [[rest.pop(0) for _ in pair] for pair in ends]
        for group in range(groups):
            for part, (a, b) in enumerate(first_refs[group]):
                span = slice(part * width, (part + 1) * width)
                pieces = [a[...], b[...]] + [ref[:, span] for ref in end_refs[group]]
                a, b, c, d = (piece.astype(jnp.float32) for piece in pieces)
                outs[group][:, span] = (RELAXATION * ((a + b) + (c + d))).astype(jnp.bfloat16)

    vmem = pl.BlockSpec(memory_space=pltpu.VMEM)
    operands = [value for parts in firsts for pair in parts for value in pair]
    operands += [value for pair in ends for value in pair]
    return pl.pallas_call(
        body,
        out_shape=[jax.ShapeDtypeStruct(pair[0].shape, jnp.bfloat16) for pair in ends],
        in_specs=[vmem] * len(operands),
        out_specs=[vmem] * groups,
        compiler_params=pltpu.CompilerParams(vmem_limit_bytes=VMEM_BYTES),
        name="totals",
    )(*operands)


def trace_spots(trace_count, trace_cell, targets, shape):
    _, cols, vols, _, by, bz = shape
    counts = trace_count[0]
    offsets = jnp.cumsum(counts) - counts
    slot_ids = jnp.arange(trace_cell.shape[2], dtype=jnp.int32)
    live = slot_ids[None, :] < counts[:, None]
    owner = jnp.where(live, offsets[:, None] + slot_ids[None, :], -1)
    cell = trace_cell[0]
    block_ids = jnp.arange(cols * vols, dtype=jnp.int32)[:, None]
    line = (block_ids % vols) * (cols * by) + (block_ids // vols) * by + (cell // bz) % by
    code = ((cell // (by * bz)) * (cols * vols * by) + line) * bz + cell % bz
    match = owner[:, :, None] == jnp.arange(targets, dtype=jnp.int32)
    code = jnp.sum(jnp.where(match, code[:, :, None], 0), axis=(0, 1))
    line = code // bz
    span = cols * vols * by
    return jnp.stack([line // span, line % span, code % bz])


def split_by_excitation(panel, density, source, class_index, class_values, trace_count, trace_cell):
    rows, cols, vols = (lax.axis_size(a) for a in ALL)
    blocks = cols * vols
    excitations, bx, by, bz = source.shape
    targets, nodes = panel.shape
    width = nodes // rows
    here = lax.axis_index("row")
    low, high = here & 1, here >> 1
    shape = (rows, cols, vols, bx, by, bz)

    def columns(array, place):
        return lax.dynamic_slice_in_dim(array, place * width, width, 1)

    def around_axis(pieces, axis):
        return [pieces[0]] + [mated(piece, axis, k) for k, piece in enumerate(pieces) if k > 0]

    kinds = class_index.reshape(bx * by, bz).astype(jnp.bfloat16)
    kinds = around_axis([kinds] * vols, "vol")
    slab = lax.all_to_all(source, ALL, 0, 0, tiled=True)
    slab = slab.reshape(rows, blocks, bx, by, bz)
    spots = trace_spots(trace_count, trace_cell, targets, shape).astype(jnp.bfloat16)
    spots = jnp.pad(spots, ((0, SPOT_ROWS - spots.shape[0]), (0, 0)))
    known = jnp.concatenate(kinds + [spots])
    made = start_call(density, panel, known, shape)
    lines, quarters = known.shape[0], made[rows:]
    known = around_axis(made[:rows], "row")
    other = [mated(piece, "col", 1) for piece in known]
    parts = list(collect_call(shape, lines, known, other))
    for k in range(1, vols):
        parts[k] = mated(parts[k], "vol", k)

    panels = [quarters[0], None, quarters[2], None]
    panels[1] = mated(quarters[1], "row", 1)
    panels[3] = mated(quarters[3], "row", 2)
    densities = [columns(density, low), columns(density, 2 + high)]

    inverse, hit, lane = prepare_call(shape, class_values, known, other)
    volume, flux = slab_call(shape, True, slab, inverse, hit, lane, parts)
    flux = flux.reshape(excitations, len(MATES), targets)
    flux = lax.all_to_all(flux, ALL, 0, 0, tiled=True)
    halves, mates, fars, parts = [], [], [], None
    for part in range(PARTS):
        *pair, far = update_call(flux, panels, part, PARTS, True)
        halves.append(pair)
        fars.append(far)
        mates.append([mated(halves[part][0], "row", 2), mated(halves[part][1], "row", 1)])
    for part in range(PARTS):
        parts = potential_call(
            densities, halves[part], mates[part], [*panels[:3], fars[part]], part, parts
        )
    parts = lax.all_to_all(parts, ALL, 0, 0, tiled=True)
    parts = parts.reshape(rows, blocks, len(MATES), targets)
    volume, flux = slab_call(shape, False, slab, inverse, hit, lane, parts, volume)
    flux = flux.reshape(excitations, len(MATES), targets)
    flux = lax.all_to_all(flux, ALL, 0, 0, tiled=True)
    volume = volume.reshape(excitations, bx, by, bz)
    volume = lax.all_to_all(volume, ALL, 0, 0, tiled=True)
    volume = landed_call(volume)
    ends = update_call(flux, panels, 0, 1, False)
    end_mates = [mated(ends[0], "row", 2), mated(ends[1], "row", 1)]
    totals = totals_call(
        [[(halves[part][g], mates[part][g]) for part in range(PARTS)] for g in range(2)],
        list(zip(ends, end_mates)),
    )
    moved = [mated(totals[0], "row", 1), mated(totals[1], "row", 2)]
    change = [
        jnp.where(low == 0, totals[0], moved[0]), jnp.where(low == 0, moved[0], totals[0]),
        jnp.where(high == 0, totals[1], moved[1]), jnp.where(high == 0, moved[1], totals[1]),
    ]
    density = density + jnp.concatenate(change, axis=1).astype(jnp.float32)
    return (density, volume)


def padded_2(value, sides, width):
    for axis, dim in sides:
        size, length = (lax.axis_size(axis), value.shape[dim])
        up = [(i, (i + 1) % size) for i in range(size - 1)]
        down = [(j, i) for i, j in up]
        last = lax.slice_in_dim(value, length - width, length, axis=dim)
        first = lax.slice_in_dim(value, 0, width, axis=dim)
        before = lax.ppermute(last, axis, up)
        after = lax.ppermute(first, axis, down)
        value = jnp.concatenate([before, value, after], axis=dim)
    return value


def neighbours(padded):
    center = padded[..., 1:-1, 1:-1, 1:-1]
    beside_all = padded[..., 2:, 1:-1, 1:-1] + padded[..., :-2, 1:-1, 1:-1]
    beside_all = beside_all + padded[..., 1:-1, 2:, 1:-1] + padded[..., 1:-1, :-2, 1:-1]
    beside_all = beside_all + padded[..., 1:-1, 1:-1, 2:] + padded[..., 1:-1, 1:-1, :-2]
    return (center, beside_all)


def split_by_block(panel, density, source, class_index, class_values, trace_count, trace_cell):
    factors = relax_factors(SWEEPS)
    conduct = conduct_of(class_index, class_values)
    diagonal = MASS_TERM + 6.0 * conduct
    counts = trace_count[0]
    block_index = lax.axis_index(("col", "vol"))
    offsets = jnp.cumsum(counts) - counts
    target_rows = panel.shape[0]
    slot_count = trace_cell.shape[2]
    slot_ids = jnp.arange(slot_count, dtype=jnp.int32)
    target_ids = jnp.arange(target_rows, dtype=jnp.int32)
    own_count = lax.dynamic_index_in_dim(counts, block_index, keepdims=False)
    first_target = lax.dynamic_index_in_dim(offsets, block_index, keepdims=False)
    cell_ids = lax.dynamic_index_in_dim(trace_cell[0], block_index, keepdims=False)
    live_slots = slot_ids < own_count
    select = (
        ((first_target + slot_ids)[:, None] == target_ids[None, :]) & live_slots[:, None]
    ).astype(jnp.float32)
    volume = jnp.zeros(source.shape, jnp.float32)
    field_shape = volume.shape
    share_width = density.shape[1] // lax.axis_size("row")
    share_state = lax.dynamic_slice_in_dim(
        density, lax.axis_index("row") * share_width, share_width, 1
    )
    rounded = density.astype(jnp.bfloat16)
    lead = field_shape[0]
    for iteration in range(OUTER):
        partial_value = lax.dot_general(
            rounded, panel, (((1,), (1,)), ((), ())), preferred_element_type=jnp.float32
        )
        potential = lax.psum(partial_value, ("col", "vol"))
        slot_values = jnp.dot(potential, select.T, precision=lax.Precision.HIGHEST)
        right_side = source.reshape(lead, -1).at[:, cell_ids].add(slot_values).reshape(field_shape)
        relax_volume = volume
        for factor in factors:
            padded = padded_2(relax_volume, (("row", 1), ("col", 2), ("vol", 3)), 1)
            center, beside_all = neighbours(padded)
            relax_volume = (
                center + factor * (right_side - diagonal * center + conduct * beside_all) / diagonal
            )
        volume = relax_volume
        mismatch = volume.reshape(lead, -1)[:, cell_ids] - slot_values
        own_fluxes = jnp.dot(mismatch, select, precision=lax.Precision.HIGHEST)
        fluxes = lax.psum(own_fluxes, ("col", "vol"))
        update = jnp.dot(fluxes.astype(jnp.bfloat16), panel, preferred_element_type=jnp.float32)
        share_state = share_state + RELAXATION * lax.psum_scatter(
            update, "row", scatter_dimension=1, tiled=True
        )
        if iteration + 1 < OUTER:
            rounded = lax.all_gather(share_state.astype(jnp.bfloat16), "row", axis=1, tiled=True)
    density = lax.all_gather(share_state, "row", axis=1, tiled=True)
    return (density, volume)


def local(*args):
    sizes = [lax.axis_size(a) for a in ALL]
    if whole_slabs(sizes, args[0].shape[0], args[2].shape):
        return split_by_excitation(*args)
    return split_by_block(*args)


def whole_slabs(sizes, targets, block):
    return math.prod(sizes) == block[0] and sizes == [4, 2, 4] and targets == block[3]


def solution(mesh):
    placed = (
        P("row", ("col", "vol")),
        P(None, ("col", "vol")),
        P(None, "row", "col", "vol"),
        P("row", "col", "vol"),
        P(),
        P("row", None),
        P("row", None, None),
    )
    return jax.shard_map(
        local,
        mesh=mesh,
        in_specs=placed,
        out_specs=(P(None, ("col", "vol")), P(None, "row", "col", "vol")),
        check_vma=False,
    )
```

```python
import math

import jax
import jax.numpy as jnp
from jax import lax
from jax.experimental import pallas as pl
from jax.experimental.pallas import tpu as pltpu
from jax.sharding import PartitionSpec as P


SWEEPS = 4
OUTER = 2


MASS_TERM = 0.1
RELAXATION = 0.5
SPECTRUM_LOW = 0.1
SPECTRUM_HIGH = 2.0

ALL = ("row", "col", "vol")
SPOT_ROWS = 32
PARTS = 2
VMEM_BYTES = 16 * 2 ** 20
SLAB_BYTES = 40 * 2 ** 20


def relax_factors(count):
    middle = (SPECTRUM_HIGH + SPECTRUM_LOW) / 2.0
    spread = (SPECTRUM_HIGH - SPECTRUM_LOW) / 2.0
    return [
        1.0 / (middle + spread * math.cos(math.pi * (2 * order + 1) / (2 * count)))
        for order in range(count)
    ]


def conduct_of(class_index, class_values):
    classes = jnp.arange(class_values.shape[0], dtype=jnp.int32)
    return jnp.sum(
        jnp.where(
            class_index[None] == classes[:, None, None, None],
            class_values[:, None, None, None],
            jnp.float32(0.0),
        ),
        axis=0,
    )


MATES = (0, 1, 2)


def mated(value, axis, mate):
    return lax.ppermute(value, axis, [(i, i ^ mate) for i in range(lax.axis_size(axis))])


def start_call(density, panel, known, shape):
    rows, cols, vols = shape[:3]
    excitations, nodes = density.shape
    targets = panel.shape[0]
    width = nodes // rows
    lines = known.shape[0]
    owners = cols * vols

    def body(density_ref, panel_ref, known_ref, *rest):
        sent, rest = rest[:rows], rest[rows:]
        quarters = rest[:rows]
        nodes_ref, panel_buf, total_ref, picked_ref, sems = rest[rows:]
        r0, c0, v0 = (lax.axis_index(a) for a in ALL)
        low, high = r0 & 1, r0 >> 1
        sources = (low, low ^ 1, 2 + high, 2 + (high ^ 1))
        order = (1, 3, 0, 2)
        loads, stores = [], []
        for q in order:
            span = pl.ds(pl.multiple_of(sources[q] * width, width), width)
            pair = (
                pltpu.make_async_copy(panel_ref.at[:, span], panel_buf.at[q], sems.at[q]),
                pltpu.make_async_copy(density_ref.at[:, span], nodes_ref.at[q], sems.at[rows + q]),
            )
            for copy in pair:
                copy.start()
            loads.append(pair)
        for k in range(rows):
            sent[k][0:lines] = known_ref[...]
        total = jnp.zeros((targets, excitations), jnp.float32)
        for q, pair in zip(order, loads):
            for copy in pair:
                copy.wait()
            store = pltpu.make_async_copy(panel_buf.at[q], quarters[q], sems.at[2 * rows + q])
            store.start()
            stores.append(store)
            total += lax.dot_general(
                panel_buf[q], nodes_ref[q].astype(jnp.bfloat16), (((1,), (1,)), ((), ())),
                preferred_element_type=jnp.float32,
            )
        total_ref[...] = total.T
        for kr in range(rows):
            for kc in range(cols):
                for kv in range(vols):
                    owner = ((r0 ^ kr) * cols + (c0 ^ kc)) * vols + (v0 ^ kv)
                    place = kc * vols + kv
                    picked_ref[kr, place:place + 1] = total_ref[pl.ds(owner, 1)]
            pieces = [piece.astype(jnp.float32) for piece in parts_of(picked_ref[kr], 3)]
            pieces.append(jnp.zeros((owners, targets), jnp.float32))
            sent[kr][lines:] = jnp.concatenate(pieces).astype(jnp.bfloat16)
        for copy in stores:
            copy.wait()

    hbm = pl.BlockSpec(memory_space=pltpu.HBM)
    vmem = pl.BlockSpec(memory_space=pltpu.VMEM)
    return pl.pallas_call(
        body,
        out_shape=[jax.ShapeDtypeStruct((lines + 4 * owners, targets), known.dtype)] * rows
        + [jax.ShapeDtypeStruct((targets, width), panel.dtype)] * rows,
        in_specs=[hbm, hbm, vmem],
        out_specs=[vmem] * rows + [hbm] * rows,
        scratch_shapes=[
            pltpu.VMEM((rows, excitations, width), jnp.float32),
            pltpu.VMEM((rows, targets, width), panel.dtype),
            pltpu.VMEM((excitations, targets), jnp.float32),
            pltpu.VMEM((rows, owners, targets), jnp.float32),
            pltpu.SemaphoreType.DMA((3 * rows,)),
        ],
        name="start",
    )(density, panel, known)


def collect_call(shape, lines, known, other):
    rows, cols, vols = shape[:3]
    targets = known[0].shape[1]
    owners = cols * vols
    height = 4 * owners

    def body(*refs):
        ins, outs = refs[:2 * rows], refs[2 * rows:]
        for k in range(rows):
            own, mate = (ins[k + side * rows][...].astype(jnp.float32) for side in range(2))
            total = jnp.zeros((vols, targets), jnp.float32)
            for p in (2, 1, 0):
                total += own[p * owners:p * owners + vols] + mate[p * owners + vols:(p + 1) * owners]
            for v in range(vols):
                outs[v][k:k + 1] = total[v:v + 1]

    block = pl.BlockSpec((height, targets), lambda i: (lines // height, 0))
    whole = pl.BlockSpec((rows, targets), lambda i: (0, 0))
    return pl.pallas_call(
        body,
        grid=(1,),
        out_shape=[jax.ShapeDtypeStruct((rows, targets), jnp.float32)] * vols,
        in_specs=[block] * (2 * rows),
        out_specs=[whole] * vols,
        compiler_params=pltpu.CompilerParams(vmem_limit_bytes=SLAB_BYTES),
        name="collect",
    )(*known, *other)


def prepare_call(shape, values, known, other):
    rows, cols, vols, bx, by, bz = shape
    blocks = cols * vols
    height = bx * blocks * by
    lines = bx * by
    targets = known[0].shape[-1]

    def body(values_ref, *refs):
        known_refs, other_refs = refs[:rows], refs[rows:2 * rows]
        inverse_ref, hit_ref, lane_ref = refs[2 * rows:]
        r0, c0, v0 = (lax.axis_index(a) for a in ALL)
        inverses = [
            1.0 / (MASS_TERM + 6.0 * jnp.full((by, bz), values_ref[i], jnp.float32))
            for i in range(values_ref.shape[0])
        ]
        row_ids = lax.broadcasted_iota(jnp.int32, (height, targets), 0)
        lane_ids = lax.broadcasted_iota(jnp.int32, (bz, targets), 0)
        for k in range(rows):
            spot = known_refs[k][vols * lines:vols * lines + SPOT_ROWS].astype(jnp.float32)
            spot = spot.astype(jnp.int32)
            line = spot[0:1] * (blocks * by) + spot[1:2]
            hit_ref[k ^ r0] = (row_ids == line).astype(jnp.bfloat16)
            lane_ref[k ^ r0] = (lane_ids == spot[2:3]).astype(jnp.bfloat16)
        for k in range(rows):
            for kc, refs_of in enumerate((known_refs, other_refs)):
                start = pl.multiple_of((kc ^ c0) * by, by)

                def plane(kv, carry, source=refs_of[k], start=start, k=k):
                    kind = source[pl.ds(pl.multiple_of(kv * lines, lines), lines)].astype(jnp.float32)
                    kind = kind.astype(jnp.int32).reshape(bx, by, bz)
                    choices, bit = [value[None] for value in inverses], 1
                    while len(choices) > 1:
                        odd = (kind & bit) != 0
                        merged = [jnp.where(odd, two, one)
                                  for one, two in zip(choices[0::2], choices[1::2])]
                        choices, bit = merged + choices[len(merged) * 2:], bit * 2
                    inverse = jnp.broadcast_to(choices[0], (bx, by, bz))
                    place = (pl.ds((k ^ r0) * bx, bx), kv ^ v0, pl.ds(start, by))
                    inverse_ref[place] = inverse
                    return carry

                lax.fori_loop(0, vols, plane, 0)

    vmem = pl.BlockSpec(memory_space=pltpu.VMEM)
    return pl.pallas_call(
        body,
        out_shape=[
            pltpu.HBM((rows * bx, vols, cols * by, bz), jnp.float32),
            pltpu.HBM((rows, height, targets), jnp.bfloat16),
            pltpu.HBM((rows, bz, targets), jnp.bfloat16),
        ],
        in_specs=[pl.BlockSpec(memory_space=pltpu.SMEM)] + [vmem] * (2 * rows),
        out_specs=[vmem] * 3,
        compiler_params=pltpu.CompilerParams(vmem_limit_bytes=SLAB_BYTES),
        name="prepare",
    )(values, *known, *other)


def landed_call(volume):
    pieces = 4
    few = volume.shape[0] // pieces

    def body(in_ref, out_ref, held_ref, sems):
        loads, stores = [], []
        for i in range(pieces):
            span = pl.ds(i * few, few)
            loads.append(pltpu.make_async_copy(in_ref.at[span], held_ref.at[span], sems.at[i]))
            stores.append(pltpu.make_async_copy(held_ref.at[span], out_ref.at[span], sems.at[pieces + i]))
            loads[i].start()
        for load, store in zip(loads, stores):
            load.wait()
            store.start()
        for store in stores:
            store.wait()

    hbm = pl.BlockSpec(memory_space=pltpu.HBM)
    return pl.pallas_call(
        body,
        out_shape=jax.ShapeDtypeStruct(volume.shape, volume.dtype),
        in_specs=[hbm],
        out_specs=hbm,
        scratch_shapes=[
            pltpu.VMEM(volume.shape, volume.dtype), pltpu.SemaphoreType.DMA((2 * pieces,))
        ],
        name="landed",
    )(volume)


def parts_of(value, count):
    pieces = []
    for _ in range(count):
        piece = value.astype(jnp.bfloat16)
        pieces.append(piece)
        value = value - piece.astype(jnp.float32)
    return pieces


def slab_call(shape, first, source, inverse, hit, lane, parts, start=None):
    rows, cols, vols, bx, by, bz = shape
    blocks = cols * vols
    targets = lane.shape[-1]
    height = bx * blocks * by
    depth = rows * bx
    planes = (depth, vols, cols * by, bz)
    padded = (depth + 2, vols, cols * by, bz)
    factors = relax_factors(SWEEPS)

    def body(source_ref, inverse_ref, hit_ref, lane_ref, *rest):
        if first:
            *part_refs, out_ref, flux_ref, other_ref, scaled_ref, ratio_ref = rest
        else:
            parts_ref, start_ref, far_ref, flux_ref, out_ref, *rest = rest
            other_ref, scaled_ref, ratio_ref, volume_ref, sem = rest
        sub = lax.broadcasted_iota(jnp.int32, (by, bz), 0)
        lan = lax.broadcasted_iota(jnp.int32, (by, bz), 1)
        for ref in (out_ref, other_ref):
            ref[0] = jnp.zeros(planes[1:], jnp.float32)
            ref[depth + 1] = jnp.zeros(planes[1:], jnp.float32)
        here = other_ref if first else start_ref
        potentials = []
        for r in range(rows):
            if first:
                place = pl.ds(r ^ lax.axis_index("row"), 1)
                potential = sum(part[place, :] for part in part_refs)
            else:
                potential = sum(
                    jnp.sum(parts_ref[r ^ mate, :, k, :], axis=0, keepdims=True)
                    for k, mate in enumerate(MATES)
                )
            potentials.append(potential)
            weights = [
                lane_ref[r] * piece.astype(jnp.bfloat16) for piece in parts_of(potential, 3)
            ]
            added = lax.dot_general(
                hit_ref[r], jnp.concatenate(weights, axis=0), (((1,), (1,)), ((), ())),
                preferred_element_type=jnp.float32,
            )
            added = added[:, :bz] + added[:, bz:2 * bz] + added[:, 2 * bz:]
            added = added.reshape(bx, vols, cols, by, bz)
            for j in range(blocks):
                c, v = j // vols, j % vols
                span = (slice(r * bx, (r + 1) * bx), v, slice(c * by, (c + 1) * by))
                scaled = source_ref[r, j] + added[:, v, c]
                inverse = inverse_ref[span]
                scaled = scaled * inverse
                ratio_ref[span] = (1.0 - MASS_TERM * inverse) * (1.0 / 6.0)
                scaled_ref[span] = scaled
                if first:
                    here[1 + r * bx:1 + (r + 1) * bx, v, c * by:(c + 1) * by] = factors[0] * scaled

        sweeps = factors[1:] if first else factors
        for order, factor in enumerate(sweeps):
            last = order + 1 == len(sweeps)
            there = out_ref if (len(sweeps) - order) % 2 == 1 else other_ref

            def step(index, carry, here=here, there=there, last=last, factor=factor):
                for x in (index,):
                    tile = [here[x + 1, j % vols, (j // vols) * by:(j // vols + 1) * by]
                            for j in range(blocks)]
                    up = [pltpu.roll(t, 1, 1) for t in tile]
                    down = [pltpu.roll(t, bz - 1, 1) for t in tile]
                    for j in range(blocks):
                        c, v = j // vols, j % vols
                        own = slice(c * by, (c + 1) * by)
                        around = here[x, v, own] + here[x + 2, v, own]
                        if c > 0:
                            around += here[x + 1, v, c * by - 1:(c + 1) * by - 1]
                        else:
                            around += jnp.where(sub == 0, 0.0, pltpu.roll(tile[j], 1, 0))
                        if c < cols - 1:
                            around += here[x + 1, v, c * by + 1:(c + 1) * by + 1]
                        else:
                            around += jnp.where(sub == by - 1, 0.0, pltpu.roll(tile[j], by - 1, 0))
                        around += jnp.where(lan == 0, up[j - 1] if v > 0 else 0.0, up[j])
                        around += jnp.where(
                            lan == bz - 1, down[j + 1] if v < vols - 1 else 0.0, down[j]
                        )
                        value = (1.0 - factor) * tile[j] + factor * (
                            scaled_ref[x, v, own] + ratio_ref[x, v, own] * around
                        )
                        there[x + 1, v, own] = value
                        if last and not first:
                            volume_ref[x // bx, j, x % bx] = value
                return carry

            for index in range(depth):
                step(index, 0)
            here = there

        if not first:
            store = pltpu.make_async_copy(volume_ref, far_ref, sem)
            store.start()
        for r in range(rows):
            part = here[1 + r * bx:1 + (r + 1) * bx].reshape(height, bz)
            met = sum(
                jnp.dot(piece, lane_ref[r], preferred_element_type=jnp.float32)
                for piece in parts_of(part, 2)
            )
            value = jnp.sum(met * hit_ref[r].astype(jnp.float32), axis=0, keepdims=True)
            value = value - potentials[r]
            for k, mate in enumerate(MATES):
                flux_ref[r ^ mate, :, k, :] = jnp.broadcast_to(value, (blocks, targets))
        if not first:
            store.wait()

    vmem = pl.BlockSpec(memory_space=pltpu.VMEM)
    operands = [source, inverse, hit, lane] + (list(parts) if first else [parts, start])
    fluxes = jax.ShapeDtypeStruct((rows, blocks, len(MATES), targets), jnp.float32)
    field = padded if first else (rows, blocks, bx, by, bz)
    field = jax.ShapeDtypeStruct(field, jnp.float32)
    scratch = [pltpu.VMEM(padded, jnp.float32)] + [pltpu.VMEM(planes, jnp.float32)] * 2
    if not first:
        scratch = [pltpu.VMEM(padded, jnp.float32)] + scratch
        scratch += [pltpu.VMEM(field.shape, jnp.float32), pltpu.SemaphoreType.DMA(())]
    return pl.pallas_call(
        body,
        out_shape=[field if first else pltpu.HBM(field.shape, field.dtype), fluxes],
        in_specs=[vmem] * len(operands),
        out_specs=[vmem if first else pl.BlockSpec(memory_space=pltpu.HBM), vmem],
        scratch_shapes=scratch,
        compiler_params=None if first else pltpu.CompilerParams(vmem_limit_bytes=SLAB_BYTES),
        name="slab_first" if first else "slab_last",
    )(*operands)


def update_call(flux, panels, part, parts, keep):
    excitations, width = flux.shape[0], panels[0].shape[1] // parts
    span = slice(part * width, (part + 1) * width)
    far = jax.ShapeDtypeStruct((panels[3].shape[0], width), panels[3].dtype)

    def body(flux_ref, a_own, a_mate, b_own, b_far, a_ref, b_ref, b_mate, sem):
        load = pltpu.make_async_copy(b_far.at[:, span], b_mate, sem)
        load.start()
        fluxes = [flux_ref[:, k, :].astype(jnp.bfloat16) for k in range(len(MATES))]
        value = jnp.dot(fluxes[0], a_own[:, span], preferred_element_type=jnp.float32)
        value += jnp.dot(fluxes[1], a_mate[:, span], preferred_element_type=jnp.float32)
        a_ref[...] = value.astype(jnp.bfloat16)
        value = jnp.dot(fluxes[0], b_own[:, span], preferred_element_type=jnp.float32)
        load.wait()
        value += jnp.dot(fluxes[2], b_mate[...], preferred_element_type=jnp.float32)
        b_ref[...] = value.astype(jnp.bfloat16)

    vmem = pl.BlockSpec(memory_space=pltpu.VMEM)
    return pl.pallas_call(
        body,
        out_shape=[jax.ShapeDtypeStruct((excitations, width), jnp.bfloat16)] * 2 + ([far] if keep else []),
        in_specs=[vmem] * 4 + [pl.BlockSpec(memory_space=pltpu.HBM)],
        out_specs=[vmem] * (3 if keep else 2),
        scratch_shapes=([] if keep else [pltpu.VMEM(far.shape, far.dtype)]) + [pltpu.SemaphoreType.DMA(())],
        compiler_params=pltpu.CompilerParams(vmem_limit_bytes=VMEM_BYTES),
        name="update",
    )(flux, *panels)


def potential_call(densities, halves, mates, panels, part, before):
    excitations = densities[0].shape[0]
    targets, width = panels[0].shape[0], panels[0].shape[1] // PARTS
    span = slice(part * width, (part + 1) * width)

    def body(a_density, b_density, a_half, b_half, a_other, b_other,
             a_own, a_mate, b_own, b_mate, *rest):
        out_ref = rest[-1]
        rounded = [
            (density[:, span] + RELAXATION * (half[...].astype(jnp.float32)
                                              + other[...].astype(jnp.float32))).astype(jnp.bfloat16)
            for density, half, other in (
                (a_density, a_half, a_other), (b_density, b_half, b_other))
        ]

        def met(value, panel):
            return lax.dot_general(
                panel, value, (((1,), (1,)), ((), ())), preferred_element_type=jnp.float32
            )

        def put(k, value):
            value = value.T
            out_ref[:, k, :] = value + rest[0][:, k, :] if before is not None else value

        put(0, met(rounded[0], a_own[:, span]) + met(rounded[1], b_own[:, span]))
        put(1, met(rounded[0], a_mate[:, span]))
        put(2, met(rounded[1], b_mate[...]))

    vmem = pl.BlockSpec(memory_space=pltpu.VMEM)
    operands = [*densities, *halves, *mates, *panels] + ([] if before is None else [before])
    return pl.pallas_call(
        body,
        out_shape=jax.ShapeDtypeStruct((excitations, len(MATES), targets), jnp.float32),
        in_specs=[vmem] * len(operands),
        out_specs=vmem,
        compiler_params=pltpu.CompilerParams(vmem_limit_bytes=VMEM_BYTES),
        name="potential",
    )(*operands)


def totals_call(firsts, ends):
    groups = len(ends)
    width = firsts[0][0][0].shape[1]

    def body(*refs):
        outs, rest = refs[-groups:], list(refs[:-groups])
        first_refs = [[[rest.pop(0) for _ in pair] for pair in parts] for parts in firsts]
        end_refs = [[rest.pop(0) for _ in pair] for pair in ends]
        for group in range(groups):
            for part, (a, b) in enumerate(first_refs[group]):
                span = slice(part * width, (part + 1) * width)
                pieces = [a[...], b[...]] + [ref[:, span] for ref in end_refs[group]]
                a, b, c, d = (piece.astype(jnp.float32) for piece in pieces)
                outs[group][:, span] = (RELAXATION * ((a + b) + (c + d))).astype(jnp.bfloat16)

    vmem = pl.BlockSpec(memory_space=pltpu.VMEM)
    operands = [value for parts in firsts for pair in parts for value in pair]
    operands += [value for pair in ends for value in pair]
    return pl.pallas_call(
        body,
        out_shape=[jax.ShapeDtypeStruct(pair[0].shape, jnp.bfloat16) for pair in ends],
        in_specs=[vmem] * len(operands),
        out_specs=[vmem] * groups,
        compiler_params=pltpu.CompilerParams(vmem_limit_bytes=VMEM_BYTES),
        name="totals",
    )(*operands)


def trace_spots(trace_count, trace_cell, targets, shape):
    _, cols, vols, _, by, bz = shape
    counts = trace_count[0]
    offsets = jnp.cumsum(counts) - counts
    slot_ids = jnp.arange(trace_cell.shape[2], dtype=jnp.int32)
    live = slot_ids[None, :] < counts[:, None]
    owner = jnp.where(live, offsets[:, None] + slot_ids[None, :], -1)
    cell = trace_cell[0]
    block_ids = jnp.arange(cols * vols, dtype=jnp.int32)[:, None]
    line = (block_ids % vols) * (cols * by) + (block_ids // vols) * by + (cell // bz) % by
    code = ((cell // (by * bz)) * (cols * vols * by) + line) * bz + cell % bz
    match = owner[:, :, None] == jnp.arange(targets, dtype=jnp.int32)
    code = jnp.sum(jnp.where(match, code[:, :, None], 0), axis=(0, 1))
    line = code // bz
    span = cols * vols * by
    return jnp.stack([line // span, line % span, code % bz])


def split_by_excitation(panel, density, source, class_index, class_values, trace_count, trace_cell):
    rows, cols, vols = (lax.axis_size(a) for a in ALL)
    blocks = cols * vols
    excitations, bx, by, bz = source.shape
    targets, nodes = panel.shape
    width = nodes // rows
    here = lax.axis_index("row")
    low, high = here & 1, here >> 1
    shape = (rows, cols, vols, bx, by, bz)

    def columns(array, place):
        return lax.dynamic_slice_in_dim(array, place * width, width, 1)

    def around_axis(pieces, axis):
        return [pieces[0]] + [mated(piece, axis, k) for k, piece in enumerate(pieces) if k > 0]

    kinds = class_index.reshape(bx * by, bz).astype(jnp.bfloat16)
    kinds = around_axis([kinds] * vols, "vol")
    slab = lax.all_to_all(source, ALL, 0, 0, tiled=True)
    slab = slab.reshape(rows, blocks, bx, by, bz)
    spots = trace_spots(trace_count, trace_cell, targets, shape).astype(jnp.bfloat16)
    spots = jnp.pad(spots, ((0, SPOT_ROWS - spots.shape[0]), (0, 0)))
    known = jnp.concatenate(kinds + [spots])
    made = start_call(density, panel, known, shape)
    lines, quarters = known.shape[0], made[rows:]
    known = around_axis(made[:rows], "row")
    other = [mated(piece, "col", 1) for piece in known]
    parts = list(collect_call(shape, lines, known, other))
    for k in range(1, vols):
        parts[k] = mated(parts[k], "vol", k)

    panels = [quarters[0], None, quarters[2], None]
    panels[1] = mated(quarters[1], "row", 1)
    panels[3] = mated(quarters[3], "row", 2)
    densities = [columns(density, low), columns(density, 2 + high)]

    inverse, hit, lane = prepare_call(shape, class_values, known, other)
    volume, flux = slab_call(shape, True, slab, inverse, hit, lane, parts)
    flux = flux.reshape(excitations, len(MATES), targets)
    flux = lax.all_to_all(flux, ALL, 0, 0, tiled=True)
    halves, mates, fars, parts = [], [], [], None
    for part in range(PARTS):
        *pair, far = update_call(flux, panels, part, PARTS, True)
        halves.append(pair)
        fars.append(far)
        mates.append([mated(halves[part][0], "row", 2), mated(halves[part][1], "row", 1)])
    for part in range(PARTS):
        parts = potential_call(
            densities, halves[part], mates[part], [*panels[:3], fars[part]], part, parts
        )
    parts = lax.all_to_all(parts, ALL, 0, 0, tiled=True)
    parts = parts.reshape(rows, blocks, len(MATES), targets)
    volume, flux = slab_call(shape, False, slab, inverse, hit, lane, parts, volume)
    flux = flux.reshape(excitations, len(MATES), targets)
    flux = lax.all_to_all(flux, ALL, 0, 0, tiled=True)
    volume = volume.reshape(excitations, bx, by, bz)
    volume = lax.all_to_all(volume, ALL, 0, 0, tiled=True)
    volume = landed_call(volume)
    ends = update_call(flux, panels, 0, 1, False)
    end_mates = [mated(ends[0], "row", 2), mated(ends[1], "row", 1)]
    totals = totals_call(
        [[(halves[part][g], mates[part][g]) for part in range(PARTS)] for g in range(2)],
        list(zip(ends, end_mates)),
    )
    moved = [mated(totals[0], "row", 1), mated(totals[1], "row", 2)]
    change = [
        jnp.where(low == 0, totals[0], moved[0]), jnp.where(low == 0, moved[0], totals[0]),
        jnp.where(high == 0, totals[1], moved[1]), jnp.where(high == 0, moved[1], totals[1]),
    ]
    density = density + jnp.concatenate(change, axis=1).astype(jnp.float32)
    return (density, volume)


def padded_2(value, sides, width):
    for axis, dim in sides:
        size, length = (lax.axis_size(axis), value.shape[dim])
        up = [(i, (i + 1) % size) for i in range(size - 1)]
        down = [(j, i) for i, j in up]
        last = lax.slice_in_dim(value, length - width, length, axis=dim)
        first = lax.slice_in_dim(value, 0, width, axis=dim)
        before = lax.ppermute(last, axis, up)
        after = lax.ppermute(first, axis, down)
        value = jnp.concatenate([before, value, after], axis=dim)
    return value


def neighbours(padded):
    center = padded[..., 1:-1, 1:-1, 1:-1]
    beside_all = padded[..., 2:, 1:-1, 1:-1] + padded[..., :-2, 1:-1, 1:-1]
    beside_all = beside_all + padded[..., 1:-1, 2:, 1:-1] + padded[..., 1:-1, :-2, 1:-1]
    beside_all = beside_all + padded[..., 1:-1, 1:-1, 2:] + padded[..., 1:-1, 1:-1, :-2]
    return (center, beside_all)


def split_by_block(panel, density, source, class_index, class_values, trace_count, trace_cell):
    factors = relax_factors(SWEEPS)
    conduct = conduct_of(class_index, class_values)
    diagonal = MASS_TERM + 6.0 * conduct
    counts = trace_count[0]
    block_index = lax.axis_index(("col", "vol"))
    offsets = jnp.cumsum(counts) - counts
    target_rows = panel.shape[0]
    slot_count = trace_cell.shape[2]
    slot_ids = jnp.arange(slot_count, dtype=jnp.int32)
    target_ids = jnp.arange(target_rows, dtype=jnp.int32)
    own_count = lax.dynamic_index_in_dim(counts, block_index, keepdims=False)
    first_target = lax.dynamic_index_in_dim(offsets, block_index, keepdims=False)
    cell_ids = lax.dynamic_index_in_dim(trace_cell[0], block_index, keepdims=False)
    live_slots = slot_ids < own_count
    select = (
        ((first_target + slot_ids)[:, None] == target_ids[None, :]) & live_slots[:, None]
    ).astype(jnp.float32)
    volume = jnp.zeros(source.shape, jnp.float32)
    field_shape = volume.shape
    share_width = density.shape[1] // lax.axis_size("row")
    share_state = lax.dynamic_slice_in_dim(
        density, lax.axis_index("row") * share_width, share_width, 1
    )
    rounded = density.astype(jnp.bfloat16)
    lead = field_shape[0]
    for iteration in range(OUTER):
        partial_value = lax.dot_general(
            rounded, panel, (((1,), (1,)), ((), ())), preferred_element_type=jnp.float32
        )
        potential = lax.psum(partial_value, ("col", "vol"))
        slot_values = jnp.dot(potential, select.T, precision=lax.Precision.HIGHEST)
        right_side = source.reshape(lead, -1).at[:, cell_ids].add(slot_values).reshape(field_shape)
        relax_volume = volume
        for factor in factors:
            padded = padded_2(relax_volume, (("row", 1), ("col", 2), ("vol", 3)), 1)
            center, beside_all = neighbours(padded)
            relax_volume = (
                center + factor * (right_side - diagonal * center + conduct * beside_all) / diagonal
            )
        volume = relax_volume
        mismatch = volume.reshape(lead, -1)[:, cell_ids] - slot_values
        own_fluxes = jnp.dot(mismatch, select, precision=lax.Precision.HIGHEST)
        fluxes = lax.psum(own_fluxes, ("col", "vol"))
        update = jnp.dot(fluxes.astype(jnp.bfloat16), panel, preferred_element_type=jnp.float32)
        share_state = share_state + RELAXATION * lax.psum_scatter(
            update, "row", scatter_dimension=1, tiled=True
        )
        if iteration + 1 < OUTER:
            rounded = lax.all_gather(share_state.astype(jnp.bfloat16), "row", axis=1, tiled=True)
    density = lax.all_gather(share_state, "row", axis=1, tiled=True)
    return (density, volume)


def local(*args):
    sizes = [lax.axis_size(a) for a in ALL]
    if whole_slabs(sizes, args[0].shape[0], args[2].shape):
        return split_by_excitation(*args)
    return split_by_block(*args)


def whole_slabs(sizes, targets, block):
    return math.prod(sizes) == block[0] and sizes == [4, 2, 4] and targets == block[3]


def solution(mesh):
    placed = (
        P("row", ("col", "vol")),
        P(None, ("col", "vol")),
        P(None, "row", "col", "vol"),
        P("row", "col", "vol"),
        P(),
        P("row", None),
        P("row", None, None),
    )
    return jax.shard_map(
        local,
        mesh=mesh,
        in_specs=placed,
        out_specs=(P(None, ("col", "vol")), P(None, "row", "col", "vol")),
        check_vma=False,
    )
```

```python
import math

import jax
import jax.numpy as jnp
from jax import lax
from jax.experimental import pallas as pl
from jax.experimental.pallas import tpu as pltpu
from jax.sharding import PartitionSpec as P


SWEEPS = 4
OUTER = 2


MASS_TERM = 0.1
RELAXATION = 0.5
SPECTRUM_LOW = 0.1
SPECTRUM_HIGH = 2.0

ALL = ("row", "col", "vol")
SPOT_ROWS = 32
PARTS = 2
VMEM_BYTES = 16 * 2 ** 20
SLAB_BYTES = 40 * 2 ** 20


def relax_factors(count):
    middle = (SPECTRUM_HIGH + SPECTRUM_LOW) / 2.0
    spread = (SPECTRUM_HIGH - SPECTRUM_LOW) / 2.0
    return [
        1.0 / (middle + spread * math.cos(math.pi * (2 * order + 1) / (2 * count)))
        for order in range(count)
    ]


def conduct_of(class_index, class_values):
    classes = jnp.arange(class_values.shape[0], dtype=jnp.int32)
    return jnp.sum(
        jnp.where(
            class_index[None] == classes[:, None, None, None],
            class_values[:, None, None, None],
            jnp.float32(0.0),
        ),
        axis=0,
    )


MATES = (0, 1, 2)


def mated(value, axis, mate):
    return lax.ppermute(value, axis, [(i, i ^ mate) for i in range(lax.axis_size(axis))])


def start_call(density, panel, known, shape):
    rows, cols, vols = shape[:3]
    excitations, nodes = density.shape
    targets = panel.shape[0]
    width = nodes // rows
    lines = known.shape[0]
    owners = cols * vols

    def body(density_ref, panel_ref, known_ref, *rest):
        sent, rest = rest[:rows], rest[rows:]
        quarters = rest[:rows]
        nodes_ref, panel_buf, total_ref, picked_ref, sems = rest[rows:]
        r0, c0, v0 = (lax.axis_index(a) for a in ALL)
        low, high = r0 & 1, r0 >> 1
        sources = (low, low ^ 1, 2 + high, 2 + (high ^ 1))
        order = (1, 3, 0, 2)
        loads, stores = [], []
        for q in order:
            span = pl.ds(pl.multiple_of(sources[q] * width, width), width)
            pair = (
                pltpu.make_async_copy(panel_ref.at[:, span], panel_buf.at[q], sems.at[q]),
                pltpu.make_async_copy(density_ref.at[:, span], nodes_ref.at[q], sems.at[rows + q]),
            )
            for copy in pair:
                copy.start()
            loads.append(pair)
        for k in range(rows):
            sent[k][0:lines] = known_ref[...]
        total = jnp.zeros((targets, excitations), jnp.float32)
        for q, pair in zip(order, loads):
            for copy in pair:
                copy.wait()
            store = pltpu.make_async_copy(panel_buf.at[q], quarters[q], sems.at[2 * rows + q])
            store.start()
            stores.append(store)
            total += lax.dot_general(
                panel_buf[q], nodes_ref[q].astype(jnp.bfloat16), (((1,), (1,)), ((), ())),
                preferred_element_type=jnp.float32,
            )
        total_ref[...] = total.T
        for kr in range(rows):
            for kc in range(cols):
                for kv in range(vols):
                    owner = ((r0 ^ kr) * cols + (c0 ^ kc)) * vols + (v0 ^ kv)
                    place = kc * vols + kv
                    picked_ref[kr, place:place + 1] = total_ref[pl.ds(owner, 1)]
            pieces = [piece.astype(jnp.float32) for piece in parts_of(picked_ref[kr], 3)]
            pieces.append(jnp.zeros((owners, targets), jnp.float32))
            sent[kr][lines:] = jnp.concatenate(pieces).astype(jnp.bfloat16)
        for copy in stores:
            copy.wait()

    hbm = pl.BlockSpec(memory_space=pltpu.HBM)
    vmem = pl.BlockSpec(memory_space=pltpu.VMEM)
    return pl.pallas_call(
        body,
        out_shape=[pltpu.VMEM((lines + 4 * owners, targets), known.dtype)]
        + [jax.ShapeDtypeStruct((lines + 4 * owners, targets), known.dtype)] * (rows - 1)
        + [jax.ShapeDtypeStruct((targets, width), panel.dtype)] * rows,
        in_specs=[hbm, hbm, vmem],
        out_specs=[vmem] * rows + [hbm] * rows,
        scratch_shapes=[
            pltpu.VMEM((rows, excitations, width), jnp.float32),
            pltpu.VMEM((rows, targets, width), panel.dtype),
            pltpu.VMEM((excitations, targets), jnp.float32),
            pltpu.VMEM((rows, owners, targets), jnp.float32),
            pltpu.SemaphoreType.DMA((3 * rows,)),
        ],
        name="start",
    )(density, panel, known)


def collect_call(shape, lines, known, other):
    rows, cols, vols = shape[:3]
    targets = known[0].shape[1]
    owners = cols * vols
    height = 4 * owners

    def body(*refs):
        ins, outs = refs[:2 * rows], refs[2 * rows:]
        for k in range(rows):
            own, mate = (ins[k + side * rows][...].astype(jnp.float32) for side in range(2))
            total = jnp.zeros((vols, targets), jnp.float32)
            for p in (2, 1, 0):
                total += own[p * owners:p * owners + vols] + mate[p * owners + vols:(p + 1) * owners]
            for v in range(vols):
                outs[v][k:k + 1] = total[v:v + 1]

    block = pl.BlockSpec((height, targets), lambda i: (lines // height, 0))
    whole = pl.BlockSpec((rows, targets), lambda i: (0, 0))
    return pl.pallas_call(
        body,
        grid=(1,),
        out_shape=[jax.ShapeDtypeStruct((rows, targets), jnp.float32)] * vols,
        in_specs=[block] * (2 * rows),
        out_specs=[whole] * vols,
        compiler_params=pltpu.CompilerParams(vmem_limit_bytes=SLAB_BYTES),
        name="collect",
    )(*known, *other)


def prepare_call(shape, values, known, other):
    rows, cols, vols, bx, by, bz = shape
    blocks = cols * vols
    height = bx * blocks * by
    lines = bx * by
    targets = known[0].shape[-1]

    def body(values_ref, *refs):
        known_refs, other_refs = refs[:rows], refs[rows:2 * rows]
        inverse_ref, hit_ref, lane_ref = refs[2 * rows:]
        r0, c0, v0 = (lax.axis_index(a) for a in ALL)
        inverses = [
            1.0 / (MASS_TERM + 6.0 * jnp.full((by, bz), values_ref[i], jnp.float32))
            for i in range(values_ref.shape[0])
        ]
        row_ids = lax.broadcasted_iota(jnp.int32, (height, targets), 0)
        lane_ids = lax.broadcasted_iota(jnp.int32, (bz, targets), 0)
        for k in range(rows):
            spot = known_refs[k][vols * lines:vols * lines + SPOT_ROWS].astype(jnp.float32)
            spot = spot.astype(jnp.int32)
            line = spot[0:1] * (blocks * by) + spot[1:2]
            hit_ref[k ^ r0] = (row_ids == line).astype(jnp.bfloat16)
            lane_ref[k ^ r0] = (lane_ids == spot[2:3]).astype(jnp.bfloat16)
        for k in range(rows):
            for kc, refs_of in enumerate((known_refs, other_refs)):
                start = pl.multiple_of((kc ^ c0) * by, by)

                def plane(kv, carry, source=refs_of[k], start=start, k=k):
                    kind = source[pl.ds(pl.multiple_of(kv * lines, lines), lines)].astype(jnp.float32)
                    kind = kind.astype(jnp.int32).reshape(bx, by, bz)
                    choices, bit = [value[None] for value in inverses], 1
                    while len(choices) > 1:
                        odd = (kind & bit) != 0
                        merged = [jnp.where(odd, two, one)
                                  for one, two in zip(choices[0::2], choices[1::2])]
                        choices, bit = merged + choices[len(merged) * 2:], bit * 2
                    inverse = jnp.broadcast_to(choices[0], (bx, by, bz))
                    place = (pl.ds((k ^ r0) * bx, bx), kv ^ v0, pl.ds(start, by))
                    inverse_ref[place] = inverse
                    return carry

                lax.fori_loop(0, vols, plane, 0)

    vmem = pl.BlockSpec(memory_space=pltpu.VMEM)
    return pl.pallas_call(
        body,
        out_shape=[
            pltpu.HBM((rows * bx, vols, cols * by, bz), jnp.float32),
            pltpu.HBM((rows, height, targets), jnp.bfloat16),
            pltpu.HBM((rows, bz, targets), jnp.bfloat16),
        ],
        in_specs=[pl.BlockSpec(memory_space=pltpu.SMEM)] + [vmem] * (2 * rows),
        out_specs=[vmem] * 3,
        compiler_params=pltpu.CompilerParams(vmem_limit_bytes=SLAB_BYTES),
        name="prepare",
    )(values, *known, *other)


def landed_call(volume):
    pieces = 4
    few = volume.shape[0] // pieces

    def body(in_ref, out_ref, held_ref, sems):
        loads, stores = [], []
        for i in range(pieces):
            span = pl.ds(i * few, few)
            loads.append(pltpu.make_async_copy(in_ref.at[span], held_ref.at[span], sems.at[i]))
            stores.append(pltpu.make_async_copy(held_ref.at[span], out_ref.at[span], sems.at[pieces + i]))
            loads[i].start()
        for load, store in zip(loads, stores):
            load.wait()
            store.start()
        for store in stores:
            store.wait()

    hbm = pl.BlockSpec(memory_space=pltpu.HBM)
    return pl.pallas_call(
        body,
        out_shape=jax.ShapeDtypeStruct(volume.shape, volume.dtype),
        in_specs=[hbm],
        out_specs=hbm,
        scratch_shapes=[
            pltpu.VMEM(volume.shape, volume.dtype), pltpu.SemaphoreType.DMA((2 * pieces,))
        ],
        name="landed",
    )(volume)


def parts_of(value, count):
    pieces = []
    for _ in range(count):
        piece = value.astype(jnp.bfloat16)
        pieces.append(piece)
        value = value - piece.astype(jnp.float32)
    return pieces


def slab_call(shape, first, source, inverse, hit, lane, parts, start=None):
    rows, cols, vols, bx, by, bz = shape
    blocks = cols * vols
    targets = lane.shape[-1]
    height = bx * blocks * by
    depth = rows * bx
    planes = (depth, vols, cols * by, bz)
    padded = (depth + 2, vols, cols * by, bz)
    factors = relax_factors(SWEEPS)

    def body(source_ref, inverse_ref, hit_ref, lane_ref, *rest):
        if first:
            *part_refs, out_ref, flux_ref, other_ref, scaled_ref, ratio_ref = rest
        else:
            parts_ref, start_ref, far_ref, flux_ref, out_ref, *rest = rest
            other_ref, scaled_ref, ratio_ref, volume_ref, sem = rest
        stores = []
        sub = lax.broadcasted_iota(jnp.int32, (by, bz), 0)
        lan = lax.broadcasted_iota(jnp.int32, (by, bz), 1)
        for ref in (out_ref, other_ref):
            ref[0] = jnp.zeros(planes[1:], jnp.float32)
            ref[depth + 1] = jnp.zeros(planes[1:], jnp.float32)
        here = other_ref if first else start_ref
        potentials = []
        for r in range(rows):
            if first:
                place = pl.ds(r ^ lax.axis_index("row"), 1)
                potential = sum(part[place, :] for part in part_refs)
            else:
                potential = sum(
                    jnp.sum(parts_ref[r ^ mate, :, k, :], axis=0, keepdims=True)
                    for k, mate in enumerate(MATES)
                )
            potentials.append(potential)
            weights = [
                lane_ref[r] * piece.astype(jnp.bfloat16) for piece in parts_of(potential, 3)
            ]
            added = lax.dot_general(
                hit_ref[r], jnp.concatenate(weights, axis=0), (((1,), (1,)), ((), ())),
                preferred_element_type=jnp.float32,
            )
            added = added[:, :bz] + added[:, bz:2 * bz] + added[:, 2 * bz:]
            added = added.reshape(bx, vols, cols, by, bz)
            for j in range(blocks):
                c, v = j // vols, j % vols
                span = (slice(r * bx, (r + 1) * bx), v, slice(c * by, (c + 1) * by))
                scaled = source_ref[r, j] + added[:, v, c]
                inverse = inverse_ref[span]
                scaled = scaled * inverse
                ratio_ref[span] = (1.0 - MASS_TERM * inverse) * (1.0 / 6.0)
                scaled_ref[span] = scaled
                if first:
                    here[1 + r * bx:1 + (r + 1) * bx, v, c * by:(c + 1) * by] = factors[0] * scaled

        sweeps = factors[1:] if first else factors
        for order, factor in enumerate(sweeps):
            last = order + 1 == len(sweeps)
            there = out_ref if (len(sweeps) - order) % 2 == 1 else other_ref

            def step(index, carry, here=here, there=there, last=last, factor=factor):
                for x in (index,):
                    tile = [here[x + 1, j % vols, (j // vols) * by:(j // vols + 1) * by]
                            for j in range(blocks)]
                    up = [pltpu.roll(t, 1, 1) for t in tile]
                    down = [pltpu.roll(t, bz - 1, 1) for t in tile]
                    for j in range(blocks):
                        c, v = j // vols, j % vols
                        own = slice(c * by, (c + 1) * by)
                        around = here[x, v, own] + here[x + 2, v, own]
                        if c > 0:
                            around += here[x + 1, v, c * by - 1:(c + 1) * by - 1]
                        else:
                            around += jnp.where(sub == 0, 0.0, pltpu.roll(tile[j], 1, 0))
                        if c < cols - 1:
                            around += here[x + 1, v, c * by + 1:(c + 1) * by + 1]
                        else:
                            around += jnp.where(sub == by - 1, 0.0, pltpu.roll(tile[j], by - 1, 0))
                        around += jnp.where(lan == 0, up[j - 1] if v > 0 else 0.0, up[j])
                        around += jnp.where(
                            lan == bz - 1, down[j + 1] if v < vols - 1 else 0.0, down[j]
                        )
                        value = (1.0 - factor) * tile[j] + factor * (
                            scaled_ref[x, v, own] + ratio_ref[x, v, own] * around
                        )
                        there[x + 1, v, own] = value
                        if last and not first:
                            volume_ref[x // bx, j, x % bx] = value
                    if last and not first and x % bx == bx - 1:
                        tile_at = x // bx
                        stores.append(pltpu.make_async_copy(
                            volume_ref.at[tile_at], far_ref.at[tile_at], sem.at[tile_at]
                        ))
                        stores[-1].start()
                return carry

            for index in range(depth):
                step(index, 0)
            here = there

        for r in range(rows):
            part = here[1 + r * bx:1 + (r + 1) * bx].reshape(height, bz)
            met = sum(
                jnp.dot(piece, lane_ref[r], preferred_element_type=jnp.float32)
                for piece in parts_of(part, 2)
            )
            value = jnp.sum(met * hit_ref[r].astype(jnp.float32), axis=0, keepdims=True)
            value = value - potentials[r]
            for k, mate in enumerate(MATES):
                flux_ref[r ^ mate, :, k, :] = jnp.broadcast_to(value, (blocks, targets))
        for store in stores:
            store.wait()

    vmem = pl.BlockSpec(memory_space=pltpu.VMEM)
    operands = [source, inverse, hit, lane] + (list(parts) if first else [parts, start])
    fluxes = jax.ShapeDtypeStruct((rows, blocks, len(MATES), targets), jnp.float32)
    field = padded if first else (rows, blocks, bx, by, bz)
    field = jax.ShapeDtypeStruct(field, jnp.float32)
    scratch = [pltpu.VMEM(padded, jnp.float32)] + [pltpu.VMEM(planes, jnp.float32)] * 2
    if not first:
        scratch = [pltpu.VMEM(padded, jnp.float32)] + scratch
        scratch += [pltpu.VMEM(field.shape, jnp.float32), pltpu.SemaphoreType.DMA((rows,))]
    return pl.pallas_call(
        body,
        out_shape=[field if first else pltpu.HBM(field.shape, field.dtype), fluxes],
        in_specs=[vmem] * len(operands),
        out_specs=[vmem if first else pl.BlockSpec(memory_space=pltpu.HBM), vmem],
        scratch_shapes=scratch,
        compiler_params=None if first else pltpu.CompilerParams(vmem_limit_bytes=SLAB_BYTES),
        name="slab_first" if first else "slab_last",
    )(*operands)


def update_call(flux, panels, part, parts, keep):
    excitations, width = flux.shape[0], panels[0].shape[1] // parts
    span = slice(part * width, (part + 1) * width)
    far = jax.ShapeDtypeStruct((panels[3].shape[0], width), panels[3].dtype)

    def body(flux_ref, a_own, a_mate, b_own, b_far, a_ref, b_ref, b_mate, sem):
        load = pltpu.make_async_copy(b_far.at[:, span], b_mate, sem)
        load.start()
        fluxes = [flux_ref[:, k, :].astype(jnp.bfloat16) for k in range(len(MATES))]
        value = jnp.dot(fluxes[0], a_own[:, span], preferred_element_type=jnp.float32)
        value += jnp.dot(fluxes[1], a_mate[:, span], preferred_element_type=jnp.float32)
        a_ref[...] = value.astype(jnp.bfloat16)
        value = jnp.dot(fluxes[0], b_own[:, span], preferred_element_type=jnp.float32)
        load.wait()
        value += jnp.dot(fluxes[2], b_mate[...], preferred_element_type=jnp.float32)
        b_ref[...] = value.astype(jnp.bfloat16)

    vmem = pl.BlockSpec(memory_space=pltpu.VMEM)
    return pl.pallas_call(
        body,
        out_shape=[jax.ShapeDtypeStruct((excitations, width), jnp.bfloat16)] * 2 + ([far] if keep else []),
        in_specs=[vmem] * 4 + [pl.BlockSpec(memory_space=pltpu.HBM)],
        out_specs=[vmem] * (3 if keep else 2),
        scratch_shapes=([] if keep else [pltpu.VMEM(far.shape, far.dtype)]) + [pltpu.SemaphoreType.DMA(())],
        compiler_params=pltpu.CompilerParams(vmem_limit_bytes=VMEM_BYTES),
        name="update",
    )(flux, *panels)


def potential_call(densities, halves, mates, panels, part, before):
    excitations = densities[0].shape[0]
    targets, width = panels[0].shape[0], panels[0].shape[1] // PARTS
    span = slice(part * width, (part + 1) * width)

    def body(a_density, b_density, a_half, b_half, a_other, b_other,
             a_own, a_mate, b_own, b_mate, *rest):
        out_ref = rest[-1]
        rounded = [
            (density[:, span] + RELAXATION * (half[...].astype(jnp.float32)
                                              + other[...].astype(jnp.float32))).astype(jnp.bfloat16)
            for density, half, other in (
                (a_density, a_half, a_other), (b_density, b_half, b_other))
        ]

        def met(value, panel):
            return lax.dot_general(
                panel, value, (((1,), (1,)), ((), ())), preferred_element_type=jnp.float32
            )

        def put(k, value):
            value = value.T
            out_ref[:, k, :] = value + rest[0][:, k, :] if before is not None else value

        put(0, met(rounded[0], a_own[:, span]) + met(rounded[1], b_own[:, span]))
        put(1, met(rounded[0], a_mate[:, span]))
        put(2, met(rounded[1], b_mate[...]))

    vmem = pl.BlockSpec(memory_space=pltpu.VMEM)
    operands = [*densities, *halves, *mates, *panels] + ([] if before is None else [before])
    return pl.pallas_call(
        body,
        out_shape=jax.ShapeDtypeStruct((excitations, len(MATES), targets), jnp.float32),
        in_specs=[vmem] * len(operands),
        out_specs=vmem,
        compiler_params=pltpu.CompilerParams(vmem_limit_bytes=VMEM_BYTES),
        name="potential",
    )(*operands)


def totals_call(firsts, ends):
    groups = len(ends)
    width = firsts[0][0][0].shape[1]

    def body(*refs):
        outs, rest = refs[-groups:], list(refs[:-groups])
        first_refs = [[[rest.pop(0) for _ in pair] for pair in parts] for parts in firsts]
        end_refs = [[rest.pop(0) for _ in pair] for pair in ends]
        for group in range(groups):
            for part, (a, b) in enumerate(first_refs[group]):
                span = slice(part * width, (part + 1) * width)
                pieces = [a[...], b[...]] + [ref[:, span] for ref in end_refs[group]]
                a, b, c, d = (piece.astype(jnp.float32) for piece in pieces)
                outs[group][:, span] = (RELAXATION * ((a + b) + (c + d))).astype(jnp.bfloat16)

    vmem = pl.BlockSpec(memory_space=pltpu.VMEM)
    operands = [value for parts in firsts for pair in parts for value in pair]
    operands += [value for pair in ends for value in pair]
    return pl.pallas_call(
        body,
        out_shape=[jax.ShapeDtypeStruct(pair[0].shape, jnp.bfloat16) for pair in ends],
        in_specs=[vmem] * len(operands),
        out_specs=[vmem] * groups,
        compiler_params=pltpu.CompilerParams(vmem_limit_bytes=VMEM_BYTES),
        name="totals",
    )(*operands)


def trace_spots(trace_count, trace_cell, targets, shape):
    _, cols, vols, _, by, bz = shape
    counts = trace_count[0]
    offsets = jnp.cumsum(counts) - counts
    slot_ids = jnp.arange(trace_cell.shape[2], dtype=jnp.int32)
    live = slot_ids[None, :] < counts[:, None]
    owner = jnp.where(live, offsets[:, None] + slot_ids[None, :], -1)
    cell = trace_cell[0]
    block_ids = jnp.arange(cols * vols, dtype=jnp.int32)[:, None]
    line = (block_ids % vols) * (cols * by) + (block_ids // vols) * by + (cell // bz) % by
    code = ((cell // (by * bz)) * (cols * vols * by) + line) * bz + cell % bz
    match = owner[:, :, None] == jnp.arange(targets, dtype=jnp.int32)
    code = jnp.sum(jnp.where(match, code[:, :, None], 0), axis=(0, 1))
    line = code // bz
    span = cols * vols * by
    return jnp.stack([line // span, line % span, code % bz])


def split_by_excitation(panel, density, source, class_index, class_values, trace_count, trace_cell):
    rows, cols, vols = (lax.axis_size(a) for a in ALL)
    blocks = cols * vols
    excitations, bx, by, bz = source.shape
    targets, nodes = panel.shape
    width = nodes // rows
    here = lax.axis_index("row")
    low, high = here & 1, here >> 1
    shape = (rows, cols, vols, bx, by, bz)

    def columns(array, place):
        return lax.dynamic_slice_in_dim(array, place * width, width, 1)

    def around_axis(pieces, axis):
        return [pieces[0]] + [mated(piece, axis, k) for k, piece in enumerate(pieces) if k > 0]

    kinds = class_index.reshape(bx * by, bz).astype(jnp.bfloat16)
    kinds = around_axis([kinds] * vols, "vol")
    slab = lax.all_to_all(source, ALL, 0, 0, tiled=True)
    slab = slab.reshape(rows, blocks, bx, by, bz)
    spots = trace_spots(trace_count, trace_cell, targets, shape).astype(jnp.bfloat16)
    spots = jnp.pad(spots, ((0, SPOT_ROWS - spots.shape[0]), (0, 0)))
    known = jnp.concatenate(kinds + [spots])
    made = start_call(density, panel, known, shape)
    lines, quarters = known.shape[0], made[rows:]
    known = around_axis(made[:rows], "row")
    other = [mated(piece, "col", 1) for piece in known]
    parts = list(collect_call(shape, lines, known, other))
    for k in range(1, vols):
        parts[k] = mated(parts[k], "vol", k)

    panels = [quarters[0], None, quarters[2], None]
    panels[1] = mated(quarters[1], "row", 1)
    panels[3] = mated(quarters[3], "row", 2)
    densities = [columns(density, low), columns(density, 2 + high)]

    inverse, hit, lane = prepare_call(shape, class_values, known, other)
    volume, flux = slab_call(shape, True, slab, inverse, hit, lane, parts)
    flux = flux.reshape(excitations, len(MATES), targets)
    flux = lax.all_to_all(flux, ALL, 0, 0, tiled=True)
    halves, mates, fars, parts = [], [], [], None
    for part in range(PARTS):
        *pair, far = update_call(flux, panels, part, PARTS, True)
        halves.append(pair)
        fars.append(far)
        mates.append([mated(halves[part][0], "row", 2), mated(halves[part][1], "row", 1)])
    for part in range(PARTS):
        parts = potential_call(
            densities, halves[part], mates[part], [*panels[:3], fars[part]], part, parts
        )
    parts = lax.all_to_all(parts, ALL, 0, 0, tiled=True)
    parts = parts.reshape(rows, blocks, len(MATES), targets)
    volume, flux = slab_call(shape, False, slab, inverse, hit, lane, parts, volume)
    flux = flux.reshape(excitations, len(MATES), targets)
    flux = lax.all_to_all(flux, ALL, 0, 0, tiled=True)
    volume = volume.reshape(excitations, bx, by, bz)
    volume = lax.all_to_all(volume, ALL, 0, 0, tiled=True)
    volume = landed_call(volume)
    ends = update_call(flux, panels, 0, 1, False)
    end_mates = [mated(ends[0], "row", 2), mated(ends[1], "row", 1)]
    totals = totals_call(
        [[(halves[part][g], mates[part][g]) for part in range(PARTS)] for g in range(2)],
        list(zip(ends, end_mates)),
    )
    moved = [mated(totals[0], "row", 1), mated(totals[1], "row", 2)]
    change = [
        jnp.where(low == 0, totals[0], moved[0]), jnp.where(low == 0, moved[0], totals[0]),
        jnp.where(high == 0, totals[1], moved[1]), jnp.where(high == 0, moved[1], totals[1]),
    ]
    density = density + jnp.concatenate(change, axis=1).astype(jnp.float32)
    return (density, volume)


def padded_2(value, sides, width):
    for axis, dim in sides:
        size, length = (lax.axis_size(axis), value.shape[dim])
        up = [(i, (i + 1) % size) for i in range(size - 1)]
        down = [(j, i) for i, j in up]
        last = lax.slice_in_dim(value, length - width, length, axis=dim)
        first = lax.slice_in_dim(value, 0, width, axis=dim)
        before = lax.ppermute(last, axis, up)
        after = lax.ppermute(first, axis, down)
        value = jnp.concatenate([before, value, after], axis=dim)
    return value


def neighbours(padded):
    center = padded[..., 1:-1, 1:-1, 1:-1]
    beside_all = padded[..., 2:, 1:-1, 1:-1] + padded[..., :-2, 1:-1, 1:-1]
    beside_all = beside_all + padded[..., 1:-1, 2:, 1:-1] + padded[..., 1:-1, :-2, 1:-1]
    beside_all = beside_all + padded[..., 1:-1, 1:-1, 2:] + padded[..., 1:-1, 1:-1, :-2]
    return (center, beside_all)


def split_by_block(panel, density, source, class_index, class_values, trace_count, trace_cell):
    factors = relax_factors(SWEEPS)
    conduct = conduct_of(class_index, class_values)
    diagonal = MASS_TERM + 6.0 * conduct
    counts = trace_count[0]
    block_index = lax.axis_index(("col", "vol"))
    offsets = jnp.cumsum(counts) - counts
    target_rows = panel.shape[0]
    slot_count = trace_cell.shape[2]
    slot_ids = jnp.arange(slot_count, dtype=jnp.int32)
    target_ids = jnp.arange(target_rows, dtype=jnp.int32)
    own_count = lax.dynamic_index_in_dim(counts, block_index, keepdims=False)
    first_target = lax.dynamic_index_in_dim(offsets, block_index, keepdims=False)
    cell_ids = lax.dynamic_index_in_dim(trace_cell[0], block_index, keepdims=False)
    live_slots = slot_ids < own_count
    select = (
        ((first_target + slot_ids)[:, None] == target_ids[None, :]) & live_slots[:, None]
    ).astype(jnp.float32)
    volume = jnp.zeros(source.shape, jnp.float32)
    field_shape = volume.shape
    share_width = density.shape[1] // lax.axis_size("row")
    share_state = lax.dynamic_slice_in_dim(
        density, lax.axis_index("row") * share_width, share_width, 1
    )
    rounded = density.astype(jnp.bfloat16)
    lead = field_shape[0]
    for iteration in range(OUTER):
        partial_value = lax.dot_general(
            rounded, panel, (((1,), (1,)), ((), ())), preferred_element_type=jnp.float32
        )
        potential = lax.psum(partial_value, ("col", "vol"))
        slot_values = jnp.dot(potential, select.T, precision=lax.Precision.HIGHEST)
        right_side = source.reshape(lead, -1).at[:, cell_ids].add(slot_values).reshape(field_shape)
        relax_volume = volume
        for factor in factors:
            padded = padded_2(relax_volume, (("row", 1), ("col", 2), ("vol", 3)), 1)
            center, beside_all = neighbours(padded)
            relax_volume = (
                center + factor * (right_side - diagonal * center + conduct * beside_all) / diagonal
            )
        volume = relax_volume
        mismatch = volume.reshape(lead, -1)[:, cell_ids] - slot_values
        own_fluxes = jnp.dot(mismatch, select, precision=lax.Precision.HIGHEST)
        fluxes = lax.psum(own_fluxes, ("col", "vol"))
        update = jnp.dot(fluxes.astype(jnp.bfloat16), panel, preferred_element_type=jnp.float32)
        share_state = share_state + RELAXATION * lax.psum_scatter(
            update, "row", scatter_dimension=1, tiled=True
        )
        if iteration + 1 < OUTER:
            rounded = lax.all_gather(share_state.astype(jnp.bfloat16), "row", axis=1, tiled=True)
    density = lax.all_gather(share_state, "row", axis=1, tiled=True)
    return (density, volume)


def local(*args):
    sizes = [lax.axis_size(a) for a in ALL]
    if whole_slabs(sizes, args[0].shape[0], args[2].shape):
        return split_by_excitation(*args)
    return split_by_block(*args)


def whole_slabs(sizes, targets, block):
    return math.prod(sizes) == block[0] and sizes == [4, 2, 4] and targets == block[3]


def solution(mesh):
    placed = (
        P("row", ("col", "vol")),
        P(None, ("col", "vol")),
        P(None, "row", "col", "vol"),
        P("row", "col", "vol"),
        P(),
        P("row", None),
        P("row", None, None),
    )
    return jax.shard_map(
        local,
        mesh=mesh,
        in_specs=placed,
        out_specs=(P(None, ("col", "vol")), P(None, "row", "col", "vol")),
        check_vma=False,
    )
```
